32 devices in a mesh: dp: 8 (over z, x), tensor: 4 (over y, core).
Axes of the slice: x: 2, y: 2, z: 4, core: 2. Of those that a mesh axis runs over, the one named last changes fastest.
Arguments:
- hidden_in: bfloat16 [32768, 768], P(('dp', 'tensor')), may hold values from -6 to 6
- teacher: float32 [32768, 768], P(('dp', 'tensor')), may hold values from -6 to 6
- valid_mask: int32 [32768], P(('dp', 'tensor')), may hold values from 0 to 1
- random_blocks: int32 [12, 32, 3, 32], replicated, may hold values from 0 to 1, as said below
- w_qkv: bfloat16 [3, 768, 768], P(None, 'dp', 'tensor'), may hold values from -0.21875 to 0.21875
- b_qv: bfloat16 [2, 12, 64], P(None, 'tensor', 'dp'), may hold values from -3 to 3
- w_out: bfloat16 [768, 768], P('tensor', 'dp'), may hold values from -3 to 3
- w_in: bfloat16 [768, 3072], P('dp', 'tensor'), may hold values from -0.21875 to 0.21875
- b_in: bfloat16 [48, 64], P('tensor', 'dp'), may hold values from -3 to 3
- w_back: bfloat16 [3072, 768], P('tensor', 'dp'), may hold values from -0.109375 to 0.109375
- ln_gains: bfloat16 [2, 768], P(None, 'dp'), may hold values from 0.25 to 1.75
- row_biases: bfloat16 [4, 768], P(None, 'dp'), may hold values from -2 to 2
Outputs:
- loss: float32 [], replicated
- encoded: float32 [32768, 768], P(('dp', 'tensor'))
- grad_in: float32 [32768, 768], P(('dp', 'tensor'))
- grad_qkv: float32 [3, 768, 768], P(None, 'dp', 'tensor')
- grad_qv_bias: float32 [2, 12, 64], P(None, 'tensor', 'dp')
- grad_out: float32 [768, 768], P('tensor', 'dp')
- grad_w_in: float32 [768, 3072], P('dp', 'tensor')
- grad_b_in: float32 [48, 64], P('tensor', 'dp')
- grad_w_back: float32 [3072, 768], P('tensor', 'dp')
- grad_gains: float32 [2, 768], P(None, ('dp', 'tensor'))
- grad_biases: float32 [4, 768], P(None, ('dp', 'tensor'))
The draws below stay inside these ranges and needn't reach their ends.
Inputs may be any that keep to these rules, and one draw needn't show every extreme that they name: `random_blocks`: each [h, j, r, :] holds a single 1; the 3 blocks chosen for one h and j are different, and none of them is block 0, block 31, or within one block of j.
All inputs are finite; a program needn't handle non-finite values.
Results may differ from the reference program's by a relative error of at most 0.015.
Values may be sent and summed in bfloat16 or wider, within the bound.
A program may use at most 192 MiB of HBM per device.

```python
import math
import jax
import jax.numpy as jnp
from jax import lax

D = 768
H = 12
HD = 64
FF = 3072
BLK = 64
RND = 3
SEQ_LEN = 2048
SEQ_DEV = 2
TOKENS = 32768
N_DP = 8


def draw_teacher(key, part):
    values = jnp.clip(jax.random.normal(key, (TOKENS, D), jnp.float32), -6.0, 6.0)
    return values


def draw_valid_mask(key, part):
    positions = jnp.arange(TOKENS, dtype=jnp.int32)
    drawn = jax.random.randint(key, (TOKENS,), 0, 4 * TOKENS, dtype=jnp.int32)
    return (drawn < TOKENS + 2 * positions).astype(jnp.int32)


def draw_random_blocks(key, part):
    count_blocks = SEQ_LEN // BLK
    drawn = jax.random.randint(key, (H, count_blocks, count_blocks), 0, 1 << 20, dtype=jnp.int32)
    columns = jnp.arange(count_blocks, dtype=jnp.int32)
    scores = drawn * count_blocks + columns[None, None, :]
    query_index = columns[:, None]
    barred = (jnp.abs(columns[None, :] - query_index) <= 1) | (columns[None, :] == 0) | (columns[None, :] == count_blocks - 1)
    scores = jnp.where(barred[None], -1, scores)
    picked = lax.top_k(scores, RND)[1]
    return (picked[..., None] == columns).astype(jnp.int32)


def shard_levels(stream_key, shape, pieces, smallest, high):
    level = 1.0
    for dim, shards_of in pieces:
        heights = jax.random.uniform(jax.random.fold_in(jax.random.fold_in(stream_key, 6), dim), (shards_of,), jnp.float32, smallest / len(pieces), high / len(pieces))
        level = level * jnp.repeat(jnp.exp(heights), shape[dim] // shards_of).reshape((-1,) + (1,) * (len(shape) - 1 - dim))
    return level


def noise(own_key, shape, scale, limit, cuts=(), kind=jnp.bfloat16):
    values = scale * jax.random.normal(own_key, shape, jnp.float32)
    if cuts:
        values = values * shard_levels(own_key, shape, cuts, -0.22, 0.18)
    return jnp.clip(values, -limit, limit).astype(kind)


def setup_inputs(seed: int = 0) -> dict:
    streams_of = jax.random.split(jax.random.key(seed), 13)
    hidden_in = noise(streams_of[0], (TOKENS, D), 1.0, 6.0, ((0, 32),))
    teacher = draw_teacher(jax.random.fold_in(streams_of[12], 71), 0)
    valid_mask = draw_valid_mask(jax.random.fold_in(streams_of[12], 71), 0)
    random_blocks = draw_random_blocks(jax.random.fold_in(streams_of[12], 71), 0)
    w_qkv = noise(streams_of[4], (3, D, D), D ** -0.5, 0.21875, ((1, 8), (2, 4)))
    b_qv = noise(streams_of[5], (2, H, HD), 0.5, 3.0, ((1, 4), (2, 8)))
    w_out = noise(streams_of[6], (D, D), (max(D // 192, 1)) ** -0.5, 3.0, ((0, 4), (1, 8)))
    w_in = noise(streams_of[7], (D, FF), D ** -0.5, 0.21875, ((0, 8), (1, 4)))
    b_in = noise(streams_of[8], (FF // 64, 64), 0.5, 3.0, ((0, 4), (1, 8)))
    w_back = noise(streams_of[9], (FF, D), FF ** -0.5, 0.109375, ((0, 4), (1, 8)))
    ln_gains = jnp.clip(1.0 + 0.15 * jax.random.normal(streams_of[10], (2, D), jnp.float32), 0.25, 1.75).astype(jnp.bfloat16)
    row_biases = noise(streams_of[11], (4, D), 0.3, 2.0, ((1, 8),))
    return dict(hidden_in=hidden_in, teacher=teacher, valid_mask=valid_mask, random_blocks=random_blocks, w_qkv=w_qkv, b_qv=b_qv, w_out=w_out, w_in=w_in, b_in=b_in, w_back=w_back, ln_gains=ln_gains, row_biases=row_biases)


@jax.custom_vjp
def low(v):
    return lax.optimization_barrier(v.astype(jnp.bfloat16)).astype(jnp.float32)

@jax.custom_vjp
def low_back(v):
    return v

def low_keep(v):
    return (low(v), None)

def low_pass(kept, grad):
    return (grad,)

def back_keep(v):
    return (v, None)

def back_low(kept, grad):
    return (low(grad),)
low.defvjp(low_keep, low_pass)
low_back.defvjp(back_keep, back_low)
epsilon = 1e-06
masked_score = -1e+30
exact_precision = lax.Precision.HIGHEST

def layer_norm(values, gain, shift):
    centred = values - lax.optimization_barrier(jnp.mean(values, axis=-1, keepdims=True))
    variance = lax.optimization_barrier(jnp.mean(centred * centred, axis=-1, keepdims=True))
    return centred * lax.rsqrt(variance + epsilon) * gain + shift

def gelu_tanh(values):
    return 0.5 * values * (1.0 + jnp.tanh(0.7978845608028654 * (values + 0.044715 * values * values * values)))

def block_pattern(chosen):
    count_blocks = chosen.shape[0]
    indices = jnp.arange(count_blocks)
    nearby = jnp.abs(indices[:, None] - indices[None, :]) <= 1
    edges = (indices == 0) | (indices == count_blocks - 1)
    picked = lax.optimization_barrier(jnp.sum(chosen, axis=1)) > 0
    return nearby | edges[:, None] | edges[None, :] | picked

def attend_head(stack, allowed):
    token_allowed = jnp.repeat(jnp.repeat(allowed, BLK, axis=0), BLK, axis=1)
    raw = jnp.dot(stack[0], stack[1].T, precision=exact_precision) * HD ** (-0.5)
    scores = jnp.where(token_allowed, low_back(raw), masked_score)
    peak = lax.optimization_barrier(jnp.max(scores, axis=-1, keepdims=True))
    weights = jnp.exp(scores - peak)
    shares = low(weights / lax.optimization_barrier(jnp.sum(weights, axis=-1, keepdims=True)))
    return jnp.dot(shares, stack[2], precision=exact_precision)

def head_item(pair):
    return attend_head(pair[0], pair[1])

def forward(params, tokens, target, mask_rows, allowed_heads):
    qkv_weight, bias_pair, out_weight, in_weight, in_bias, back_weight, gains, biases = params
    row_total = tokens.shape[0]
    seq_count = row_total // SEQ_LEN
    projected = jnp.einsum('nd,kde->kne', tokens, qkv_weight, precision=exact_precision)
    bias_rows = jnp.stack([bias_pair[0].reshape(D), jnp.zeros((D,), jnp.float32), bias_pair[1].reshape(D)])
    projected = low(low_back(projected + bias_rows[:, None, :]))
    items = projected.reshape(3, seq_count, SEQ_LEN, H, HD).transpose(1, 3, 0, 2, 4).reshape(seq_count * H, 3, SEQ_LEN, HD)
    patterns = jnp.tile(allowed_heads, (seq_count, 1, 1))
    context = lax.map(jax.checkpoint(head_item), (items, patterns))
    context = context.reshape(seq_count, H, SEQ_LEN, HD).transpose(0, 2, 1, 3).reshape(row_total, D)
    context = low(low_back(context))
    attention = low_back(jnp.dot(context, out_weight, precision=exact_precision))
    mixed = tokens + attention + biases[0]
    normed = layer_norm(mixed, gains[0], biases[1])
    inner = low_back(jnp.dot(low(normed), in_weight, precision=exact_precision) + in_bias.reshape(FF))
    active = low(gelu_tanh(inner))
    feed = low_back(jnp.dot(active, back_weight, precision=exact_precision))
    second = normed + feed + biases[2]
    encoded = layer_norm(second, gains[1], biases[3])
    error = encoded - target
    return (jnp.sum(mask_rows[:, None] * error * error), encoded)

def reference(hidden_in, teacher, valid_mask, random_blocks, w_qkv, b_qv, w_out, w_in, b_in, w_back, ln_gains, row_biases):
    params = tuple((value.astype(jnp.float32) for value in (w_qkv, b_qv, w_out, w_in, b_in, w_back, ln_gains, row_biases)))
    allowed_heads = jax.vmap(block_pattern)(random_blocks)
    per_group = math.gcd(SEQ_DEV * N_DP, max(1, 4096 // SEQ_LEN))
    group_rows = per_group * SEQ_LEN
    groups = TOKENS // group_rows
    mask_rows = valid_mask.astype(jnp.float32)
    valid_total = jnp.sum(mask_rows)
    factor = TOKENS / (2.0 * valid_total)
    token_groups = hidden_in.astype(jnp.float32).reshape(groups, group_rows, D)
    target_groups = teacher.reshape(groups, group_rows, D)
    mask_groups = mask_rows.reshape(groups, group_rows)

    def one_group(carry, inputs):
        running, grads = carry
        tokens, target, mask_part = inputs

        def loss_part(weights, values):
            return forward(weights, values, target, mask_part, allowed_heads)
        part_sum, backward, encoded = jax.vjp(loss_part, params, tokens, has_aux=True)
        grad_params, grad_tokens = backward(factor)
        grads = jax.tree.map(jnp.add, grads, grad_params)
        return ((running + part_sum, grads), (encoded, grad_tokens))
    begin = (jnp.zeros((), jnp.float32), jax.tree.map(jnp.zeros_like, params))
    (sum_sq, grads), (encoded, grad_tokens) = lax.scan(one_group, begin, (token_groups, target_groups, mask_groups))
    loss = sum_sq / (D * valid_total)
    return (loss, encoded.reshape(TOKENS, D), grad_tokens.reshape(TOKENS, D), grads[0], grads[1], grads[2], grads[3], grads[4], grads[5], grads[6], grads[7])
```

```python
import functools

import jax
import jax.numpy as jnp
from jax import lax
from jax.experimental import pallas as pl
from jax.experimental.pallas import tpu as pltpu
from jax.sharding import PartitionSpec as P

D = 768
HD = 64
BLK = 64
SEQ_LEN = 2048
epsilon = 1e-06
NEG = -1e30
F32 = jnp.float32
BF = jnp.bfloat16
MESH = pl.DeviceIdType.MESH
NT = (((1,), (1,)), ((), ()))
NN = (((1,), (0,)), ((), ()))
TN = (((0,), (0,)), ((), ()))
VM = pl.BlockSpec(memory_space=pltpu.VMEM)
SM = pl.BlockSpec(memory_space=pltpu.SMEM)
ANY = pl.BlockSpec(memory_space=pl.ANY)
SDS = jax.ShapeDtypeStruct


def dot(a, b, dims):
    return lax.dot_general(a, b, dims, preferred_element_type=F32)


def params(mib, cid=None):
    if cid is None:
        return pltpu.CompilerParams(vmem_limit_bytes=mib << 20)
    return pltpu.CompilerParams(vmem_limit_bytes=mib << 20, collective_id=cid, has_side_effects=True)


class Place:
    def __init__(self):
        self.zn = lax.axis_size("dp") // 2
        dp, t = lax.axis_index("dp"), lax.axis_index("tensor")
        self.z, self.x, self.y, self.c = dp // 2, dp % 2, t // 2, t % 2

    def at(self, z=None, x=None, y=None, c=None):
        z = self.z if z is None else z
        x = self.x if x is None else x
        y = self.y if y is None else y
        c = self.c if c is None else c
        return (z * 2 + x, y * 2 + c)

    def peer(self, axis, k=1):
        if axis == "z":
            return self.at(z=(self.z + k) % self.zn)
        return {
            "x": self.at(x=1 - self.x),
            "y": self.at(y=1 - self.y),
            "c": self.at(c=1 - self.c),
        }[axis]

    def peers(self, axes):
        out = []
        for axis in axes:
            for k in range(1, self.zn if axis == "z" else 2):
                out.append(self.peer(axis, k))
        return out


def greet(place, axes):
    barrier = pltpu.get_barrier_semaphore()
    peers = place.peers(axes)
    for peer in peers:
        pl.semaphore_signal(barrier, inc=1, device_id=peer, device_id_type=MESH)
    pl.semaphore_wait(barrier, len(peers))


class Sems:
    def __init__(self, send, recv):
        self.send, self.recv, self.used = send, recv, 0

    def copy(self, src, dst, device):
        i = self.used
        self.used += 1
        return pltpu.make_async_remote_copy(
            src_ref=src,
            dst_ref=dst,
            send_sem=self.send.at[i],
            recv_sem=self.recv.at[i],
            device_id=device,
            device_id_type=MESH,
        )
class Gather:
    def __init__(self, place, sems, shard, out, spec):
        self.place, self.sems, self.shard, self.out = place, sems, shard, out
        self.order, self.pre, self.axes, self.lanes = spec
        self.live = []

    def piece(self, whole):
        p = self.place
        own = {"y": p.y, "c": p.c, "z": p.z, "x": p.x}
        idx = (slice(None),) * self.pre
        idx += tuple(slice(None) if a in whole else own[a] for a in self.axes)
        if self.lanes is not None:
            idx += (slice(None),) * (len(self.out.shape) - len(idx) - 1) + (self.lanes,)
        return self.out.at[idx]

    def mine(self):
        ref = self.shard
        if self.lanes is None:
            return ref
        return ref.at[(slice(None),) * (len(ref.shape) - 1) + (self.lanes,)]

    def local(self, sem):
        return pltpu.make_async_copy(self.mine(), self.piece(""), sem)

    def start(self, stage):
        axis = self.order[stage]
        if stage == 0:
            src, dst = self.mine(), self.piece("")
        else:
            src = dst = self.piece(self.order[:stage])
        for k in range(1, self.place.zn if axis == "z" else 2):
            copy = self.sems.copy(src, dst, self.place.peer(axis, k))
            copy.start()
            self.live.append(copy)

    def wait(self):
        for copy in self.live:
            copy.wait()
        self.live = []


def gather_kernel(plan, n_in, *refs):
    ins, outs = refs[:n_in], refs[n_in : 2 * n_in]
    send, recv, here = refs[2 * n_in :]
    place = Place()
    greet(place, "zxyc")
    sems = Sems(send, recv)
    chunks = [Gather(place, sems, ins[i], outs[i], spec) for i, spec in plan]
    locals_ = []
    for n, chunk in enumerate(chunks):
        chunk.start(0)
        copy = chunk.local(here.at[n])
        copy.start()
        locals_.append(copy)
    for copy in locals_:
        copy.wait()
    for stage in range(1, 5):
        for chunk in chunks:
            if stage <= len(chunk.order):
                chunk.wait()
            if stage < len(chunk.order):
                chunk.start(stage)


def copies_of(order, zn):
    return sum(zn - 1 if a == "z" else 1 for a in order)


def gathered_shape(a, spec, zn):
    size = {"y": 2, "c": 2, "z": zn, "x": 2}
    pre = spec[1]
    return SDS(a.shape[:pre] + tuple(size[s] for s in spec[2]) + a.shape[pre:], a.dtype)


def gather_all(shards, plan, zn, cid):
    spec_of = {i: spec for i, spec in plan}
    copies = sum(copies_of(spec[0], zn) for _, spec in plan)
    n = len(shards)
    return pl.pallas_call(
        functools.partial(gather_kernel, plan, n),
        out_shape=tuple(gathered_shape(a, spec_of[i], zn) for i, a in enumerate(shards)),
        in_specs=[ANY] * n,
        out_specs=(ANY,) * n,
        scratch_shapes=[
            pltpu.SemaphoreType.DMA((copies,)),
            pltpu.SemaphoreType.DMA((copies,)),
            pltpu.SemaphoreType.DMA((len(plan),)),
        ],
        compiler_params=params(16, cid),
        name="gather_weights",
    )(*shards)


def swap_kernel(x_ref, o_ref, send, recv):
    place = Place()
    greet(place, "c")
    copy = pltpu.make_async_remote_copy(
        src_ref=x_ref.at[1 - place.c],
        dst_ref=o_ref,
        send_sem=send,
        recv_sem=recv,
        device_id=place.peer("c"),
        device_id_type=MESH,
    )
    copy.start()
    copy.wait()


def swap_cores(x, cid):
    return pl.pallas_call(
        swap_kernel,
        out_shape=SDS(x.shape[1:], x.dtype),
        in_specs=[ANY],
        out_specs=ANY,
        scratch_shapes=[pltpu.SemaphoreType.DMA, pltpu.SemaphoreType.DMA],
        compiler_params=params(16, cid),
        name="swap_cores",
    )(x)


class Scatter:
    def __init__(self, place, sems, grad, out, spec, bufs):
        self.place, self.sems, self.grad, self.out, self.bufs = place, sems, grad, out, bufs
        self.order, self.pre, self.axes = spec
        self.live = []

    @staticmethod
    def buffers(a, spec, zn):
        order, pre, axes = spec
        size = {"y": 2, "c": 2, "z": zn, "x": 2}
        lead, tail = a.shape[:pre], a.shape[pre + len(axes) :]
        left = list(axes)
        out = []
        for n, axis in enumerate(order):
            before = tuple(size[s] for s in left)
            left.remove(axis)
            after = tuple(size[s] for s in left)
            if axis == "z":
                recv = (zn - 1,) + lead + after + tail
            else:
                recv = lead + after + tail
            if n == 0:
                out.append((pltpu.VMEM(recv, BF), pltpu.VMEM(lead + after + tail, BF)))
            else:
                send = ((zn,) + lead + tail) if axis == "z" else lead + after + tail
                out.append((pltpu.VMEM(recv, BF), pltpu.VMEM(send, BF), pltpu.VMEM(lead + after + tail, F32)))
        return [b for group in out for b in group]

    def groups(self):
        out, rest = [], list(self.bufs)
        for n in range(len(self.order)):
            take = 2 if n == 0 else 3
            out.append(rest[:take])
            rest = rest[take:]
        return out

    def own(self, axis):
        p = self.place
        return {"y": p.y, "c": p.c, "z": p.z, "x": p.x}[axis]

    def begin(self, here):
        axis = self.order[0]
        at = self.pre + self.axes.index(axis)
        recv, keep = self.groups()[0]

        def half(i):
            return self.grad.at[(slice(None),) * at + (i,)]

        copy = self.sems.copy(half(1 - self.own(axis)), recv, self.place.peer(axis))
        copy.start()
        self.live = [copy]
        self.mine = pltpu.make_async_copy(half(self.own(axis)), keep, here)
        self.mine.start()
        self.left = [a for a in self.axes if a != axis]
        self.stage = 0

    def wait(self):
        for copy in self.live:
            copy.wait()
        self.live = []
        if self.stage == 0:
            self.mine.wait()

    def add(self):
        p, n = self.place, self.stage
        axis = self.order[n]
        group = self.groups()[n]
        recv, keep = group[0], group[-1]
        size = {"y": 2, "c": 2, "z": p.zn, "x": 2}
        lead = [range(s) for s in self.grad.shape[: self.pre]]

        def total(idx):
            if axis == "z":
                t = keep[idx]
                for k in range(p.zn - 1):
                    t = t + recv[(k,) + idx].astype(F32)
                return t
            return keep[idx].astype(F32) + recv[idx].astype(F32)

        def each(ranges, fn):
            if not ranges:
                fn(())
                return
            if isinstance(ranges[0], range):
                for i in ranges[0]:
                    each(ranges[1:], lambda rest, i=i: fn((i,) + rest))
            else:

                def body(i, carry):
                    each(ranges[1:], lambda rest: fn((i,) + rest))
                    return carry

                lax.fori_loop(0, ranges[0], body, 0)

        if n == len(self.order) - 1:

            def last(idx):
                self.out[idx] = total(idx)

            each(lead, last)
            return
        nxt = self.order[n + 1]
        recv2, send2, keep2 = self.groups()[n + 1]
        pos = self.left.index(nxt)
        own = self.own(nxt)
        rest_axes = [a for a in self.left if a != nxt]
        rest = lead + [size[a] if a == "z" else range(size[a]) for a in rest_axes]

        def place_of(idx, i):
            cut = self.pre + pos
            return idx[:cut] + (i,) + idx[cut:]

        def keep_one(idx):
            keep2[idx] = total(place_of(idx, own))

        if nxt == "z":
            for k in range(1, p.zn):
                i = (p.z + k) % p.zn

                def send_one(idx, i=i, k=k):
                    send2[(k,) + idx] = total(place_of(idx, i)).astype(BF)

                each(rest, send_one)
                copy = self.sems.copy(send2.at[k], recv2.at[k - 1], p.peer("z", k))
                copy.start()
                self.live.append(copy)
        else:

            def send_other(idx):
                send2[idx] = total(place_of(idx, 1 - own)).astype(BF)

            each(rest, send_other)
            copy = self.sems.copy(send2, recv2, p.peer(nxt))
            copy.start()
            self.live.append(copy)
        each(rest, keep_one)
        self.left = rest_axes
        self.stage = n + 1


class SumAll:
    order = "cyxz"

    def __init__(self, place, sems, value, out, recv, held):
        self.place, self.sems, self.value, self.out, self.recv, self.held = place, sems, value, out, recv, held
        self.live = []

    @staticmethod
    def buffers(a, zn):
        return [pltpu.VMEM((2 + zn,) + a.shape, F32), pltpu.VMEM((3,) + a.shape, F32)]

    def begin(self):
        self.stage = 0
        self.send(self.value)

    def send(self, src):
        p, n = self.place, self.stage
        axis = self.order[n]
        for k in range(1, p.zn if axis == "z" else 2):
            copy = self.sems.copy(src, self.recv.at[n + k - 1], p.peer(axis, k))
            copy.start()
            self.live.append(copy)

    def wait(self):
        for copy in self.live:
            copy.wait()
        self.live = []

    def add(self):
        n = self.stage
        mine = self.value[...] if n == 0 else self.held[n - 1]
        if n == 3:
            for k in range(self.place.zn - 1):
                mine = mine + self.recv[n + k]
            self.out[...] = mine
            return
        self.held[n] = mine + self.recv[n]
        self.stage = n + 1
        self.send(self.held.at[n])


def scatter_kernel(plan, shapes, zn, n_in, *refs):
    ins, outs, rest = refs[:n_in], refs[n_in : 2 * n_in], list(refs[2 * n_in :])
    send, recv, here = rest[:3]
    rest = rest[3:]
    place = Place()
    greet(place, "zxyc")
    sems = Sems(send, recv)
    chunks = []
    for n, spec in enumerate(plan):
        count = len(Scatter.buffers(shapes[n], spec, zn))
        chunks.append(Scatter(place, sems, ins[n], outs[n], spec, rest[:count]))
        rest = rest[count:]
    small = SumAll(place, sems, ins[-1], outs[-1], *rest)
    for n, chunk in enumerate(chunks):
        chunk.begin(here.at[n])
    small.begin()
    for stage in range(4):
        for chunk in chunks + [small]:
            if stage < len(chunk.order):
                chunk.wait()
                chunk.add()


def scatter_all(grads, plan, vector, zn, cid):
    shapes = tuple(SDS(g.shape, g.dtype) for g in grads)
    bufs = []
    for g, spec in zip(shapes, plan):
        bufs += Scatter.buffers(g, spec, zn)
    bufs += SumAll.buffers(vector, zn)
    copies = sum(copies_of(spec[0], zn) for spec in plan) + copies_of("cyxz", zn)
    out = [SDS(g.shape[: s[1]] + g.shape[s[1] + len(s[2]) :], F32) for g, s in zip(shapes, plan)]
    n = len(grads) + 1
    return pl.pallas_call(
        functools.partial(scatter_kernel, plan, shapes, zn, n),
        out_shape=tuple(out) + (SDS(vector.shape, F32),),
        in_specs=[ANY] * len(grads) + [VM],
        out_specs=(VM,) * n,
        scratch_shapes=[
            pltpu.SemaphoreType.DMA((copies,)),
            pltpu.SemaphoreType.DMA((copies,)),
            pltpu.SemaphoreType.DMA((len(grads),)),
        ]
        + bufs,
        compiler_params=params(56, cid),
        name="sum_gradients",
    )(*grads, vector)
def stack_heads(q):
    lo=lax.broadcasted_iota(jnp.int32,q.shape,1)<64
    z=jnp.zeros_like(q)
    return jnp.concatenate([jnp.where(lo,q,z),jnp.where(lo,z,q)],axis=0)

def slots_of(ref, j, picks, lanes, nb):
    lo=lax.broadcasted_iota(jnp.int32,(BLK,128),1)<64
    parts=[ref[0:BLK,lanes],ref[(nb-1)*BLK:nb*BLK,lanes],ref[pl.ds(pl.multiple_of((j-1)*BLK,BLK),3*BLK),lanes]]
    for a,b in picks:
        parts.append(jnp.where(lo,ref[pl.ds(pl.multiple_of(a*BLK,BLK),BLK),lanes],ref[pl.ds(pl.multiple_of(b*BLK,BLK),BLK),lanes]))
    return jnp.concatenate(parts,axis=0)

def picks_of(idx_ref,p,j):
    return [(idx_ref[2*p,j*3+r],idx_ref[2*p+1,j*3+r]) for r in range(3)]

def fwd_pair(p, idx_ref, q_ref, k_ref, v_ref, ctx_ref, lse_ref, lse_t, unroll=2):
    lanes=slice(p*128,(p+1)*128)
    nb=q_ref.shape[0]//BLK
    lo=lax.broadcasted_iota(jnp.int32,(BLK,128),1)<64
    col=lax.broadcasted_iota(jnp.int32,(128,128),1)
    def finish(o,l,m,j):
        inv=1.0/l
        o=o*inv
        ctx_ref[pl.ds(pl.multiple_of(j*BLK,BLK),BLK),lanes]=jnp.where(lo,o[:BLK],o[BLK:]).astype(BF)
        lse=m+jnp.log(l)
        lse_t[...]=jnp.where(col==j,lse,lse_t[...])
    def tile(j):
        picks=picks_of(idx_ref,p,j)
        q=stack_heads(q_ref[pl.ds(pl.multiple_of(j*BLK,BLK),BLK),lanes])
        ks=slots_of(k_ref,j,picks,lanes,nb); vs=slots_of(v_ref,j,picks,lanes,nb)
        s=dot(q,ks,NT)
        dup=((col<BLK)&(j==1))|((col>=BLK)&(j==nb-2))
        s=jnp.concatenate([jnp.where(dup,NEG,s[:,:128]),s[:,128:]],axis=1)
        m=jnp.max(s,axis=1,keepdims=True)
        e=jnp.exp(s-m)
        l=jnp.sum(e,axis=1,keepdims=True)
        o=dot(e.astype(BF),vs,NN)
        finish(o,l,m,j)
    def body(i,c):
        for u in range(unroll): tile(1+i*unroll+u)
        return c
    for j in (0,nb-1):
        q=stack_heads(q_ref[j*BLK:(j+1)*BLK,lanes])
        s=dot(q,k_ref[:,lanes],NT)
        m=jnp.max(s,axis=1,keepdims=True)
        e=jnp.exp(s-m)
        l=jnp.sum(e,axis=1,keepdims=True)
        o=dot(e.astype(BF),v_ref[:,lanes],NN)
        finish(o,l,m,j)
    lax.fori_loop(0,(nb-2)//unroll,body,0)
    lse_ref[p]=jnp.transpose(lse_t[...])[:nb]

def delta_row(do,ctx):
    d=jnp.transpose(do.astype(F32)*ctx.astype(F32))
    a=jnp.sum(d[:64],axis=0,keepdims=True); b=jnp.sum(d[64:],axis=0,keepdims=True)
    return jnp.concatenate([a,b],axis=1)

def bwd_pair(p, idx_ref, q_ref, k_ref, v_ref, ctx_ref, do_ref, lse_ref, dq_ref, dk_acc, dv_acc, unroll=1):
    lanes=slice(p*128,(p+1)*128)
    nb=q_ref.shape[0]//BLK
    lo=lax.broadcasted_iota(jnp.int32,(BLK,128),1)<64
    row=lax.broadcasted_iota(jnp.int32,(128,128),0)
    def core_math(q,do,ks,vs,lse,delta,dup=None):
        st=dot(ks,q,NT)
        pt=jnp.exp(st-lse)
        if dup is not None:
            pt=jnp.concatenate([jnp.where(dup,0.0,pt[:128]),pt[128:]],axis=0)
        dpt=dot(vs,do,NT)
        dst=(pt*(dpt-delta)).astype(BF)
        dv=dot(pt.astype(BF),do,NN)
        dk=dot(dst,q,NN)
        dq=dot(dst,ks,TN)
        return dq,dk,dv
    qs=[];dos=[];ls=[];ds=[]
    for j in (0,nb-1):
        rows=slice(j*BLK,(j+1)*BLK)
        qs.append(stack_heads(q_ref[rows,lanes])); dos.append(stack_heads(do_ref[rows,lanes]))
        ls.append(lse_ref[p,j:j+1,:]); ds.append(delta_row(do_ref[rows,lanes],ctx_ref[rows,lanes]))
    q=jnp.concatenate(qs,axis=0);do=jnp.concatenate(dos,axis=0);lse=jnp.concatenate(ls,axis=1);delta=jnp.concatenate(ds,axis=1)
    dqe=jnp.zeros((256,128),F32)
    ck=512
    for c in range(nb*BLK//ck):
        r=slice(c*ck,(c+1)*ck)
        dq,dk,dv=core_math(q,do,k_ref[r,lanes],v_ref[r,lanes],lse,delta)
        dqe=dqe+dq; dk_acc[r,:]=dk; dv_acc[r,:]=dv
    dqe=dqe*0.125
    dq_ref[0:BLK,lanes]=jnp.where(lo,dqe[0:64],dqe[64:128]).astype(BF)
    dq_ref[(nb-1)*BLK:nb*BLK,lanes]=jnp.where(lo,dqe[128:192],dqe[192:256]).astype(BF)
    def tile(j):
        picks=picks_of(idx_ref,p,j)
        rows=pl.ds(pl.multiple_of(j*BLK,BLK),BLK)
        qb=q_ref[rows,lanes]; dob=do_ref[rows,lanes]
        delta=delta_row(dob,ctx_ref[rows,lanes])
        ks=slots_of(k_ref,j,picks,lanes,nb); vs=slots_of(v_ref,j,picks,lanes,nb)
        dup=((row<BLK)&(j==1))|((row>=BLK)&(j==nb-2))
        dq,dk,dv=core_math(stack_heads(qb),stack_heads(dob),ks,vs,lse_ref[p,pl.ds(j,1),:],delta,dup)
        dq_ref[rows,lanes]=(jnp.where(lo,dq[:64],dq[64:])*0.125).astype(BF)
        win=pl.ds(pl.multiple_of((j-1)*BLK,BLK),3*BLK)
        for acc,g in ((dk_acc,dk),(dv_acc,dv)):
            acc[0:BLK,:]+=g[0:64]; acc[(nb-1)*BLK:nb*BLK,:]+=g[64:128]
            acc[win,:]+=g[128:320]
            for r,(a,b) in enumerate(picks):
                t=g[320+64*r:384+64*r]
                acc[pl.ds(pl.multiple_of(a*BLK,BLK),BLK),:]+=jnp.where(lo,t,0.0)
                acc[pl.ds(pl.multiple_of(b*BLK,BLK),BLK),:]+=jnp.where(lo,0.0,t)
    def body(i,c):
        for u in range(unroll): tile(1+i*unroll+u)
        return c
    lax.fori_loop(0,(nb-2)//unroll,body,0)

def concat_lanes(parts):
    return jnp.concatenate(parts, axis=1)


def project_kernel(unroll, idx_ref, h_ref, w_ref, b_ref, q_ref, k_ref, v_ref, ctx_ref, lse_ref, lse_t):
    rows = h_ref.shape[0]
    for k, out in enumerate((q_ref, k_ref, v_ref)):
        w = concat_lanes([w_ref[k, 0], w_ref[k, 1]])

        def some(i, carry, k=k, out=out, w=w):
            r = pl.ds(pl.multiple_of(i * 512, 512), 512)
            t = dot(h_ref[r, :], w, NN)
            if k != 1:
                t = t + b_ref[k // 2 : k // 2 + 1, :]
            t = t.astype(BF)
            if k == 0:
                t = (t.astype(F32) * 0.125).astype(BF)
            out[r, :] = t
            return carry

        lax.fori_loop(0, rows // 512, some, 0)
    for p in range(q_ref.shape[1] // 128):
        fwd_pair(p, idx_ref, q_ref, k_ref, v_ref, ctx_ref, lse_ref, lse_t, unroll)


def project_attend(idx, hidden, w, bias, unroll):
    n = hidden.shape[0]
    e = 2 * w.shape[-1]
    s = SDS((n, e), BF)
    return pl.pallas_call(
        functools.partial(project_kernel, unroll),
        out_shape=(s, s, s, s, SDS((e // 128, n // BLK, 128), F32)),
        in_specs=[SM, VM, VM, VM],
        out_specs=(VM,) * 5,
        scratch_shapes=[pltpu.VMEM((128, 128), F32)],
        compiler_params=params(56),
        name="project_attend",
    )(idx, hidden, w, bias)


def attend_back_kernel(unroll, idx_ref, q_ref, k_ref, v_ref, c_ref, do_ref, lse_ref, dq_ref, dk_ref, dv_ref, dka, dva):
    for p in range(q_ref.shape[1] // 128):
        bwd_pair(p, idx_ref, q_ref, k_ref, v_ref, c_ref, do_ref, lse_ref, dq_ref, dka, dva, unroll)
        lanes = slice(p * 128, (p + 1) * 128)
        dk_ref[:, lanes] = dka[...].astype(BF)
        dv_ref[:, lanes] = dva[...].astype(BF)


def attend_back(idx, q, k, v, ctx, do, lse, unroll):
    n, e = q.shape
    s = SDS((n, e), BF)
    return pl.pallas_call(
        functools.partial(attend_back_kernel, unroll),
        out_shape=(s, s, s),
        in_specs=[SM] + [VM] * 6,
        out_specs=(VM,) * 3,
        scratch_shapes=[pltpu.VMEM((n, 128), F32)] * 2,
        compiler_params=params(56),
        name="attend_back",
    )(idx, q, k, v, ctx, do, lse)


def norm(v):
    centred = v - jnp.mean(v, axis=-1, keepdims=True)
    rs = lax.rsqrt(jnp.mean(centred * centred, axis=-1, keepdims=True) + epsilon)
    return centred * rs, rs


def norm_back(g, gain, xhat, rs):
    gx = gain * g
    return rs * (gx - jnp.mean(gx, axis=-1, keepdims=True) - xhat * jnp.mean(gx * xhat, axis=-1, keepdims=True))


def gelu_both(v):
    k, a = 0.7978845608028654, 0.044715
    v2 = v * v
    th = jnp.tanh(k * v * (1.0 + a * v2))
    half = 0.5 * (1.0 + th)
    slope = half + (0.5 * k) * v * (1.0 - th * th) * (1.0 + (3.0 * a) * v2)
    return v * half, slope


def rows_kernel(
    scale_ref,
    ctx_ref,
    h_ref,
    t_ref,
    m_ref,
    w_in,
    w_bt,
    w_ot,
    b_in,
    gains,
    biases,
    enc_ref,
    gmix_ref,
    gctx_ref,
    gin_ref,
    gbt_ref,
    got_ref,
    vec_ref,
    gbin_ref,
    sq_ref,
    slope,
    act,
    ginner,
    nlow_t,
    slow_t,
    mlow_t,
):
    step = pl.program_id(0)
    tile = h_ref.shape[0]
    units = w_in.shape[0]
    r = pl.ds(pl.multiple_of(step * tile, tile), tile)

    @pl.when(step == 0)
    def _():
        vec_ref[...] = jnp.zeros_like(vec_ref)
        gbin_ref[...] = jnp.zeros_like(gbin_ref)
        sq_ref[...] = jnp.zeros_like(sq_ref)

    w_o = concat_lanes([w_ot[0, 0], w_ot[1, 0], w_ot[0, 1], w_ot[1, 1]])
    ctx = concat_lanes([ctx_ref[0], ctx_ref[1]])
    mixed = h_ref[...].astype(F32) + dot(ctx, w_o, NT) + biases[0:1, :]
    xhat1, rs1 = norm(mixed)
    normed = xhat1 * gains[0:1, :] + biases[1:2, :]
    nlow = normed.astype(BF)
    nlow_t[:, r] = nlow.T
    second = normed + biases[2:3, :]
    for u in range(units):
        inner = dot(nlow, w_in[u], NN) + b_in[u : u + 1, :]
        a, s = gelu_both(inner)
        a = a.astype(BF)
        act[u, r, :] = a
        slope[u] = s
        second = second + dot(a, w_bt[u], NT)
    xhat2, rs2 = norm(second)
    encoded = xhat2 * gains[1:2, :] + biases[3:4, :]
    enc_ref[...] = encoded
    error = encoded - t_ref[...]
    merr = m_ref[...] * error
    sq_ref[...] += jnp.sum(merr * error, axis=0, keepdims=True)
    genc = merr * scale_ref[0, 0]
    gsec = norm_back(genc, gains[1:2, :], xhat2, rs2)
    slow = gsec.astype(BF)
    slow_t[:, r] = slow.T
    gnorm = gsec
    for u in range(units):
        gi = (dot(slow, w_bt[u], NN) * slope[u]).astype(BF)
        ginner[u, r, :] = gi
        gbin_ref[u : u + 1, :] += jnp.sum(gi.astype(F32), axis=0, keepdims=True)
        gnorm = gnorm + dot(gi, w_in[u], NT)
    gmix = norm_back(gnorm, gains[0:1, :], xhat1, rs1)
    gmix_ref[...] = gmix
    mlow = gmix.astype(BF)
    mlow_t[:, r] = mlow.T
    gctx = dot(mlow, w_o, NN).astype(BF)
    gctx_ref[0] = gctx[:, : D // 2]
    gctx_ref[1] = gctx[:, D // 2 :]
    for n, value in enumerate((gnorm * xhat1, genc * xhat2, gmix, gnorm, gsec, genc)):
        vec_ref[n : n + 1, :] += jnp.sum(value, axis=0, keepdims=True)
    part = dot(mlow_t[:, r], ctx, NN)

    @pl.when(step == 0)
    def _():
        got_ref[...] = part

    @pl.when(step > 0)
    def _():
        got_ref[...] += part

    @pl.when(step == pl.num_programs(0) - 1)
    def _():
        for u in range(units):
            gin_ref[u] = dot(nlow_t[...], ginner[u], NN).astype(BF)
            gbt_ref[u] = dot(slow_t[...], act[u], NN).astype(BF)


def row_pass(scale, ctx, hidden, teacher, mask, w_in, w_bt, w_ot, b_in, gains, biases, tile):
    n = hidden.shape[0]
    units, _, wide = w_in.shape
    once = pl.Buffered(1)

    def whole(a):
        return pl.BlockSpec(a.shape, lambda i, nd=len(a.shape): (0,) * nd, pipeline_mode=once)

    def rows(width):
        return pl.BlockSpec((tile, width), lambda i: (i, 0))

    pair = pl.BlockSpec((2, tile, D // 2), lambda i: (0, i, 0))
    outs = (
        SDS((n, D), F32),
        SDS((n, D), F32),
        SDS((2, n, D // 2), BF),
        SDS(w_in.shape, BF),
        SDS(w_in.shape, BF),
        SDS((D, D), F32),
        SDS((6, D), F32),
        SDS((units, wide), F32),
        SDS((1, D), F32),
    )
    return pl.pallas_call(
        rows_kernel,
        grid=(n // tile,),
        out_shape=outs,
        in_specs=[SM, pair, rows(D), rows(D), rows(1)] + [whole(a) for a in (w_in, w_bt, w_ot, b_in, gains, biases)],
        out_specs=(rows(D), rows(D), pair) + tuple(whole(a) for a in outs[3:]),
        scratch_shapes=[
            pltpu.VMEM((units, tile, wide), F32),
            pltpu.VMEM((units, n, wide), BF),
            pltpu.VMEM((units, n, wide), BF),
            pltpu.VMEM((D, n), BF),
            pltpu.VMEM((D, n), BF),
            pltpu.VMEM((D, n), BF),
        ],
        compiler_params=params(62),
        name="row_pass",
    )(scale, ctx, hidden, teacher, mask, w_in, w_bt, w_ot, b_in, gains, biases)


def project_back_kernel(h_ref, dq_ref, dk_ref, dv_ref, w_ref, gw_ref, gh_ref, gb_ref):
    e = dq_ref.shape[1]
    half = e // 2
    hidden_t = h_ref[...].T
    for k, g in enumerate((dq_ref, dk_ref, dv_ref)):
        t = dot(hidden_t, g[...], NN).astype(BF)
        gw_ref[k, 0] = t[:, :half]
        gw_ref[k, 1] = t[:, half:]
        if k != 1:
            gb_ref[k // 2 : k // 2 + 1, :] = jnp.sum(g[...].astype(F32), axis=0, keepdims=True)
    w = [concat_lanes([w_ref[k, 0], w_ref[k, 1]]) for k in range(3)]

    def some(i, carry):
        r = pl.ds(pl.multiple_of(i * 256, 256), 256)
        t = dot(dq_ref[r, :], w[0], NT) + dot(dk_ref[r, :], w[1], NT) + dot(dv_ref[r, :], w[2], NT)
        gh_ref[r, :] = t.astype(BF)
        return carry

    lax.fori_loop(0, h_ref.shape[0] // 256, some, 0)


def project_back(hidden, dq, dk, dv, w):
    n = hidden.shape[0]
    return pl.pallas_call(
        project_back_kernel,
        out_shape=(SDS(w.shape, BF), SDS((n, D), BF), SDS((2, dq.shape[1]), F32)),
        in_specs=[VM] * 5,
        out_specs=(VM,) * 3,
        compiler_params=params(56),
        name="project_back",
    )(hidden, dq, dk, dv, w)
def per_device(
    hidden_in, teacher, valid_mask, random_blocks, w_qkv, b_qv, w_out, w_in, b_in, w_back, ln_gains, row_biases
):
    local = hidden_in.shape[0]
    dp, tensor = lax.axis_size("dp"), lax.axis_size("tensor")
    zn = dp // 2
    tokens_total = local * tensor * dp
    dpi, ti = lax.axis_index("dp"), lax.axis_index("tensor")
    y, c = ti // 2, ti % 2
    share = ln_gains.shape[1]
    heads = b_qv.shape[1]
    hd = b_qv.shape[2]
    mask = valid_mask.astype(F32)
    small = jnp.concatenate(
        [a.astype(F32).reshape(-1) for a in (b_qv, b_in, ln_gains, row_biases)] + [jnp.sum(mask).reshape(1)]
    )
    rows8 = -(-small.shape[0] // 1024) * 8
    small_pad = jnp.pad(small, (0, rows8 * 128 - small.shape[0])).reshape(rows8, 128)
    w_bt, w_ot = w_back.T, w_out.T
    half = w_in.shape[1] // 2
    lo, hi = slice(0, half), slice(half, 2 * half)
    full_qkv, whole_in, full_small, full_in, full_bt, full_ot = gather_all(
        (w_qkv, hidden_in, small_pad, w_in, w_bt, w_ot),
        [
            (0, ("zxy", 1, "yzx", None)),
            (1, ("c", 0, "c", None)),
            (2, ("zyxc", 0, "yczx", None)),
            (3, ("zxyc", 0, "yczx", lo)),
            (4, ("zyxc", 0, "yczx", lo)),
            (3, ("zxyc", 0, "yczx", hi)),
            (4, ("zyxc", 0, "yczx", hi)),
            (5, ("zyxc", 0, "yczx", None)),
        ],
        zn,
        0,
    )
    whole_in = whole_in.reshape(2 * local, D)
    full_qkv = full_qkv.reshape(3, 2, D, w_qkv.shape[2])
    full_in = full_in.reshape(4, D, w_in.shape[1])
    full_bt = full_bt.reshape(4, D, w_in.shape[1])
    full_ot = full_ot.reshape(2, 2, D, w_out.shape[0])
    flat = full_small.reshape(2, 2, dp, rows8 * 128)
    n0 = 2 * heads * hd
    n1 = n0 + b_in.size
    n2 = n1 + 2 * share
    n3 = n2 + 4 * share
    bias_qv = lax.dynamic_index_in_dim(flat, c, 1, False)[:, :, :n0].reshape(2, dp, 2, heads, hd)
    bias_qv = bias_qv.transpose(2, 0, 3, 1, 4).reshape(2, 2 * heads * hd * dp)
    bias_in = flat[..., n0:n1].reshape(4, dp, b_in.shape[0], hd).transpose(0, 2, 1, 3).reshape(4, -1)
    gains = flat[0, 0, :, n1:n2].reshape(dp, 2, share).transpose(1, 0, 2).reshape(2, D)
    biases = flat[0, 0, :, n2:n3].reshape(dp, 4, share).transpose(1, 0, 2).reshape(4, D)
    valid_total = jnp.sum(flat[..., n3])
    scale = (tokens_total / valid_total).reshape(1, 1)

    blocks = random_blocks.shape[1]
    idx = jnp.sum(random_blocks * jnp.arange(blocks, dtype=jnp.int32), axis=-1)
    idx = lax.dynamic_index_in_dim(idx.reshape(2, 2, heads, blocks * 3), c, 1, False).reshape(2 * heads, blocks * 3)

    q, k, v, ctx, lse = project_attend(idx, whole_in, full_qkv, bias_qv, 5)
    ctx_by_core = ctx.reshape(2, local, -1)
    ctx_there = swap_cores(ctx_by_core, 1)
    ctx_here = lax.dynamic_index_in_dim(ctx_by_core, c, 0, False)
    first = c == 0
    ctx_rows = jnp.stack([jnp.where(first, ctx_here, ctx_there), jnp.where(first, ctx_there, ctx_here)])
    encoded, gmix, gctx, g_in, g_bt, g_ot, vec, g_bin, sq = row_pass(
        scale, ctx_rows, hidden_in, teacher, mask[:, None], full_in, full_bt, full_ot, bias_in, gains, biases, 256
    )
    gctx_there = swap_cores(gctx, 2)
    gctx_here = lax.dynamic_index_in_dim(gctx, c, 0, False)
    gctx_seq = jnp.concatenate([jnp.where(first, gctx_here, gctx_there), jnp.where(first, gctx_there, gctx_here)])
    dq, dk, dv = attend_back(idx, q, k, v, ctx, gctx_seq, lse, 5)
    g_qkv, g_hidden, g_bias = project_back(whole_in, dq, dk, dv, full_qkv)
    g_hidden = g_hidden.reshape(2, local, D)
    there = swap_cores(g_hidden, 3)
    grad_in = gmix + lax.dynamic_index_in_dim(g_hidden, c, 0, False).astype(F32) + there.astype(F32)

    g_ot = g_ot.astype(BF).reshape(D, 2, 2, -1).transpose(2, 1, 0, 3)
    g_bias_all = lax.dynamic_update_index_in_dim(
        jnp.zeros((2, 2, 2, g_bias.shape[1] // 2), F32), g_bias.reshape(2, 2, -1), c, 2
    )
    vector = jnp.concatenate([vec.reshape(-1), g_bin.reshape(-1), g_bias_all.reshape(-1), jnp.sum(sq).reshape(1)])
    vrows = -(-vector.shape[0] // 1024) * 8
    vector = jnp.pad(vector, (0, vrows * 128 - vector.shape[0])).reshape(vrows, 128)
    s_in, s_bt, s_ot, s_qkv, vector = scatter_all(
        (
            g_in.reshape(2, 2, zn, 2, share, -1),
            g_bt.reshape(2, 2, zn, 2, share, -1),
            g_ot.reshape(2, 2, zn, 2, share, -1),
            g_qkv.reshape(3, 2, zn, 2, share, -1),
        ),
        [("cyxz", 0, "yczx"), ("cxyz", 0, "yczx"), ("cxyz", 0, "yczx"), ("yxz", 1, "yzx")],
        vector,
        zn,
        4,
    )
    vector = vector.reshape(-1)
    m0 = 6 * D
    m1 = m0 + g_bin.size
    m2 = m1 + g_bias_all.size
    part = dpi * tensor + ti
    cols = D // (dp * tensor)
    gains_biases = lax.dynamic_slice_in_dim(vector[:m0].reshape(6, D), part * cols, cols, 1)
    grad_b_in = lax.dynamic_index_in_dim(vector[m0:m1].reshape(tensor, b_in.shape[0], dp, hd), ti, 0, False)
    grad_b_in = lax.dynamic_index_in_dim(grad_b_in, dpi, 1, False)
    grad_qv = lax.dynamic_index_in_dim(vector[m1:m2].reshape(2, tensor, heads, dp, hd), ti, 1, False)
    grad_qv = lax.dynamic_index_in_dim(grad_qv, dpi, 2, False)
    loss = vector[m2] / (D * valid_total)
    return (
        loss,
        encoded,
        grad_in,
        s_qkv,
        grad_qv,
        s_ot.T,
        s_in,
        grad_b_in,
        s_bt.T,
        gains_biases[:2],
        gains_biases[2:],
    )


def solution(mesh):
    rows = P(("dp", "tensor"), None)
    in_specs = (
        rows,
        rows,
        P(("dp", "tensor")),
        P(),
        P(None, "dp", "tensor"),
        P(None, "tensor", "dp"),
        P("tensor", "dp"),
        P("dp", "tensor"),
        P("tensor", "dp"),
        P("tensor", "dp"),
        P(None, "dp"),
        P(None, "dp"),
    )
    out_specs = (
        P(),
        rows,
        rows,
        P(None, "dp", "tensor"),
        P(None, "tensor", "dp"),
        P("tensor", "dp"),
        P("dp", "tensor"),
        P("tensor", "dp"),
        P("tensor", "dp"),
        P(None, ("dp", "tensor")),
        P(None, ("dp", "tensor")),
    )
    return jax.shard_map(per_device, mesh=mesh, in_specs=in_specs, out_specs=out_specs, check_vma=False)
```

```python
import functools

import jax
import jax.numpy as jnp
from jax import lax
from jax.experimental import pallas as pl
from jax.experimental.pallas import tpu as pltpu
from jax.sharding import PartitionSpec as P

D = 768
HD = 64
BLK = 64
SEQ_LEN = 2048
epsilon = 1e-06
NEG = -1e30
F32 = jnp.float32
BF = jnp.bfloat16
MESH = pl.DeviceIdType.MESH
NT = (((1,), (1,)), ((), ()))
NN = (((1,), (0,)), ((), ()))
TN = (((0,), (0,)), ((), ()))
VM = pl.BlockSpec(memory_space=pltpu.VMEM)
SM = pl.BlockSpec(memory_space=pltpu.SMEM)
ANY = pl.BlockSpec(memory_space=pl.ANY)
SDS = jax.ShapeDtypeStruct


def dot(a, b, dims):
    return lax.dot_general(a, b, dims, preferred_element_type=F32)


def params(mib, cid=None):
    if cid is None:
        return pltpu.CompilerParams(vmem_limit_bytes=mib << 20)
    return pltpu.CompilerParams(vmem_limit_bytes=mib << 20, collective_id=cid, has_side_effects=True)


class Place:
    def __init__(self):
        self.zn = lax.axis_size("dp") // 2
        dp, t = lax.axis_index("dp"), lax.axis_index("tensor")
        self.z, self.x, self.y, self.c = dp // 2, dp % 2, t // 2, t % 2

    def at(self, z=None, x=None, y=None, c=None):
        z = self.z if z is None else z
        x = self.x if x is None else x
        y = self.y if y is None else y
        c = self.c if c is None else c
        return (z * 2 + x, y * 2 + c)

    def peer(self, axis, k=1):
        if axis == "z":
            return self.at(z=(self.z + k) % self.zn)
        return {
            "x": self.at(x=1 - self.x),
            "y": self.at(y=1 - self.y),
            "c": self.at(c=1 - self.c),
        }[axis]

    def peers(self, axes):
        out = []
        for axis in axes:
            for k in range(1, self.zn if axis == "z" else 2):
                out.append(self.peer(axis, k))
        return out


def greet(place, axes):
    barrier = pltpu.get_barrier_semaphore()
    peers = place.peers(axes)
    for peer in peers:
        pl.semaphore_signal(barrier, inc=1, device_id=peer, device_id_type=MESH)
    pl.semaphore_wait(barrier, len(peers))


class Sems:
    def __init__(self, send, recv):
        self.send, self.recv, self.used = send, recv, 0

    def take(self, count):
        at = self.used
        self.used += count
        return at

    def copy(self, i, src, dst, device):
        return pltpu.make_async_remote_copy(
            src_ref=src,
            dst_ref=dst,
            send_sem=self.send.at[i],
            recv_sem=self.recv.at[i],
            device_id=device,
            device_id_type=MESH,
        )


def copies_of(order, zn):
    return sum(zn - 1 if a == "z" else 1 for a in order)


def concat_lanes(parts):
    return jnp.concatenate(parts, axis=1)


class Gather:
    def __init__(self, place, sems, shard, out, spec):
        self.place, self.shard, self.out = place, shard, out
        self.order, self.pre, self.axes, self.lanes = spec
        self.sems = sems
        self.base = sems.take(copies_of(self.order, place.zn))

    def piece(self, whole):
        p = self.place
        own = {"y": p.y, "c": p.c, "z": p.z, "x": p.x}
        idx = (slice(None),) * self.pre
        idx += tuple(slice(None) if a in whole else own[a] for a in self.axes)
        if self.lanes is not None:
            idx += (slice(None),) * (len(self.out.shape) - len(idx) - 1) + (self.lanes,)
        return self.out.at[idx]

    def mine(self):
        ref = self.shard
        if self.lanes is None:
            return ref
        return ref.at[(slice(None),) * (len(ref.shape) - 1) + (self.lanes,)]

    def local(self, sem):
        return pltpu.make_async_copy(self.mine(), self.piece(""), sem)

    def copies(self, stage):
        axis, zn = self.order[stage], self.place.zn
        if stage == 0:
            src, dst = self.mine(), self.piece("")
        else:
            src = dst = self.piece(self.order[:stage])
        at = self.base + copies_of(self.order[:stage], zn)
        return [
            self.sems.copy(at + k - 1, src, dst, self.place.peer(axis, k))
            for k in range(1, zn if axis == "z" else 2)
        ]

    def start(self, stage):
        for copy in self.copies(stage):
            copy.start()

    def wait(self, stage):
        for copy in self.copies(stage):
            copy.wait()


class Scatter:
    def __init__(self, place, sems, grad, out, spec, bufs):
        self.place, self.sems, self.grad, self.out = place, sems, grad, out
        self.order, self.pre, self.axes, self.lanes = spec
        self.base = sems.take(copies_of(self.order, place.zn))
        self.keep, self.recv, self.send = bufs[0], [bufs[1]] + list(bufs[2::2]), [None] + list(bufs[3::2])
        self.own = {"y": place.y, "c": place.c, "z": place.z, "x": place.x}
        self.size = {"y": 2, "c": 2, "z": place.zn, "x": 2}

    @staticmethod
    def buffers(a, spec, zn):
        order, pre, axes, lanes = spec
        size = {"y": 2, "c": 2, "z": zn, "x": 2}
        lead, tail = a.shape[:pre], a.shape[pre + len(axes) :]
        if lanes is not None:
            tail = tail[:-1] + (lanes.stop - lanes.start,)
        out = []
        for n, axis in enumerate(order):
            after = tuple(size[s] for s in axes if s not in order[: n + 1])
            one = lead + after + tail
            if n == 0:
                out.append(pltpu.VMEM(one, BF))
            out.append(pltpu.VMEM(((zn - 1,) if axis == "z" else ()) + one, BF))
            if n > 0:
                out.append(pltpu.VMEM(((zn,) if axis == "z" else ()) + one, BF))
        return out

    def copies(self, stage, only=None):
        p, axis = self.place, self.order[stage]
        at = self.base + copies_of(self.order[:stage], p.zn)
        recv, send = self.recv[stage], self.send[stage]
        if axis == "z":
            return [
                self.sems.copy(at + k - 1, send.at[k], recv.at[k - 1], p.peer("z", k))
                for k in (range(1, p.zn) if only is None else (only,))
            ]
        return [self.sems.copy(at, self.half(1 - self.own[axis]) if stage == 0 else send, recv, p.peer(axis))]

    def half(self, i):
        idx = (slice(None),) * (self.pre + self.axes.index(self.order[0])) + (i,)
        if self.lanes is not None:
            idx += (slice(None),) * (len(self.grad.shape) - len(idx) - 1) + (self.lanes,)
        return self.grad.at[idx]

    def kept(self, here):
        return pltpu.make_async_copy(self.half(self.own[self.order[0]]), self.keep, here)

    def begin(self, here):
        self.copies(0)[0].start()
        self.kept(here).start()

    def wait(self, stage, here=None):
        for copy in self.copies(stage):
            copy.wait()
        if stage == 0:
            self.kept(here).wait()

    def total(self, n, lead, coords):
        def at(done):
            return lead + tuple(coords.get(a, self.own[a]) for a in self.axes if a not in done)

        t = self.keep[at(self.order[:1])].astype(F32)
        for m in range(n + 1):
            idx = at(self.order[: m + 1])
            if self.order[m] == "z":
                for k in range(self.place.zn - 1):
                    t = t + self.recv[m][(k,) + idx].astype(F32)
            else:
                t = t + self.recv[m][idx].astype(F32)
        return t

    def each(self, axes, fn, coords=None, lead=()):
        coords = coords or {}
        if len(lead) < self.pre:
            for i in range(self.grad.shape[len(lead)]):
                self.each(axes, fn, coords, lead + (i,))
        elif not axes:
            fn(lead, coords)
        elif axes[0] == "z":

            def body(i, carry):
                self.each(axes[1:], fn, {**coords, "z": i}, lead)
                return carry

            lax.fori_loop(0, self.size["z"], body, 0)
        else:
            for i in range(2):
                self.each(axes[1:], fn, {**coords, axes[0]: i}, lead)

    def add(self, n):
        p = self.place
        if n == len(self.order) - 1:

            def last(lead, coords):
                if self.lanes is None:
                    self.out[lead] = self.total(n, lead, coords)
                else:
                    self.out[lead + (slice(None), self.lanes)] = self.total(n, lead, coords)

            self.each("", last)
            return
        nxt = self.order[n + 1]
        send = self.send[n + 1]
        left = [a for a in self.axes if a not in self.order[: n + 2]]
        if nxt == "z":
            for k in range(1, p.zn):
                to = (p.z + k) % p.zn

                def put(lead, coords, k=k, to=to):
                    send[(k,) + lead] = self.total(n, lead, {**coords, "z": to}).astype(BF)

                self.each(left, put)
                self.copies(n + 1, k)[0].start()
        else:

            def put(lead, coords):
                idx = lead + tuple(coords[a] for a in left)
                send[idx] = self.total(n, lead, {**coords, nxt: 1 - self.own[nxt]}).astype(BF)

            self.each(left, put)
            self.copies(n + 1)[0].start()


class SumAll:
    order = "cyxz"

    def __init__(self, place, sems, value, out, recv, held):
        self.place, self.sems, self.value, self.out, self.recv, self.held = place, sems, value, out, recv, held
        self.base = sems.take(copies_of(self.order, place.zn))

    @staticmethod
    def buffers(a, zn):
        return [pltpu.VMEM((2 + zn,) + a.shape, F32), pltpu.VMEM((3,) + a.shape, F32)]

    def copies(self, n):
        p = self.place
        axis = self.order[n]
        src = self.value if n == 0 else self.held.at[n - 1]
        at = self.base + n
        return [
            self.sems.copy(at + k - 1, src, self.recv.at[n + k - 1], p.peer(axis, k))
            for k in range(1, p.zn if axis == "z" else 2)
        ]

    def begin(self):
        self.copies(0)[0].start()

    def wait(self, n):
        for copy in self.copies(n):
            copy.wait()

    def add(self, n):
        mine = self.value[...] if n == 0 else self.held[n - 1]
        if n == 3:
            for k in range(self.place.zn - 1):
                mine = mine + self.recv[n + k]
            self.out[...] = mine
            return
        self.held[n] = mine + self.recv[n]
        for copy in self.copies(n + 1):
            copy.start()


UNROLL = 5


def stack_heads(q):
    lo = lax.broadcasted_iota(jnp.int32, q.shape, 1) < HD
    z = jnp.zeros_like(q)
    return jnp.concatenate([jnp.where(lo, q, z), jnp.where(lo, z, q)], axis=0)


def block_rows(j, count=1):
    return pl.ds(pl.multiple_of(j * BLK, BLK), count * BLK)


def flat_rows(t):
    return t.reshape(t.shape[0] * t.shape[1], t.shape[2])


def picks_of(idx_ref, p, j):
    pairs = idx_ref.shape[0] // 2
    return [(idx_ref[p, j * 3 + r], idx_ref[pairs + p, j * 3 + r]) for r in range(3)]


def slots_of(ref, p, j, picks, nb):
    lo = lax.broadcasted_iota(jnp.int32, (BLK, 2 * HD), 1) < HD
    parts = [ref[p, 0], ref[p, nb - 1], flat_rows(ref[p, pl.ds(j - 1, 3)])]
    for a, b in picks:
        parts.append(jnp.where(lo, ref[p, a], ref[p, b]))
    return jnp.concatenate(parts, axis=0)


class Forward:
    def __init__(self, idx_ref, q_ref, k_ref, v_ref, ctx_ref, lse_ref, lse_t):
        self.idx, self.q, self.k, self.v, self.ctx, self.lse, self.lse_t = (
            idx_ref,
            q_ref,
            k_ref,
            v_ref,
            ctx_ref,
            lse_ref,
            lse_t,
        )
        self.nb = q_ref.shape[1] // BLK
        self.steps = (self.nb - 2) // UNROLL

    def close(self, p, j, s, v):
        lo = lax.broadcasted_iota(jnp.int32, (BLK, 2 * HD), 1) < HD
        col = lax.broadcasted_iota(jnp.int32, (2 * BLK, 128), 1)
        m = jnp.max(s, axis=1, keepdims=True)
        e = jnp.exp(s - m)
        total = jnp.sum(e, axis=1, keepdims=True)
        o = dot(e.astype(BF), v, NN) * (1.0 / total)
        self.ctx[p, block_rows(j), :] = jnp.where(lo, o[:BLK], o[BLK:]).astype(BF)
        self.lse_t[...] = jnp.where(col == j, m + jnp.log(total), self.lse_t[...])

    def edges(self, p):
        for j in (0, self.nb - 1):
            q = stack_heads(self.q[p, j * BLK : (j + 1) * BLK, :])
            self.close(p, j, dot(q, flat_rows(self.k[p]), NT), flat_rows(self.v[p]))

    def tile(self, p, j):
        picks = picks_of(self.idx, p, j)
        q = stack_heads(self.q[p, block_rows(j), :])
        ks = slots_of(self.k, p, j, picks, self.nb)
        vs = slots_of(self.v, p, j, picks, self.nb)
        s = dot(q, ks, NT)
        col = lax.broadcasted_iota(jnp.int32, (2 * BLK, 128), 1)
        double = ((col < BLK) & (j == 1)) | ((col >= BLK) & (j == self.nb - 2))
        s = jnp.concatenate([jnp.where(double, NEG, s[:, :128]), s[:, 128:]], axis=1)
        self.close(p, j, s, vs)

    def step(self, p, i):
        for u in range(UNROLL):
            self.tile(p, 1 + i * UNROLL + u)

    def finish(self, p):
        self.lse[p] = jnp.transpose(self.lse_t[...])[: self.nb]

    def run(self, pairs, at=None):
        def body(g, carry):
            p, i = g // self.steps, g % self.steps
            if at is not None:
                at(g)

            @pl.when(i == 0)
            def _():
                self.edges(p)

            self.step(p, i)

            @pl.when(i == self.steps - 1)
            def _():
                self.finish(p)

            return carry

        lax.fori_loop(0, pairs * self.steps, body, 0)


def delta_row(do, ctx):
    d = jnp.transpose(do.astype(F32) * ctx.astype(F32))
    a = jnp.sum(d[:HD], axis=0, keepdims=True)
    b = jnp.sum(d[HD:], axis=0, keepdims=True)
    return jnp.concatenate([a, b], axis=1)


class Backward:
    def __init__(self, idx_ref, prev_ref, last_ref, q, k, v, ctx, do, lse, dq, dk, dv, dk_acc, dv_acc, dk_run, dv_run):
        self.idx, self.prev, self.last = idx_ref, prev_ref, last_ref
        self.q, self.k, self.v, self.ctx, self.do, self.lse = q, k, v, ctx, do, lse
        self.dq, self.dk, self.dv = dq, dk, dv
        self.accs = ((dk_acc, dk_run), (dv_acc, dv_run))
        self.nb = q.shape[1] // BLK
        self.steps = (self.nb - 2) // UNROLL

    def math(self, q, do, ks, vs, lse, delta, double=None):
        st = dot(ks, q, NT)
        pt = jnp.exp(st - lse)
        if double is not None:
            pt = jnp.concatenate([jnp.where(double, 0.0, pt[:128]), pt[128:]], axis=0)
        dst = (pt * (dot(vs, do, NT) - delta)).astype(BF)
        return dot(dst, ks, TN), dot(dst, q, NN), dot(pt.astype(BF), do, NN)

    def edges(self, p):
        qs, dos, ls, ds = [], [], [], []
        lo = lax.broadcasted_iota(jnp.int32, (BLK, 2 * HD), 1) < HD
        for j in (0, self.nb - 1):
            rows = slice(j * BLK, (j + 1) * BLK)
            do = self.do_block(p, j)
            qs.append(stack_heads(self.q[p, rows, :]))
            dos.append(stack_heads(do))
            ls.append(self.lse[p, j : j + 1, :])
            ds.append(delta_row(do, self.ctx[p, rows, :]))
        q, do = jnp.concatenate(qs, axis=0), jnp.concatenate(dos, axis=0)
        lse, delta = jnp.concatenate(ls, axis=1), jnp.concatenate(ds, axis=1)
        dq_sum = jnp.zeros((4 * BLK, 2 * HD), F32)
        for n in range(self.nb // 8):
            r = slice(n * 8 * BLK, (n + 1) * 8 * BLK)
            ks, vs = flat_rows(self.k[p, n * 8 : (n + 1) * 8]), flat_rows(self.v[p, n * 8 : (n + 1) * 8])
            dq, dk, dv = self.math(q, do, ks, vs, lse, delta)
            dq_sum = dq_sum + dq
            self.accs[0][0][r, :] = dk
            self.accs[1][0][r, :] = dv
        dq_sum = dq_sum * 0.125
        for n, j in enumerate((0, self.nb - 1)):
            part = dq_sum[n * 2 * BLK : (n + 1) * 2 * BLK]
            self.dq[p, j * BLK : (j + 1) * BLK, :] = jnp.where(lo, part[:BLK], part[BLK:]).astype(BF)
        for _, run in self.accs:
            run[0] = jnp.zeros((BLK, 2 * HD), F32)

    def do_block(self, p, j):
        half = self.nb // 2
        if isinstance(j, int):
            return self.do[j // half, p, (j % half) * BLK : (j % half + 1) * BLK, :]
        return self.do[j // half, p, block_rows(j % half), :]

    def tile(self, p, j):
        lo = lax.broadcasted_iota(jnp.int32, (BLK, 2 * HD), 1) < HD
        row = lax.broadcasted_iota(jnp.int32, (2 * BLK, 128), 0)
        nb, pairs = self.nb, self.idx.shape[0] // 2
        picks = picks_of(self.idx, p, j)
        q, do = self.q[p, block_rows(j), :], self.do_block(p, j)
        delta = delta_row(do, self.ctx[p, block_rows(j), :])
        ks = slots_of(self.k, p, j, picks, nb)
        vs = slots_of(self.v, p, j, picks, nb)
        double = ((row < BLK) & (j == 1)) | ((row >= BLK) & (j == nb - 2))
        dq, dk, dv = self.math(
            stack_heads(q), stack_heads(do), ks, vs, self.lse[p, pl.ds(j, 1), :], delta, double
        )
        self.dq[p, block_rows(j), :] = (jnp.where(lo, dq[:BLK], dq[BLK:]) * 0.125).astype(BF)
        for (acc, run), g in zip(self.accs, (dk, dv)):
            acc[0:BLK, :] += g[0:BLK]
            acc[(nb - 1) * BLK : nb * BLK, :] += g[BLK : 2 * BLK]
            acc[block_rows(j - 1, 3), :] += g[2 * BLK : 5 * BLK]
            for r in range(3):
                s = j * 3 + r
                before = jnp.where(lo, run[self.prev[p, s]], run[self.prev[pairs + p, s]])
                run[s - 2] = g[(5 + r) * BLK : (6 + r) * BLK] + before

    def step(self, p, i):
        for u in range(UNROLL):
            self.tile(p, 1 + i * UNROLL + u)

    def finish(self, p):
        lo = lax.broadcasted_iota(jnp.int32, (BLK, 2 * HD), 1) < HD
        pairs = self.idx.shape[0] // 2

        def body(n, carry):
            a, b = self.last[p, n], self.last[pairs + p, n]
            for (acc, run), out in zip(self.accs, (self.dk, self.dv)):
                t = acc[block_rows(n), :] + jnp.where(lo, run[a], run[b])
                out[p, block_rows(n), :] = t.astype(BF)
            return carry

        lax.fori_loop(0, self.nb, body, 0)

    def run(self, pairs, at=None, done=None):
        def body(g, carry):
            p, i = g // self.steps, g % self.steps
            if at is not None:
                at(g)

            @pl.when(i == 0)
            def _():
                self.edges(p)

            self.step(p, i)

            @pl.when(i == self.steps - 1)
            def _():
                self.finish(p)
                if done is not None:
                    done(p)

            return carry

        lax.fori_loop(0, pairs * self.steps, body, 0)


def block_tables(random_blocks, place_c):
    heads, blocks = random_blocks.shape[:2]
    own = lax.dynamic_index_in_dim(
        random_blocks.reshape((2, 2, heads // 4) + random_blocks.shape[1:]), place_c, 1, False
    ).reshape(heads // 2, blocks * 3, blocks)
    idx = jnp.sum(own * jnp.arange(blocks, dtype=jnp.int32), axis=-1)
    slots = blocks * 3
    s = jnp.arange(slots, dtype=jnp.int32)
    middle = (s >= 3) & (s < slots - 3)
    number = jnp.where(middle, s - 2, 0)
    same = (idx[:, :, None] == idx[:, None, :]) & (s[None, None, :] < s[None, :, None])
    prev = jnp.max(jnp.where(same, number[None, None, :], 0), axis=-1)
    last = jnp.max(jnp.where(own > 0, number[None, :, None], 0), axis=1)
    return idx, prev, last
SMALL_ROWS = 16


class Due:
    def __init__(self):
        self.todo = {}

    def add(self, step, fn):
        self.todo.setdefault(step, []).append(fn)

    def __call__(self, g):
        for step, fns in self.todo.items():

            @pl.when(g == step)
            def _(fns=fns):
                for fn in fns:
                    fn()


def assemble_qkv(parts, w, pairs):
    zn, half = parts.shape[1], parts.shape[3]
    wide = parts.shape[4] // 2

    def body(n, carry):
        z, x = n // 2, n % 2
        for h in range(2):
            rows = pl.ds(pl.multiple_of(n * 2 * half + h * half, half), half)
            src = [parts[y, z, x, :, h * wide : (h + 1) * wide] for y in range(2)]
            for kp in range(3 * pairs):
                w[rows, kp * 128 : (kp + 1) * 128] = jnp.concatenate(
                    [s[:, kp * HD : (kp + 1) * HD] for s in src], axis=1
                )
        return carry

    lax.fori_loop(0, zn * 2, body, 0)


def project_rows(i, chunk, hid, w, bias, q, k, v):
    pairs = q.shape[0]
    e = pairs * 128
    per = hid.shape[1] // chunk
    src = hid[i // per, pl.ds(pl.multiple_of(i % per * chunk, chunk), chunk), :]
    rows = pl.ds(pl.multiple_of(i * chunk, chunk), chunk)
    t = dot(src, w[...], NN)
    for n, out in enumerate((q, k, v)):
        part = t[:, n * e : (n + 1) * e]
        if n == 0:
            part = (part + bias[0:1, :]).astype(BF).astype(F32) * 0.125
        if n == 2:
            part = part + bias[1:2, :]
        part = part.astype(BF)
        for p in range(pairs):
            one = part[:, p * 128 : (p + 1) * 128]
            if n == 0:
                out[p, rows, :] = one
            else:
                out[p, pl.ds(i * (chunk // BLK), chunk // BLK)] = one.reshape(chunk // BLK, BLK, 128)


def gather_attend_kernel(
    cuts,
    idx_ref,
    wq_ref,
    h_ref,
    small_ref,
    win_ref,
    wb_ref,
    wo_ref,
    q_ref,
    k_ref,
    v_ref,
    ctx_ref,
    lse_ref,
    rows_ref,
    hid_ref,
    w_ref,
    fin_ref,
    fbt_ref,
    fot_ref,
    par_ref,
    send,
    recv,
    here,
    parts,
    wbt,
    wot,
    s_recv,
    s_held,
    lse_t,
):
    place = Place()
    c = place.c
    local = h_ref.shape[0]
    pairs = q_ref.shape[0]
    greet(place, "zxyc")
    sems = Sems(send, recv)
    qkv = [
        Gather(place, sems, wq_ref, parts, ("zxy" if n % 2 == 0 else "zyx", 0, "yzx", slice(a, b)))
        for n, (a, b) in enumerate(cuts)
    ]
    hid = Gather(place, sems, h_ref, hid_ref, ("c", 0, "c", None))
    small = SumAll(place, sems, small_ref, par_ref, s_recv, s_held)
    half = win_ref.shape[1] // 2
    lo, hi = slice(0, half), slice(half, 2 * half)
    ffn = [
        Gather(place, sems, win_ref, fin_ref, ("zxyc", 0, "yczx", lo)),
        Gather(place, sems, wbt, fbt_ref, ("zyxc", 0, "yczx", lo)),
        Gather(place, sems, win_ref, fin_ref, ("zxyc", 0, "yczx", hi)),
        Gather(place, sems, wbt, fbt_ref, ("zyxc", 0, "yczx", hi)),
        Gather(place, sems, wot, fot_ref, ("zyxc", 0, "yczx", None)),
    ]
    swap_at = sems.take(pairs)
    for chunk in qkv:
        chunk.start(0)
    hid.start(0)
    small.begin()
    own = [pltpu.make_async_copy(wq_ref, parts.at[place.y, place.z, place.x], here.at[0]), hid.local(here.at[1])]
    for copy in own:
        copy.start()
    wbt[...] = wb_ref[...].T
    t = wo_ref[...].T
    hr = wot.shape[0]
    wot[...] = concat_lanes([t[:hr], t[hr:]])
    late = [
        pltpu.make_async_copy(src, out.at[place.y, c, place.z, place.x], here.at[2 + n])
        for n, (src, out) in enumerate(((win_ref, fin_ref), (wbt, fbt_ref), (wot, fot_ref)))
    ]
    for copy in late:
        copy.start()
    for copy in own:
        copy.wait()
    small.wait(0)
    small.add(0)
    for chunk in qkv:
        chunk.wait(0)
        chunk.start(1)
    small.wait(1)
    small.add(1)
    for chunk in ffn:
        chunk.start(0)
    for chunk in qkv:
        chunk.wait(1)
        chunk.start(2)
    small.wait(2)
    small.add(2)
    for copy in late:
        copy.wait()
    hid.wait(0)
    small.wait(3)
    small.add(3)
    for chunk in qkv:
        chunk.wait(2)
    assemble_qkv(parts, w_ref, pairs)

    def pass_on(n, stage):
        def fn():
            ffn[n].wait(stage)
            ffn[n].start(stage + 1)

        return fn

    early, due = Due(), Due()
    for step, n, stage in ((0, 0, 0), (0, 1, 0), (1, 2, 0), (3, 3, 0)):
        early.add(step, pass_on(n, stage))
    for step, n, stage in (
        (0, 4, 0),
        (0, 0, 1),
        (1, 1, 1),
        (3, 2, 1),
        (4, 3, 1),
        (6, 4, 1),
        (6, 0, 2),
        (8, 1, 2),
        (12, 2, 2),
        (15, 3, 2),
        (17, 4, 2),
    ):
        due.add(step, pass_on(n, stage))
    e = pairs * 128
    bias = jnp.where(c == 0, par_ref[11:13, :e], par_ref[11:13, e:])
    chunk_rows = local // 2

    def project(i, carry):
        early(i)
        project_rows(i, chunk_rows, hid_ref, w_ref, bias, q_ref, k_ref, v_ref)
        return carry

    lax.fori_loop(0, 4, project, 0)
    attend = Forward(idx_ref, q_ref, k_ref, v_ref, ctx_ref, lse_ref, lse_t)
    attend.run(pairs, due)

    def there(p):
        rows = pl.ds(pl.multiple_of((1 - c) * local, local), local)
        return sems.copy(swap_at + p, ctx_ref.at[p, rows, :], rows_ref.at[c, p], place.peer("c"))

    for p in range(pairs):
        there(p).start()
    mine = pltpu.make_async_copy(
        ctx_ref.at[:, pl.ds(pl.multiple_of(c * local, local), local), :], rows_ref.at[c], here.at[0]
    )
    mine.start()
    for chunk in ffn:
        chunk.wait(3)
    mine.wait()
    for p in range(pairs):
        there(p).wait()


def gather_attend(idx, wq, hidden, small, w_in, w_back, w_out, pairs, zn, cid):
    local = hidden.shape[0]
    n = 2 * local
    e = pairs * 128
    share, wide = w_in.shape
    width = wq.shape[1]
    step = width // 128 // 4 * 128
    cuts = [(i * step, (i + 1) * step if i < 3 else width) for i in range(4)]
    heads_shape = SDS((pairs, n, 128), BF)
    blocks_shape = SDS((pairs, n // BLK, BLK, 128), BF)
    wot = (share // 2, 2 * w_out.shape[0])
    copies = 4 * copies_of("zxy", zn) + 1 + copies_of("cyxz", zn) + 5 * copies_of("zxyc", zn) + pairs
    return pl.pallas_call(
        functools.partial(gather_attend_kernel, cuts),
        out_shape=(
            heads_shape,
            blocks_shape,
            blocks_shape,
            heads_shape,
            SDS((pairs, n // BLK, 128), F32),
            SDS((2, pairs, local, 128), BF),
            SDS((2, local, D), BF),
            SDS((D, 3 * e), BF),
            SDS((2, 2, zn, 2, share, wide), BF),
            SDS((2, 2, zn, 2, share, wide), BF),
            SDS((2, 2, zn, 2) + wot, BF),
            SDS(small.shape, F32),
        ),
        in_specs=[SM, ANY, ANY, VM, ANY, VM, VM],
        out_specs=(VM,) * 5 + (ANY, VM, VM, ANY, ANY, ANY, VM),
        scratch_shapes=[
            pltpu.SemaphoreType.DMA((copies,)),
            pltpu.SemaphoreType.DMA((copies,)),
            pltpu.SemaphoreType.DMA((5,)),
            pltpu.VMEM((2, zn, 2) + wq.shape, BF),
            pltpu.VMEM((share, wide), BF),
            pltpu.VMEM(wot, BF),
        ]
        + SumAll.buffers(small, zn)
        + [pltpu.VMEM((128, 128), F32)],
        compiler_params=params(56, cid),
        name="gather_attend",
    )(idx, wq, hidden, small, w_in, w_back, w_out)
def norm(v):
    centred = v - jnp.mean(v, axis=-1, keepdims=True)
    rs = lax.rsqrt(jnp.mean(centred * centred, axis=-1, keepdims=True) + epsilon)
    return centred * rs, rs


def norm_back(g, gain, xhat, rs):
    gx = gain * g
    return rs * (gx - jnp.mean(gx, axis=-1, keepdims=True) - xhat * jnp.mean(gx * xhat, axis=-1, keepdims=True))


def gelu_both(v):
    k, a = 0.7978845608028654, 0.044715
    v2 = v * v
    th = jnp.tanh(k * v * (1.0 + a * v2))
    half = 0.5 * (1.0 + th)
    slope = half + (0.5 * k) * v * (1.0 - th * th) * (1.0 + (3.0 * a) * v2)
    return v * half, slope


def assemble_out(parts, w):
    zn, half = parts.shape[2], parts.shape[4]
    wide = parts.shape[5] // 2
    pairs = wide // HD

    def body(n, carry):
        z, x = n // 2, n % 2
        for h in range(2):
            rows = pl.ds(pl.multiple_of(n * 2 * half + h * half, half), half)
            for c in range(2):
                for p in range(pairs):
                    at = h * wide + p * HD
                    w[rows, (c * pairs + p) * 128 : (c * pairs + p + 1) * 128] = concat_lanes(
                        [parts[y, c, z, x, :, at : at + HD] for y in range(2)]
                    )
        return carry

    lax.fori_loop(0, zn * 2, body, 0)


def scatter_out(w, parts):
    zn, half = parts.shape[2], parts.shape[4]
    wide = parts.shape[5] // 2
    pairs = wide // HD

    def body(n, carry):
        z, x = n // 2, n % 2
        src = [w[pl.ds(pl.multiple_of(n * 2 * half + h * half, half), half), :] for h in range(2)]
        for y in range(2):
            for c in range(2):
                cols = [(c * pairs + p) * 128 + y * HD for p in range(pairs)]
                parts[y, c, z, x] = concat_lanes([s[:, a : a + HD] for s in src for a in cols]).astype(BF)
        return carry

    lax.fori_loop(0, zn * 2, body, 0)


def rows_kernel(
    tokens_total,
    packed,
    ctx_ref,
    h_ref,
    t_ref,
    m_ref,
    w_in,
    w_bt,
    w_ot,
    par,
    enc_ref,
    gmix_ref,
    gctx_ref,
    gin_ref,
    gbt_ref,
    got_ref,
    vec_ref,
    slope,
    act,
    ginner,
    nlow_t,
    slow_t,
    w_o,
    got,
):
    step = pl.program_id(0)
    tile = h_ref.shape[0]
    units = w_in.shape[0]
    pairs = ctx_ref.shape[1]
    r = pl.ds(pl.multiple_of(step * tile, tile), tile)

    @pl.when(step == 0)
    def _():
        vec_ref[...] = jnp.zeros_like(vec_ref)
        got[...] = jnp.zeros_like(got)
        if packed:
            assemble_out(w_ot, w_o)
        else:
            w_o[...] = w_ot[...]

    gains, biases = par[4:6, :], par[6:10, :]
    scale = tokens_total / par[10:11, 0:1]
    ctx = concat_lanes([ctx_ref[n, p] for n in range(2) for p in range(pairs)])
    mixed = h_ref[...].astype(F32) + dot(ctx, w_o[...], NT) + biases[0:1, :]
    xhat1, rs1 = norm(mixed)
    normed = xhat1 * gains[0:1, :] + biases[1:2, :]
    nlow = normed.astype(BF)
    nlow_t[:, r] = nlow.T
    second = normed + biases[2:3, :]
    for u in range(units):
        inner = dot(nlow, w_in[u], NN) + par[u : u + 1, :]
        a, s = gelu_both(inner)
        a = a.astype(BF)
        act[u, r, :] = a
        slope[u] = s
        second = second + dot(a, w_bt[u], NT)
    xhat2, rs2 = norm(second)
    encoded = xhat2 * gains[1:2, :] + biases[3:4, :]
    enc_ref[...] = encoded
    error = encoded - t_ref[...]
    merr = m_ref[...] * error
    genc = merr * scale
    gsec = norm_back(genc, gains[1:2, :], xhat2, rs2)
    slow = gsec.astype(BF)
    slow_t[:, r] = slow.T
    gnorm = gsec
    for u in range(units):
        gi = (dot(slow, w_bt[u], NN) * slope[u]).astype(BF)
        ginner[u, r, :] = gi
        vec_ref[6 + u : 7 + u, :] += jnp.sum(gi.astype(F32), axis=0, keepdims=True)
        gnorm = gnorm + dot(gi, w_in[u], NT)
    gmix = norm_back(gnorm, gains[0:1, :], xhat1, rs1)
    gmix_ref[...] = gmix
    mlow = gmix.astype(BF)
    gctx = dot(mlow, w_o[...], NN).astype(BF)
    for n in range(2):
        for p in range(pairs):
            gctx_ref[n, p] = gctx[:, (n * pairs + p) * 128 : (n * pairs + p + 1) * 128]
    sums = (gnorm * xhat1, genc * xhat2, gmix, gnorm, gsec, genc)
    for n, value in enumerate(sums):
        vec_ref[n : n + 1, :] += jnp.sum(value, axis=0, keepdims=True)
    vec_ref[10:11, :] += jnp.sum(merr * error, axis=0, keepdims=True)
    got[...] += dot(mlow.T, ctx, NN)

    @pl.when(step == pl.num_programs(0) - 1)
    def _():
        if packed:
            scatter_out(got, got_ref)
        else:
            got_ref[...] = got[...].astype(BF)
        for u in range(units):
            gin_ref[u] = dot(nlow_t[...], ginner[u], NN).astype(BF)
            gbt_ref[u] = dot(slow_t[...], act[u], NN).astype(BF)


def row_pass(tokens_total, ctx, hidden, teacher, mask, w_in, w_bt, w_ot, par, tile):
    n = hidden.shape[0]
    units, _, wide = w_in.shape
    pairs = ctx.shape[1]
    once = pl.Buffered(1)

    def whole(a):
        return pl.BlockSpec(a.shape, lambda i, nd=len(a.shape): (0,) * nd, pipeline_mode=once)

    def rows(width):
        return pl.BlockSpec((tile, width), lambda i: (i, 0))

    heads = pl.BlockSpec((2, pairs, tile, 128), lambda i: (0, 0, i, 0))
    outs = (
        SDS((n, D), F32),
        SDS((n, D), F32),
        SDS((2, pairs, n, 128), BF),
        SDS(w_in.shape, BF),
        SDS(w_in.shape, BF),
        SDS(w_ot.shape, BF),
        SDS((SMALL_ROWS, D), F32),
    )
    return pl.pallas_call(
        functools.partial(rows_kernel, float(tokens_total), len(w_ot.shape) > 2),
        grid=(n // tile,),
        out_shape=outs,
        in_specs=[heads, rows(D), rows(D), rows(1)] + [whole(a) for a in (w_in, w_bt, w_ot, par)],
        out_specs=(rows(D), rows(D), heads) + tuple(whole(a) for a in outs[3:]),
        scratch_shapes=[
            pltpu.VMEM((units, tile, wide), F32),
            pltpu.VMEM((units, n, wide), BF),
            pltpu.VMEM((units, n, wide), BF),
            pltpu.VMEM((D, n), BF),
            pltpu.VMEM((D, n), BF),
            pltpu.VMEM((D, D), BF),
            pltpu.VMEM((D, D), F32),
        ],
        compiler_params=params(62),
        name="row_pass",
    )(ctx, hidden, teacher, mask, w_in, w_bt, w_ot, par)
QKV_ORDERS = ("yxz", "xyz", "yxz")
FFN_ORDERS = ("cyxz", "cxyz", "cyxz", "cxyz")
OUT_ORDER = "cxyz"


def weight_grad(p, hid_t, dq, dk, dv):
    return dot(hid_t[...], concat_lanes([dq[p], dk[p], dv[p]]), NN)


def hidden_grad(dq, dk, dv, w, rows):
    pairs = dq.shape[0]
    return dot(concat_lanes([g[p, rows, :] for g in (dq, dk, dv) for p in range(pairs)]), w[...], NT)


def attend_sum_kernel(
    idx_ref,
    prev_ref,
    last_ref,
    q_ref,
    k_ref,
    v_ref,
    ctx_ref,
    lse_ref,
    gctx_ref,
    hid_ref,
    w_ref,
    gmix_ref,
    gin_ref,
    gbt_ref,
    got_ref,
    vec_ref,
    out_ref,
    sin_ref,
    sbt_ref,
    sot_ref,
    sq_ref,
    vsum_ref,
    send,
    recv,
    here,
    do_ref,
    dq,
    dk,
    dv,
    dk_acc,
    dv_acc,
    dk_run,
    dv_run,
    hid_t,
    gq,
    gh_send,
    gh_recv,
    v_recv,
    v_held,
    *bufs,
):
    place = Place()
    c = place.c
    pairs = q_ref.shape[0]
    local = gmix_ref.shape[0]
    greet(place, "zxyc")
    sems = Sems(send, recv)
    wide = gin_ref.shape[-1]
    halves = (slice(0, wide // 2), slice(wide // 2, wide))
    jobs = []
    rest = list(bufs)
    for grad, out, order, lanes in (
        (gin_ref, sin_ref, FFN_ORDERS[0], halves[0]),
        (gbt_ref, sbt_ref, FFN_ORDERS[1], halves[0]),
        (gin_ref, sin_ref, FFN_ORDERS[2], halves[1]),
        (gbt_ref, sbt_ref, FFN_ORDERS[3], halves[1]),
        (got_ref, sot_ref, OUT_ORDER, None),
    ):
        spec = (order, 0, "yczx", lanes)
        count = len(Scatter.buffers(grad, spec, place.zn))
        jobs.append(Scatter(place, sems, grad, out, spec, rest[:count]))
        rest = rest[count:]
    for p in range(pairs):
        spec = (QKV_ORDERS[p % 3], 0, "yzx", None)
        count = len(Scatter.buffers(gq.at[p], spec, place.zn))
        jobs.append(Scatter(place, sems, gq.at[p], sq_ref.at[p], spec, rest[:count]))
        rest = rest[count:]
    small = SumAll(place, sems, vec_ref, vsum_ref, v_recv, v_held)
    swaps = sems.take(2)
    first = sems.copy(swaps, gctx_ref.at[1 - c], do_ref.at[c], place.peer("c"))
    first.start()
    mine = pltpu.make_async_copy(gctx_ref.at[c], do_ref.at[c], here.at[len(jobs)])
    mine.start()
    start_out = pltpu.make_async_copy(gmix_ref, out_ref, here.at[len(jobs) + 1])
    start_out.start()
    for n in range(5):
        jobs[n].begin(here.at[n])
    for i in range(2):
        hid_t[:, i * local : (i + 1) * local] = hid_ref[i].T
    mine.wait()
    first.wait()

    def advance(n, stage):
        def fn():
            jobs[n].wait(stage, here.at[n])
            jobs[n].add(stage)

        return fn

    due = Due()
    for step, n, stage in (
        (0, 0, 0),
        (1, 1, 0),
        (2, 2, 0),
        (3, 3, 0),
        (4, 4, 0),
        (6, 0, 1),
        (6, 1, 1),
        (9, 0, 2),
        (9, 1, 2),
        (10, 2, 1),
        (10, 3, 1),
        (11, 4, 1),
        (12, 0, 3),
        (12, 1, 3),
        (12, 5, 0),
        (14, 2, 2),
        (14, 3, 2),
        (14, 5, 1),
        (15, 4, 2),
        (15, 6, 0),
        (16, 5, 2),
        (17, 2, 3),
        (17, 3, 3),
        (17, 6, 1),
    ):
        due.add(step, advance(n, stage))
    attend = Backward(
        idx_ref, prev_ref, last_ref, q_ref, k_ref, v_ref, ctx_ref, do_ref, lse_ref, dq, dk, dv,
        dk_acc, dv_acc, dk_run, dv_run,
    )
    half = gq.shape[4]

    def done(p):
        t = weight_grad(p, hid_t, dq, dk, dv).astype(BF)
        for z in range(place.zn):
            for x in range(2):
                at = (z * 2 + x) * 2 * half
                src = [t[at + h * half : at + (h + 1) * half] for h in range(2)]
                for y in range(2):
                    gq[p, y, z, x] = concat_lanes(
                        [s[:, k * 128 + y * HD : k * 128 + (y + 1) * HD] for s in src for k in range(3)]
                    )
        lanes = pl.ds(pl.multiple_of((c * pairs + p) * 128, 128), 128)
        for row, g in ((11, dq), (12, dv)):
            vec_ref[row : row + 1, lanes] = jnp.sum(g[p].astype(F32), axis=0, keepdims=True)
        for n in range(pairs):

            @pl.when(p == n)
            def _(n=n):
                jobs[5 + n].begin(here.at[5 + n])

    attend.run(pairs, due, done)
    small.begin()
    size = local // 4

    def other(i, carry):
        t = hidden_grad(dq, dk, dv, w_ref, pl.ds(pl.multiple_of((1 - c) * local + i * size, size), size))
        gh_send[pl.ds(pl.multiple_of(i * size, size), size), :] = t.astype(BF)
        return carry

    lax.fori_loop(0, 4, other, 0)
    swap = sems.copy(swaps + 1, gh_send, gh_recv, place.peer("c"))
    swap.start()
    start_out.wait()
    small.wait(0)
    small.add(0)
    advance(7, 0)()

    def own(i, carry):
        rows = pl.ds(pl.multiple_of(i * size, size), size)
        t = hidden_grad(dq, dk, dv, w_ref, pl.ds(pl.multiple_of(c * local + i * size, size), size))
        out_ref[rows, :] += t
        return carry

    lax.fori_loop(0, 4, own, 0)
    for n, stage in ((4, 3), (6, 2)):
        advance(n, stage)()
    small.wait(1)
    small.add(1)
    advance(7, 1)()
    swap.wait()

    def last(i, carry):
        rows = pl.ds(pl.multiple_of(i * size, size), size)
        out_ref[rows, :] += gh_recv[rows, :].astype(F32)
        return carry

    lax.fori_loop(0, 4, last, 0)
    small.wait(2)
    small.add(2)
    advance(7, 2)()
    small.wait(3)
    small.add(3)


def attend_sum(tables, q, k, v, ctx, lse, gctx, hid, w, gmix, g_in, g_bt, g_ot, vec, zn, cid):
    pairs, n, _ = q.shape
    local = gmix.shape[0]
    share, wide = g_in.shape[-2:]
    blocks = n // BLK
    packed = g_ot.shape[-2:]
    gq = (pairs, 2, zn, 2) + packed
    heads = pltpu.VMEM((pairs, n, 128), BF)
    half = slice(0, wide // 2)
    bufs = []
    copies = copies_of("cyxz", zn) + 2
    big = [(g_in, order, "yczx", half) for order in FFN_ORDERS]
    for a, order, axes, lanes in big + [(g_ot, OUT_ORDER, "yczx", None)] + [
        (SDS(gq[1:], BF), QKV_ORDERS[p % 3], "yzx", None) for p in range(pairs)
    ]:
        bufs += Scatter.buffers(a, (order, 0, axes, lanes), zn)
        copies += copies_of(order, zn)
    return pl.pallas_call(
        attend_sum_kernel,
        out_shape=(
            SDS((local, D), F32),
            SDS((share, wide), F32),
            SDS((share, wide), F32),
            SDS(packed, F32),
            SDS((pairs,) + packed, F32),
            SDS(vec.shape, F32),
        ),
        in_specs=[SM] * 3 + [VM] * 5 + [ANY, VM, VM, ANY, ANY, ANY, ANY, VM],
        out_specs=(VM,) * 6,
        scratch_shapes=[
            pltpu.SemaphoreType.DMA((copies,)),
            pltpu.SemaphoreType.DMA((copies,)),
            pltpu.SemaphoreType.DMA((7 + pairs,)),
            pltpu.VMEM(gctx.shape, BF),
            heads,
            heads,
            heads,
            pltpu.VMEM((n, 128), F32),
            pltpu.VMEM((n, 128), F32),
            pltpu.VMEM((3 * (blocks - 2) + 1, BLK, 128), F32),
            pltpu.VMEM((3 * (blocks - 2) + 1, BLK, 128), F32),
            pltpu.VMEM((D, n), BF),
            pltpu.VMEM(gq, BF),
            pltpu.VMEM((local, D), BF),
            pltpu.VMEM((local, D), BF),
        ]
        + SumAll.buffers(vec, zn)
        + bufs,
        compiler_params=params(62, cid),
        name="attend_sum",
    )(*tables, q, k, v, ctx, lse, gctx, hid, w, gmix, g_in, g_bt, g_ot, vec)
def small_parts(b_qv, b_in, ln_gains, row_biases, count):
    dp, dpi = lax.axis_size("dp"), lax.axis_index("dp")
    t = lax.axis_index("tensor")
    y, c = t // 2, t % 2

    def at(i, size):
        return (jnp.arange(size) == i).astype(F32)

    heads, hd = b_qv.shape[1:]
    units = at(t, 4)[:, None, None, None] * b_in.astype(F32)[None, :, None, :] * at(dpi, dp)[None, None, :, None]
    rows = jnp.concatenate([ln_gains, row_biases]).astype(F32)
    rows = rows[:, None, :] * at(dpi, dp)[None, :, None] * (t == 0).astype(F32)
    total = count * at(0, D)
    bias = b_qv.astype(F32)[:, None, :, None, None, :] * at(c, 2)[None, :, None, None, None, None]
    bias = bias * at(y, 2)[None, None, None, :, None, None] * at(dpi, dp)[None, None, None, None, :, None]
    out = jnp.concatenate([units.reshape(4, D), rows.reshape(6, D), total.reshape(1, D), bias.reshape(2, D)])
    return jnp.pad(out, ((0, SMALL_ROWS - out.shape[0]), (0, 0)))


def finish(vector, par, encoded, grad_in, s_qkv, s_out, s_in, s_back, b_in, pairs, hd):
    dp, tensor = lax.axis_size("dp"), lax.axis_size("tensor")
    dpi, ti = lax.axis_index("dp"), lax.axis_index("tensor")
    part = dpi * tensor + ti
    cols = D // (dp * tensor)
    gains_biases = lax.dynamic_slice_in_dim(vector[:6], part * cols, cols, 1)
    grad_b_in = lax.dynamic_index_in_dim(vector[6:10].reshape(tensor, b_in.shape[0], dp, hd), ti, 0, False)
    grad_b_in = lax.dynamic_index_in_dim(grad_b_in, dpi, 1, False)
    grad_qv = lax.dynamic_index_in_dim(vector[11:13].reshape(2, 2, pairs, 2, dp, hd), ti % 2, 1, False)
    grad_qv = lax.dynamic_index_in_dim(grad_qv, ti // 2, 2, False)
    grad_qv = lax.dynamic_index_in_dim(grad_qv, dpi, 2, False)
    loss = jnp.sum(vector[10]) / (D * par[10, 0])
    return (
        loss,
        encoded,
        grad_in,
        s_qkv,
        grad_qv,
        s_out,
        s_in,
        grad_b_in,
        s_back,
        gains_biases[:2],
        gains_biases[2:],
    )


def per_device(
    hidden_in, teacher, valid_mask, random_blocks, w_qkv, b_qv, w_out, w_in, b_in, w_back, ln_gains, row_biases
):
    local = hidden_in.shape[0]
    dp, tensor = lax.axis_size("dp"), lax.axis_size("tensor")
    zn = dp // 2
    tokens_total = local * tensor * dp
    c = lax.axis_index("tensor") % 2
    share = ln_gains.shape[1]
    pairs = b_qv.shape[1]
    hd = b_qv.shape[2]
    mask = valid_mask.astype(F32)
    small = small_parts(b_qv, b_in, ln_gains, row_biases, jnp.sum(mask))
    tables = block_tables(random_blocks, c)
    half = share // 2
    wq = jnp.concatenate([w_qkv[k, h * half : (h + 1) * half] for h in range(2) for k in range(3)], axis=1)
    q, k, v, ctx, lse, ctx_rows, hid, w, full_in, full_bt, full_ot, par = gather_attend(
        tables[0], wq, hidden_in, small, w_in, w_back, w_out, pairs, zn, 0
    )
    units = (tensor, D, w_in.shape[1])
    encoded, gmix, gctx, g_in, g_bt, g_ot, vec = row_pass(
        tokens_total, ctx_rows, hidden_in, teacher, mask[:, None], full_in.reshape(units), full_bt.reshape(units),
        full_ot, par, 256,
    )
    grad_in, s_in, s_bt, s_ot, s_q, vector = attend_sum(
        tables, q, k, v, ctx, lse, gctx, hid, w, gmix, g_in.reshape(full_in.shape), g_bt.reshape(full_in.shape),
        g_ot, vec, zn, 1,
    )
    s_qkv = s_q.reshape(pairs, half, 2, 3, HD).transpose(3, 2, 1, 0, 4).reshape(w_qkv.shape)
    s_ot = s_ot.reshape(half, 2, -1).transpose(2, 1, 0).reshape(w_out.shape)
    return finish(vector, par, encoded, grad_in, s_qkv, s_ot, s_in, s_bt.T, b_in, pairs, hd)


def project_attend_kernel(idx_ref, hid_ref, w_ref, b_ref, q_ref, k_ref, v_ref, ctx_ref, lse_ref, lse_t):
    chunk = hid_ref.shape[1] // 2

    def project(i, carry):
        project_rows(i, chunk, hid_ref, w_ref, b_ref[...], q_ref, k_ref, v_ref)
        return carry

    lax.fori_loop(0, 4, project, 0)
    Forward(idx_ref, q_ref, k_ref, v_ref, ctx_ref, lse_ref, lse_t).run(q_ref.shape[0])


def project_attend(idx, hid, w, bias, pairs):
    n = 2 * hid.shape[1]
    heads = SDS((pairs, n, 128), BF)
    blocks = SDS((pairs, n // BLK, BLK, 128), BF)
    return pl.pallas_call(
        project_attend_kernel,
        out_shape=(heads, blocks, blocks, heads, SDS((pairs, n // BLK, 128), F32)),
        in_specs=[SM, VM, VM, VM],
        out_specs=(VM,) * 5,
        scratch_shapes=[pltpu.VMEM((128, 128), F32)],
        compiler_params=params(56),
        name="project_attend",
    )(idx, hid, w, bias)


def attend_back_kernel(
    idx_ref, prev_ref, last_ref, q_ref, k_ref, v_ref, ctx_ref, lse_ref, do_ref, hid_ref, w_ref, gw_ref, gh_ref, gb_ref,
    dq, dk, dv, dk_acc, dv_acc, dk_run, dv_run, hid_t,
):
    pairs = q_ref.shape[0]
    local = hid_ref.shape[1]
    for i in range(2):
        hid_t[:, i * local : (i + 1) * local] = hid_ref[i].T
    attend = Backward(
        idx_ref, prev_ref, last_ref, q_ref, k_ref, v_ref, ctx_ref, do_ref, lse_ref, dq, dk, dv,
        dk_acc, dv_acc, dk_run, dv_run,
    )

    def done(p):
        gw_ref[p] = weight_grad(p, hid_t, dq, dk, dv)
        for n, g in enumerate((dq, dv)):
            gb_ref[p, n : n + 1, :] = jnp.sum(g[p].astype(F32), axis=0, keepdims=True)

    attend.run(pairs, None, done)
    size = local // 4

    def some(i, carry):
        rows = pl.ds(pl.multiple_of(i * size, size), size)
        gh_ref[rows, :] = hidden_grad(dq, dk, dv, w_ref, rows)
        return carry

    lax.fori_loop(0, 8, some, 0)


def attend_back(tables, q, k, v, ctx, lse, do, hid, w):
    pairs, n, _ = q.shape
    slots = 3 * (n // BLK - 2) + 1
    heads = pltpu.VMEM((pairs, n, 128), BF)
    return pl.pallas_call(
        attend_back_kernel,
        out_shape=(SDS((pairs, D, 3 * 128), F32), SDS((n, D), F32), SDS((pairs, 2, 128), F32)),
        in_specs=[SM] * 3 + [VM] * 8,
        out_specs=(VM,) * 3,
        scratch_shapes=[heads] * 3
        + [pltpu.VMEM((n, 128), F32)] * 2
        + [pltpu.VMEM((slots, BLK, 128), F32)] * 2
        + [pltpu.VMEM((D, n), BF)],
        compiler_params=params(60),
        name="attend_back",
    )(*tables, q, k, v, ctx, lse, do, hid, w)


def plain_device(
    hidden_in, teacher, valid_mask, random_blocks, w_qkv, b_qv, w_out, w_in, b_in, w_back, ln_gains, row_biases
):
    local = hidden_in.shape[0]
    dp, tensor = lax.axis_size("dp"), lax.axis_size("tensor")
    tokens_total = local * tensor * dp
    dpi, ti = lax.axis_index("dp"), lax.axis_index("tensor")
    y, c = ti // 2, ti % 2
    pairs, hd = b_qv.shape[1:]
    everyone = ("dp", "tensor")
    mask = valid_mask.astype(F32)
    par = lax.psum(small_parts(b_qv, b_in, ln_gains, row_biases, jnp.sum(mask)), everyone)
    tables = block_tables(random_blocks, c)

    def swap(x):
        there = lax.ppermute(x[1 - c], "tensor", [(i, i ^ 1) for i in range(tensor)])
        here = x[c]
        return jnp.stack([jnp.where(c == 0, here, there), jnp.where(c == 0, there, here)])

    hid = swap(jnp.stack([hidden_in, hidden_in]))
    w = lax.all_gather(lax.all_gather(w_qkv, "dp", axis=1, tiled=True), "tensor", axis=0)
    w = w.reshape(2, 2, 3, D, pairs, HD)[:, c].transpose(2, 1, 3, 0, 4).reshape(D, -1)
    w_o = lax.all_gather(lax.all_gather(w_out, "dp", axis=1, tiled=True), "tensor", axis=0)
    w_o = w_o.reshape(2, 2, pairs, HD, D).transpose(4, 1, 2, 0, 3).reshape(D, D)
    full_in = lax.all_gather(lax.all_gather(w_in, "dp", axis=0, tiled=True), "tensor", axis=0)
    full_bt = lax.all_gather(lax.all_gather(w_back.T, "dp", axis=0, tiled=True), "tensor", axis=0)
    bias = lax.dynamic_index_in_dim(par[11:13].reshape(2, 2, -1), c, 1, False)
    q, k, v, ctx, lse = project_attend(tables[0], hid, w, bias, pairs)
    ctx_rows = swap(ctx.reshape(pairs, 2, local, 128).swapaxes(0, 1))
    encoded, gmix, gctx, g_in, g_bt, g_ot, vec = row_pass(
        tokens_total, ctx_rows, hidden_in, teacher, mask[:, None], full_in, full_bt, w_o, par, 256
    )
    gw, gh, gb = attend_back(tables, q, k, v, ctx, lse, swap(gctx), hid, w)
    there = lax.ppermute(gh.reshape(2, local, D)[1 - c].astype(BF), "tensor", [(i, i ^ 1) for i in range(tensor)])
    grad_in = gmix + gh.reshape(2, local, D)[c] + there.astype(F32)

    def spread(g):
        g = lax.psum_scatter(g, "tensor", scatter_dimension=0, tiled=False)
        return lax.psum_scatter(g, "dp", scatter_dimension=0, tiled=True)

    s_in, s_bt = spread(g_in.astype(F32)), spread(g_bt.astype(F32))
    s_ot = spread(g_ot.astype(F32).reshape(D, 2, pairs, 2, HD).transpose(3, 1, 0, 2, 4).reshape(tensor, D, -1))
    own = (jnp.arange(2) == c).astype(F32)
    gw = gw.reshape(pairs, D, 3, 2, HD).transpose(3, 1, 2, 0, 4).reshape(2, 1, D, -1) * own[None, :, None, None]
    s_qkv = spread(gw.reshape(tensor, D, -1)).reshape(-1, 3, pairs * HD).swapaxes(0, 1)
    gb = gb.swapaxes(0, 1).reshape(2, 1, -1) * own[None, :, None]
    vector = lax.psum(vec.at[11:13].set(gb.reshape(2, D)), everyone)
    return finish(vector, par, encoded, grad_in, s_qkv, s_ot.T, s_in, s_bt.T, b_in, pairs, hd)


def solution(mesh):
    rows = P(("dp", "tensor"), None)
    in_specs = (
        rows,
        rows,
        P(("dp", "tensor")),
        P(),
        P(None, "dp", "tensor"),
        P(None, "tensor", "dp"),
        P("tensor", "dp"),
        P("dp", "tensor"),
        P("tensor", "dp"),
        P("tensor", "dp"),
        P(None, "dp"),
        P(None, "dp"),
    )
    out_specs = (
        P(),
        rows,
        rows,
        P(None, "dp", "tensor"),
        P(None, "tensor", "dp"),
        P("tensor", "dp"),
        P("dp", "tensor"),
        P("tensor", "dp"),
        P("tensor", "dp"),
        P(None, ("dp", "tensor")),
        P(None, ("dp", "tensor")),
    )
    fills_tiles = (D // mesh.shape["dp"]) % 32 == 0
    step = per_device if fills_tiles else plain_device
    return jax.shard_map(step, mesh=mesh, in_specs=in_specs, out_specs=out_specs, check_vma=False)
```

```python
import functools

import jax
import jax.numpy as jnp
from jax import lax
from jax.experimental import pallas as pl
from jax.experimental.pallas import tpu as pltpu
from jax.sharding import PartitionSpec as P

D = 768
HD = 64
BLK = 64
SEQ_LEN = 2048
epsilon = 1e-06
NEG = -1e30
F32 = jnp.float32
BF = jnp.bfloat16
MESH = pl.DeviceIdType.MESH
NT = (((1,), (1,)), ((), ()))
NN = (((1,), (0,)), ((), ()))
TN = (((0,), (0,)), ((), ()))
VM = pl.BlockSpec(memory_space=pltpu.VMEM)
SM = pl.BlockSpec(memory_space=pltpu.SMEM)
ANY = pl.BlockSpec(memory_space=pl.ANY)
SDS = jax.ShapeDtypeStruct


def dot(a, b, dims):
    return lax.dot_general(a, b, dims, preferred_element_type=F32)


def params(mib, cid=None):
    if cid is None:
        return pltpu.CompilerParams(vmem_limit_bytes=mib << 20)
    return pltpu.CompilerParams(vmem_limit_bytes=mib << 20, collective_id=cid, has_side_effects=True)


class Place:
    def __init__(self):
        self.zn = lax.axis_size("dp") // 2
        dp, t = lax.axis_index("dp"), lax.axis_index("tensor")
        self.z, self.x, self.y, self.c = dp // 2, dp % 2, t // 2, t % 2

    def at(self, z=None, x=None, y=None, c=None):
        z = self.z if z is None else z
        x = self.x if x is None else x
        y = self.y if y is None else y
        c = self.c if c is None else c
        return (z * 2 + x, y * 2 + c)

    def peer(self, axis, k=1):
        if axis == "z":
            return self.at(z=(self.z + k) % self.zn)
        return {
            "x": self.at(x=1 - self.x),
            "y": self.at(y=1 - self.y),
            "c": self.at(c=1 - self.c),
        }[axis]

    def peers(self, axes):
        out = []
        for axis in axes:
            for k in range(1, self.zn if axis == "z" else 2):
                out.append(self.peer(axis, k))
        return out


def greet(place, axes):
    barrier = pltpu.get_barrier_semaphore()
    peers = place.peers(axes)
    for peer in peers:
        pl.semaphore_signal(barrier, inc=1, device_id=peer, device_id_type=MESH)
    pl.semaphore_wait(barrier, len(peers))


class Sems:
    def __init__(self, send, recv):
        self.send, self.recv, self.used = send, recv, 0

    def take(self, count):
        at = self.used
        self.used += count
        return at

    def copy(self, i, src, dst, device):
        return pltpu.make_async_remote_copy(
            src_ref=src,
            dst_ref=dst,
            send_sem=self.send.at[i],
            recv_sem=self.recv.at[i],
            device_id=device,
            device_id_type=MESH,
        )


def copies_of(order, zn):
    return sum(zn - 1 if a == "z" else 1 for a in order)


def concat_lanes(parts):
    return jnp.concatenate(parts, axis=1)


class Gather:
    def __init__(self, place, sems, shard, out, spec):
        self.place, self.shard, self.out = place, shard, out
        self.order, self.pre, self.axes, self.cut = spec
        self.sems = sems
        self.base = sems.take(copies_of(self.order, place.zn))

    def piece(self, whole):
        p = self.place
        own = {"y": p.y, "c": p.c, "z": p.z, "x": p.x}
        idx = (slice(None),) * self.pre
        idx += tuple(slice(None) if a in whole else own[a] for a in self.axes)
        return self.out.at[idx + self.cut]

    def mine(self):
        return self.shard.at[(slice(None),) * self.pre + self.cut] if self.cut else self.shard

    def local(self, sem):
        return pltpu.make_async_copy(self.mine(), self.piece(""), sem)

    def copies(self, stage):
        axis, zn = self.order[stage], self.place.zn
        if stage == 0:
            src, dst = self.mine(), self.piece("")
        else:
            src = dst = self.piece(self.order[:stage])
        at = self.base + copies_of(self.order[:stage], zn)
        return [
            self.sems.copy(at + k - 1, src, dst, self.place.peer(axis, k))
            for k in range(1, zn if axis == "z" else 2)
        ]

    def start(self, stage):
        for copy in self.copies(stage):
            copy.start()

    def wait(self, stage):
        for copy in self.copies(stage):
            copy.wait()


class Scatter:
    def __init__(self, place, sems, grad, out, spec, bufs):
        self.place, self.sems, self.grad, self.out = place, sems, grad, out
        self.order, self.pre, self.axes, self.cut = spec
        self.base = sems.take(copies_of(self.order, place.zn))
        self.keep, self.recv, self.send = bufs[0], [bufs[1]] + list(bufs[2::2]), [None] + list(bufs[3::2])
        self.own = {"y": place.y, "c": place.c, "z": place.z, "x": place.x}
        self.size = {"y": 2, "c": 2, "z": place.zn, "x": 2}

    @staticmethod
    def buffers(a, spec, zn):
        order, pre, axes, cut = spec
        size = {"y": 2, "c": 2, "z": zn, "x": 2}
        lead, tail = a.shape[:pre], a.shape[pre + len(axes) :]
        tail = tuple(len(range(*s.indices(d))) for s, d in zip(cut, tail)) + tail[len(cut) :]
        out = []
        for n, axis in enumerate(order):
            after = tuple(size[s] for s in axes if s not in order[: n + 1])
            one = lead + after + tail
            if n == 0:
                out.append(pltpu.VMEM(one, BF))
            out.append(pltpu.VMEM(((zn - 1,) if axis == "z" else ()) + one, BF))
            if n > 0:
                out.append(pltpu.VMEM(((zn,) if axis == "z" else ()) + one, BF))
        return out

    def copies(self, stage, only=None):
        p, axis = self.place, self.order[stage]
        at = self.base + copies_of(self.order[:stage], p.zn)
        recv, send = self.recv[stage], self.send[stage]
        if axis == "z":
            return [
                self.sems.copy(at + k - 1, send.at[k], recv.at[k - 1], p.peer("z", k))
                for k in (range(1, p.zn) if only is None else (only,))
            ]
        return [self.sems.copy(at, self.half(1 - self.own[axis]) if stage == 0 else send, recv, p.peer(axis))]

    def half(self, i):
        first = self.order[0]
        idx = (slice(None),) * self.pre + tuple(i if a == first else slice(None) for a in self.axes)
        return self.grad.at[idx + self.cut]

    def kept(self, here):
        return pltpu.make_async_copy(self.half(self.own[self.order[0]]), self.keep, here)

    def begin(self, here):
        self.copies(0)[0].start()
        self.kept(here).start()

    def wait(self, stage, here=None):
        for copy in self.copies(stage):
            copy.wait()
        if stage == 0:
            self.kept(here).wait()

    def total(self, n, lead, coords):
        def at(done):
            return lead + tuple(coords.get(a, self.own[a]) for a in self.axes if a not in done)

        t = self.keep[at(self.order[:1])].astype(F32)
        for m in range(n + 1):
            idx = at(self.order[: m + 1])
            if self.order[m] == "z":
                for k in range(self.place.zn - 1):
                    t = t + self.recv[m][(k,) + idx].astype(F32)
            else:
                t = t + self.recv[m][idx].astype(F32)
        return t

    def each(self, axes, fn, coords=None, lead=()):
        coords = coords or {}
        if len(lead) < self.pre:
            for i in range(self.grad.shape[len(lead)]):
                self.each(axes, fn, coords, lead + (i,))
        elif not axes:
            fn(lead, coords)
        elif axes[0] == "z":

            def body(i, carry):
                self.each(axes[1:], fn, {**coords, "z": i}, lead)
                return carry

            lax.fori_loop(0, self.size["z"], body, 0)
        else:
            for i in range(2):
                self.each(axes[1:], fn, {**coords, axes[0]: i}, lead)

    def add(self, n):
        p = self.place
        if n == len(self.order) - 1:

            def last(lead, coords):
                self.out[lead + self.cut] = self.total(n, lead, coords)

            self.each("", last)
            return
        nxt = self.order[n + 1]
        send = self.send[n + 1]
        left = [a for a in self.axes if a not in self.order[: n + 2]]
        if nxt == "z":
            for k in range(1, p.zn):
                to = (p.z + k) % p.zn

                def put(lead, coords, k=k, to=to):
                    send[(k,) + lead] = self.total(n, lead, {**coords, "z": to}).astype(BF)

                self.each(left, put)
                self.copies(n + 1, k)[0].start()
        else:

            def put(lead, coords):
                idx = lead + tuple(coords[a] for a in left)
                send[idx] = self.total(n, lead, {**coords, nxt: 1 - self.own[nxt]}).astype(BF)

            self.each(left, put)
            self.copies(n + 1)[0].start()


class SumAll:
    def __init__(self, place, sems, value, out, order, recv, held):
        self.order = order
        self.place, self.sems, self.value, self.out, self.recv, self.held = place, sems, value, out, recv, held
        self.base = sems.take(copies_of(self.order, place.zn))

    @staticmethod
    def buffers(a, order, zn):
        hops = len(order)
        return [pltpu.VMEM((hops - 2 + zn,) + a.shape, F32), pltpu.VMEM((hops - 1,) + a.shape, F32)]

    def copies(self, n):
        p = self.place
        axis = self.order[n]
        src = self.value if n == 0 else self.held.at[n - 1]
        at = self.base + n
        return [
            self.sems.copy(at + k - 1, src, self.recv.at[n + k - 1], p.peer(axis, k))
            for k in range(1, p.zn if axis == "z" else 2)
        ]

    def begin(self, here=None):
        self.copies(0)[0].start()

    def wait(self, n, here=None):
        for copy in self.copies(n):
            copy.wait()

    def add(self, n):
        mine = self.value[...] if n == 0 else self.held[n - 1]
        if n == len(self.order) - 1:
            for k in range(self.place.zn - 1):
                mine = mine + self.recv[n + k]
            self.out[...] = mine
            return
        self.held[n] = mine + self.recv[n]
        for copy in self.copies(n + 1):
            copy.start()


AFTER = 90


class Due:
    def __init__(self):
        self.todo = {}

    def add(self, step, fn):
        self.todo.setdefault(step, []).append(fn)

    def now(self, step):
        for fn in self.todo.get(step, []):
            fn()

    def __call__(self, g, first=0, last=AFTER):
        for step, fns in sorted(self.todo.items()):
            if first <= step < last:

                @pl.when(g == step - first)
                def _(fns=fns):
                    for fn in fns:
                        fn()


def relay(table, jobs, waves, window, finish):
    due, stage, behind = Due(), {}, list(waves[window:])
    for step, name in table:
        n = stage.get(name, 0)
        stage[name] = n + 1
        wave = [w for w in waves if name in w]
        begin = []
        if n == 0 and behind and wave and all(stage.get(other) for other in wave[0]):
            begin = behind.pop(0)
        due.add(step, functools.partial(finish, name, n, begin))
    assert not behind and all(stage.get(name) == len(job.order) for name, job in jobs.items())
    return due


UNROLL = 5


def stack_heads(q):
    lo = lax.broadcasted_iota(jnp.int32, q.shape, 1) < HD
    z = jnp.zeros_like(q)
    return jnp.concatenate([jnp.where(lo, q, z), jnp.where(lo, z, q)], axis=0)


def block_rows(j, count=1):
    return pl.ds(pl.multiple_of(j * BLK, BLK), count * BLK)


def flat_rows(t):
    return t.reshape(t.shape[0] * t.shape[1], t.shape[2])


def picks_of(idx_ref, p, j):
    pairs = idx_ref.shape[0] // 2
    return [(idx_ref[p, j * 3 + r], idx_ref[pairs + p, j * 3 + r]) for r in range(3)]


def slots_of(ref, p, j, picks, nb):
    lo = lax.broadcasted_iota(jnp.int32, (BLK, 2 * HD), 1) < HD
    parts = [ref[p, 0], ref[p, nb - 1], flat_rows(ref[p, pl.ds(j - 1, 3)])]
    for a, b in picks:
        parts.append(jnp.where(lo, ref[p, a], ref[p, b]))
    return jnp.concatenate(parts, axis=0)


class Forward:
    def __init__(self, idx_ref, q_ref, k_ref, v_ref, ctx_ref, lse_ref, lse_t):
        self.idx, self.q, self.k, self.v, self.ctx, self.lse, self.lse_t = (
            idx_ref,
            q_ref,
            k_ref,
            v_ref,
            ctx_ref,
            lse_ref,
            lse_t,
        )
        self.nb = q_ref.shape[1] // BLK
        self.steps = (self.nb - 2) // UNROLL

    def close(self, p, j, s, v):
        lo = lax.broadcasted_iota(jnp.int32, (BLK, 2 * HD), 1) < HD
        col = lax.broadcasted_iota(jnp.int32, (2 * BLK, 128), 1)
        m = jnp.max(s, axis=1, keepdims=True)
        e = jnp.exp(s - m)
        total = jnp.sum(e, axis=1, keepdims=True)
        o = dot(e.astype(BF), v, NN) * (1.0 / total)
        self.ctx[p, block_rows(j), :] = jnp.where(lo, o[:BLK], o[BLK:]).astype(BF)
        self.lse_t[...] = jnp.where(col == j, m + jnp.log(total), self.lse_t[...])

    def edges(self, p):
        for j in (0, self.nb - 1):
            q = stack_heads(self.q[p, j * BLK : (j + 1) * BLK, :])
            self.close(p, j, dot(q, flat_rows(self.k[p]), NT), flat_rows(self.v[p]))

    def tile(self, p, j):
        picks = picks_of(self.idx, p, j)
        q = stack_heads(self.q[p, block_rows(j), :])
        ks = slots_of(self.k, p, j, picks, self.nb)
        vs = slots_of(self.v, p, j, picks, self.nb)
        s = dot(q, ks, NT)
        col = lax.broadcasted_iota(jnp.int32, (2 * BLK, 128), 1)
        double = ((col < BLK) & (j == 1)) | ((col >= BLK) & (j == self.nb - 2))
        s = jnp.concatenate([jnp.where(double, NEG, s[:, :128]), s[:, 128:]], axis=1)
        self.close(p, j, s, vs)

    def step(self, p, i):
        for u in range(UNROLL):
            self.tile(p, 1 + i * UNROLL + u)

    def finish(self, p):
        self.lse[p] = jnp.transpose(self.lse_t[...])[: self.nb]

    def run(self, pairs, at=None):
        def body(g, carry):
            p, i = g // self.steps, g % self.steps
            if at is not None:
                at(g)

            @pl.when(i == 0)
            def _():
                self.edges(p)

            self.step(p, i)

            @pl.when(i == self.steps - 1)
            def _():
                self.finish(p)

            return carry

        lax.fori_loop(0, pairs * self.steps, body, 0)


def delta_row(do, ctx):
    d = jnp.transpose(do.astype(F32) * ctx.astype(F32))
    a = jnp.sum(d[:HD], axis=0, keepdims=True)
    b = jnp.sum(d[HD:], axis=0, keepdims=True)
    return jnp.concatenate([a, b], axis=1)


class Backward:
    def __init__(self, idx_ref, prev_ref, last_ref, q, k, v, ctx, do, lse, dq, dk, dv, dk_acc, dv_acc, dk_run, dv_run):
        self.idx, self.prev, self.last = idx_ref, prev_ref, last_ref
        self.q, self.k, self.v, self.ctx, self.do, self.lse = q, k, v, ctx, do, lse
        self.dq, self.dk, self.dv = dq, dk, dv
        self.accs = ((dk_acc, dk_run), (dv_acc, dv_run))
        self.nb = q.shape[1] // BLK
        self.steps = (self.nb - 2) // UNROLL

    def math(self, q, do, ks, vs, lse, delta, double=None):
        st = dot(ks, q, NT)
        pt = jnp.exp(st - lse)
        if double is not None:
            pt = jnp.concatenate([jnp.where(double, 0.0, pt[:128]), pt[128:]], axis=0)
        dst = (pt * (dot(vs, do, NT) - delta)).astype(BF)
        return dot(dst, ks, TN), dot(dst, q, NN), dot(pt.astype(BF), do, NN)

    def edges(self, p):
        qs, dos, ls, ds = [], [], [], []
        lo = lax.broadcasted_iota(jnp.int32, (BLK, 2 * HD), 1) < HD
        for j in (0, self.nb - 1):
            rows = slice(j * BLK, (j + 1) * BLK)
            do = self.do_block(p, j)
            qs.append(stack_heads(self.q[p, rows, :]))
            dos.append(stack_heads(do))
            ls.append(self.lse[p, j : j + 1, :])
            ds.append(delta_row(do, self.ctx[p, rows, :]))
        q, do = jnp.concatenate(qs, axis=0), jnp.concatenate(dos, axis=0)
        lse, delta = jnp.concatenate(ls, axis=1), jnp.concatenate(ds, axis=1)
        dq_sum = jnp.zeros((4 * BLK, 2 * HD), F32)
        for n in range(self.nb // 8):
            r = slice(n * 8 * BLK, (n + 1) * 8 * BLK)
            ks, vs = flat_rows(self.k[p, n * 8 : (n + 1) * 8]), flat_rows(self.v[p, n * 8 : (n + 1) * 8])
            dq, dk, dv = self.math(q, do, ks, vs, lse, delta)
            dq_sum = dq_sum + dq
            self.accs[0][0][r, :] = dk
            self.accs[1][0][r, :] = dv
        dq_sum = dq_sum * 0.125
        for n, j in enumerate((0, self.nb - 1)):
            part = dq_sum[n * 2 * BLK : (n + 1) * 2 * BLK]
            self.dq[p, j * BLK : (j + 1) * BLK, :] = jnp.where(lo, part[:BLK], part[BLK:]).astype(BF)
        for _, run in self.accs:
            run[0] = jnp.zeros((BLK, 2 * HD), F32)

    def do_block(self, p, j):
        half = self.nb // 2
        if isinstance(j, int):
            return self.do[j // half, p, (j % half) * BLK : (j % half + 1) * BLK, :]
        return self.do[j // half, p, block_rows(j % half), :]

    def tile(self, p, j):
        lo = lax.broadcasted_iota(jnp.int32, (BLK, 2 * HD), 1) < HD
        row = lax.broadcasted_iota(jnp.int32, (2 * BLK, 128), 0)
        nb, pairs = self.nb, self.idx.shape[0] // 2
        picks = picks_of(self.idx, p, j)
        q, do = self.q[p, block_rows(j), :], self.do_block(p, j)
        delta = delta_row(do, self.ctx[p, block_rows(j), :])
        ks = slots_of(self.k, p, j, picks, nb)
        vs = slots_of(self.v, p, j, picks, nb)
        double = ((row < BLK) & (j == 1)) | ((row >= BLK) & (j == nb - 2))
        dq, dk, dv = self.math(
            stack_heads(q), stack_heads(do), ks, vs, self.lse[p, pl.ds(j, 1), :], delta, double
        )
        self.dq[p, block_rows(j), :] = (jnp.where(lo, dq[:BLK], dq[BLK:]) * 0.125).astype(BF)
        for (acc, run), g in zip(self.accs, (dk, dv)):
            acc[0:BLK, :] += g[0:BLK]
            acc[(nb - 1) * BLK : nb * BLK, :] += g[BLK : 2 * BLK]
            acc[block_rows(j - 1, 3), :] += g[2 * BLK : 5 * BLK]
            for r in range(3):
                s = j * 3 + r
                before = jnp.where(lo, run[self.prev[p, s]], run[self.prev[pairs + p, s]])
                run[s - 2] = g[(5 + r) * BLK : (6 + r) * BLK] + before

    def step(self, p, i):
        for u in range(UNROLL):
            self.tile(p, 1 + i * UNROLL + u)

    def finish(self, p):
        lo = lax.broadcasted_iota(jnp.int32, (BLK, 2 * HD), 1) < HD
        pairs = self.idx.shape[0] // 2

        def body(n, carry):
            a, b = self.last[p, n], self.last[pairs + p, n]
            for (acc, run), out in zip(self.accs, (self.dk, self.dv)):
                t = acc[block_rows(n), :] + jnp.where(lo, run[a], run[b])
                out[p, block_rows(n), :] = t.astype(BF)
            return carry

        lax.fori_loop(0, self.nb, body, 0)

    def run(self, pairs, at=None, done=None):
        def body(g, carry):
            p, i = g // self.steps, g % self.steps
            if at is not None:
                at(g)

            @pl.when(i == 0)
            def _():
                self.edges(p)

            self.step(p, i)

            @pl.when(i == self.steps - 1)
            def _():
                self.finish(p)
                if done is not None:
                    done(p)

            return carry

        lax.fori_loop(0, pairs * self.steps, body, 0)


def block_tables(random_blocks, place_c):
    heads, blocks = random_blocks.shape[:2]
    own = lax.dynamic_index_in_dim(
        random_blocks.reshape((2, 2, heads // 4) + random_blocks.shape[1:]), place_c, 1, False
    ).reshape(heads // 2, blocks * 3, blocks)
    idx = jnp.sum(own * jnp.arange(blocks, dtype=jnp.int32), axis=-1)
    slots = blocks * 3
    s = jnp.arange(slots, dtype=jnp.int32)
    middle = (s >= 3) & (s < slots - 3)
    number = jnp.where(middle, s - 2, 0)
    same = (idx[:, :, None] == idx[:, None, :]) & (s[None, None, :] < s[None, :, None])
    prev = jnp.max(jnp.where(same, number[None, None, :], 0), axis=-1)
    last = jnp.max(jnp.where(own > 0, number[None, :, None], 0), axis=1)
    return idx, prev, last
SMALL_ROWS = 16


FORWARD_TABLE = (
    (-1000, "q0b"),
    (-999, "q1b"),
    (-998, "q0a"),
    (-997, "q1a"),
    (-996, "q0b"),
    (-995, "q1b"),
    (-994, "q0a"),
    (-993, "q1a"),
    (-992, "q2b"),
    (-991, "q0b"),
    (-990, "q1b"),
    (-989, "q2a"),
    (-988, "a0"),
    (-987, "b0"),
    (-986, "q2b"),
    (-985, "q1a"),
    (-984, "q0a"),
    (-983, "q2a"),
    (-982, "q2b"),
    (-981, "b0"),
    (-980, "a0"),
    (-979, "a1"),
    (-978, "b1"),
    (-977, "q2a"),
    (0, "o"),
    (1, "a2"),
    (1, "b2"),
    (5, "a1"),
    (6, "b0"),
    (6, "a2"),
    (7, "o"),
    (7, "b1"),
    (9, "b0"),
    (9, "b2"),
    (11, "a0"),
    (14, "a0"),
    (16, "a1"),
    (17, "a2"),
    (17, "o"),
    (18, "a1"),
    (19, "b1"),
    (20, "b2"),
    (20, "o"),
    (20, "a2"),
    (AFTER, "b1"),
    (AFTER, "b2"),
)
FORWARD_WINDOW = 2


def assemble_qkv(p, parts, w):
    zn, half = parts.shape[2], parts.shape[4]

    def body(n, carry):
        z, x = n // 2, n % 2
        for h in range(2):
            rows = pl.ds(pl.multiple_of(n * 2 * half + h * half, half), half)
            src = [parts[p, y, z, x, :, h * 3 * HD : (h + 1) * 3 * HD] for y in range(2)]
            for k in range(3):
                w[p, rows, k * 128 : (k + 1) * 128] = concat_lanes([s[:, k * HD : (k + 1) * HD] for s in src])
        return carry

    lax.fori_loop(0, zn * 2, body, 0)


def project_rows(p, i, chunk, hid, w, bias, q, k, v):
    per = hid.shape[1] // chunk
    src = hid[i // per, pl.ds(pl.multiple_of(i % per * chunk, chunk), chunk), :]
    t = dot(src, w[p], NN)
    part = (t[:, :128] + bias[0:1, :]).astype(BF).astype(F32) * 0.125
    q[p, pl.ds(pl.multiple_of(i * chunk, chunk), chunk), :] = part.astype(BF)
    rows = pl.ds(i * (chunk // BLK), chunk // BLK)
    k[p, rows] = t[:, 128:256].astype(BF).reshape(chunk // BLK, BLK, 128)
    v[p, rows] = (t[:, 256:] + bias[1:2, :]).astype(BF).reshape(chunk // BLK, BLK, 128)


def place_small(place, out, b_qv, b_in, ln_gains, row_biases, mask):
    def lane(rows):
        return lax.broadcasted_iota(jnp.int32, (rows, D), 1)

    def row(rows):
        return lax.broadcasted_iota(jnp.int32, (rows, D), 0)

    def ones(where):
        return where.astype(F32).astype(BF)

    dp = place.z * 2 + place.x
    t = place.y * 2 + place.c
    pairs, _, n = b_qv.shape
    units = b_in.shape[1]
    share = ln_gains.shape[1]
    out[...] = jnp.zeros_like(out)
    wide = dot(b_in[...], ones(lane(units) // HD == row(units)), NN)
    own = jnp.sum(jnp.where(lane(n) % HD == dp * n + row(n), wide, 0.0), axis=0, keepdims=True)
    for i in range(4):
        out[i : i + 1, :] = jnp.where(t == i, own, 0.0)
    at = ones(lane(share) == dp * share + row(share))
    one = jnp.where(t == 0, 1.0, 0.0)
    out[4:6, :] = dot(ln_gains[...], at, NN) * one
    out[6:10, :] = dot(row_biases[...], at, NN) * one
    count = jnp.sum(mask[...].astype(F32))
    out[10:11, :] = jnp.where(lane(1) == 0, count, 0.0)
    at = ones(lane(n) % HD == dp * n + row(n))
    total = jnp.zeros((2, D), F32)
    for p in range(pairs):
        here = (lane(2) // 128 == place.c * pairs + p) & (lane(2) % 128 // HD == place.y)
        total = total + jnp.where(here, dot(b_qv[p], at, NN), 0.0)
    out[11:13, :] = total


def gather_attend_kernel(
    idx_ref,
    wqkv_ref,
    h_ref,
    bqv_ref,
    bin_ref,
    gain_ref,
    rowb_ref,
    mask_ref,
    win_ref,
    wbt,
    wo_ref,
    q_ref,
    k_ref,
    v_ref,
    ctx_ref,
    lse_ref,
    rows_ref,
    hidt_ref,
    w_ref,
    fin_ref,
    fbt_ref,
    fot_ref,
    par_ref,
    send,
    recv,
    here,
    hid_ref,
    wq,
    parts,
    small_ref,
    wot,
    s_recv,
    s_held,
    lse_t,
):
    place = Place()
    c = place.c
    local = h_ref.shape[0]
    pairs = q_ref.shape[0]
    share = win_ref.shape[0]
    half = share // 2
    for p in range(pairs):
        cols = slice(p * HD, (p + 1) * HD)
        wq[p] = concat_lanes([wqkv_ref[k, h * half : (h + 1) * half, cols] for h in range(2) for k in range(3)])
    greet(place, "zxyc")
    sems = Sems(send, recv)
    jobs, waves = {}, []
    for p in range(pairs):
        orders = ("zxy", "zyx") if p % 2 == 0 else ("zyx", "zxy")
        lanes = (slice(0, 2 * 128), slice(2 * 128, 3 * 128))
        for name, order, lane in zip("ab", orders, lanes):
            spec = (order, 0, "yzx", (slice(None), lane))
            jobs[f"q{p}{name}"] = Gather(place, sems, wq.at[p], parts.at[p], spec)
        waves.append([f"q{p}a", f"q{p}b"])
    count = 3
    size = share // count
    for n in range(count):
        rows = (slice(n * size, (n + 1) * size),)
        jobs[f"a{n}"] = Gather(place, sems, win_ref, fin_ref, ("zxyc", 0, "yczx", rows))
        jobs[f"b{n}"] = Gather(place, sems, wbt, fbt_ref, ("zyxc", 0, "yczx", rows))
        waves.append([f"a{n}", f"b{n}"])
    jobs["o"] = Gather(place, sems, wot, fot_ref, ("zyxc", 0, "yczx", ()))
    waves[-1].append("o")
    hid = Gather(place, sems, h_ref, hid_ref, ("c", 0, "c", ()))
    small = SumAll(place, sems, small_ref, par_ref, "cyxz", s_recv, s_held)
    swap_at = sems.take(pairs)
    for wave in waves[:FORWARD_WINDOW]:
        for name in wave:
            jobs[name].start(0)
    hid.start(0)
    own = [pltpu.make_async_copy(wq.at[p], parts.at[p, place.y, place.z, place.x], here.at[p]) for p in range(pairs)]
    own.append(hid.local(here.at[pairs]))
    for copy in own:
        copy.start()
    place_small(place, small_ref, bqv_ref, bin_ref, gain_ref, rowb_ref, mask_ref)
    small.begin()
    t = wo_ref[...].T
    wot[...] = concat_lanes([t[:half], t[half:]])
    late = [
        pltpu.make_async_copy(src, out.at[place.y, c, place.z, place.x], here.at[pairs + 1 + n])
        for n, (src, out) in enumerate(((win_ref, fin_ref), (wbt, fbt_ref), (wot, fot_ref)))
    ]
    for copy in late:
        copy.start()
    for copy in own + late:
        copy.wait()

    def pass_on(name, stage, begin):
        jobs[name].wait(stage)
        if stage + 1 < len(jobs[name].order):
            jobs[name].start(stage + 1)
        for other in begin:
            jobs[other].start(0)

    due = relay(FORWARD_TABLE, jobs, waves, FORWARD_WINDOW, pass_on)
    early = sorted(step for step in due.todo if step < 0)
    for n, step in enumerate(early):
        due.now(step)
        if n == 1:
            hid.wait(0)
            for i in range(2):
                hidt_ref[:, i * local : (i + 1) * local] = hid_ref[i].T
        if n < 4:
            small.wait(n)
            small.add(n)
    chunk = local // 2
    attend = Forward(idx_ref, q_ref, k_ref, v_ref, ctx_ref, lse_ref, lse_t)

    def there(p):
        rows = pl.ds(pl.multiple_of((1 - c) * local, local), local)
        return sems.copy(swap_at + p, ctx_ref.at[p, rows, :], rows_ref.at[c, p], place.peer("c"))

    bias = jnp.where(c == 0, par_ref[11:13, : pairs * 128], par_ref[11:13, pairs * 128 :])
    for p in range(pairs):
        assemble_qkv(p, parts, w_ref)

    def project(i, carry):
        due(i, 0, 4)
        for p in range(pairs):
            project_rows(p, i, chunk, hid_ref, w_ref, bias[:, p * 128 : (p + 1) * 128], q_ref, k_ref, v_ref)
        return carry

    lax.fori_loop(0, 4, project, 0)
    attend.run(pairs, lambda g: due(g, 4))
    for p in range(pairs):
        there(p).start()
    mine = pltpu.make_async_copy(
        ctx_ref.at[:, pl.ds(pl.multiple_of(c * local, local), local), :], rows_ref.at[c], here.at[0]
    )
    mine.start()
    due.now(AFTER)
    mine.wait()
    for p in range(pairs):
        there(p).wait()


def gather_attend(idx, w_qkv, hidden, smalls, w_in, w_bt, w_out, pairs, zn, cid):
    local = hidden.shape[0]
    n = 2 * local
    share, wide = w_in.shape
    heads_shape = SDS((pairs, n, 128), BF)
    blocks_shape = SDS((pairs, n // BLK, BLK, 128), BF)
    packed = (share // 2, 6 * HD)
    small = SDS((SMALL_ROWS, D), F32)
    copies = 2 * pairs * copies_of("zxy", zn) + 1 + copies_of("cyxz", zn) + 7 * copies_of("zxyc", zn) + pairs
    return pl.pallas_call(
        gather_attend_kernel,
        out_shape=(
            heads_shape,
            blocks_shape,
            blocks_shape,
            heads_shape,
            SDS((pairs, n // BLK, 128), F32),
            SDS((2, pairs, local, 128), BF),
            SDS((D, n), BF),
            SDS((pairs, D, 3 * 128), BF),
            SDS((2, 2, zn, 2, share, wide), BF),
            SDS((2, 2, zn, 2, share, wide), BF),
            SDS((2, 2, zn, 2) + packed, BF),
            SDS(small.shape, F32),
        ),
        in_specs=[SM, VM, ANY] + [VM] * len(smalls) + [ANY, ANY, VM],
        out_specs=(VM,) * 5 + (ANY, VM, VM, ANY, ANY, ANY, VM),
        scratch_shapes=[
            pltpu.SemaphoreType.DMA((copies,)),
            pltpu.SemaphoreType.DMA((copies,)),
            pltpu.SemaphoreType.DMA((pairs + 4,)),
            pltpu.VMEM((2, local, D), BF),
            pltpu.VMEM((pairs,) + packed, BF),
            pltpu.VMEM((pairs, 2, zn, 2) + packed, BF),
            pltpu.VMEM(small.shape, F32),
            pltpu.VMEM(packed, BF),
        ]
        + SumAll.buffers(small, "cyxz", zn)
        + [pltpu.VMEM((128, 128), F32)],
        compiler_params=params(56, cid),
        name="gather_attend",
    )(idx, w_qkv, hidden, *smalls, w_in, w_bt, w_out)
def norm(v):
    centred = v - jnp.mean(v, axis=-1, keepdims=True)
    rs = lax.rsqrt(jnp.mean(centred * centred, axis=-1, keepdims=True) + epsilon)
    return centred * rs, rs


def norm_back(g, gain, xhat, rs):
    gx = gain * g
    return rs * (gx - jnp.mean(gx, axis=-1, keepdims=True) - xhat * jnp.mean(gx * xhat, axis=-1, keepdims=True))


def gelu_both(v):
    k, a = 0.7978845608028654, 0.044715
    v2 = v * v
    th = jnp.tanh(k * v * (1.0 + a * v2))
    half = 0.5 * (1.0 + th)
    slope = half + (0.5 * k) * v * (1.0 - th * th) * (1.0 + (3.0 * a) * v2)
    return v * half, slope


def assemble_out(parts, w):
    zn, half = parts.shape[2], parts.shape[4]
    wide = parts.shape[5] // 2
    pairs = wide // HD

    def body(n, carry):
        z, x = n // 2, n % 2
        for h in range(2):
            rows = pl.ds(pl.multiple_of(n * 2 * half + h * half, half), half)
            for c in range(2):
                for p in range(pairs):
                    at = h * wide + p * HD
                    w[rows, (c * pairs + p) * 128 : (c * pairs + p + 1) * 128] = concat_lanes(
                        [parts[y, c, z, x, :, at : at + HD] for y in range(2)]
                    )
        return carry

    lax.fori_loop(0, zn * 2, body, 0)


def scatter_out(w, parts):
    zn, half = parts.shape[2], parts.shape[4]
    wide = parts.shape[5] // 2
    pairs = wide // HD

    def body(n, carry):
        z, x = n // 2, n % 2
        src = [w[pl.ds(pl.multiple_of(n * 2 * half + h * half, half), half), :] for h in range(2)]
        for y in range(2):
            for c in range(2):
                cols = [(c * pairs + p) * 128 + y * HD for p in range(pairs)]
                parts[y, c, z, x] = concat_lanes([s[:, a : a + HD] for s in src for a in cols]).astype(BF)
        return carry

    lax.fori_loop(0, zn * 2, body, 0)


def mask_rows(m_ref, step, tile):
    columns = m_ref[...].astype(F32).T
    at = lax.broadcasted_iota(jnp.int32, columns.shape, 1)
    per = tile // 128
    parts = [
        jnp.sum(jnp.where(at == step * per + i, columns, 0.0), axis=1, keepdims=True) for i in range(per)
    ]
    return jnp.concatenate(parts, axis=0)


def rows_kernel(
    tokens_total,
    packed,
    ctx_ref,
    h_ref,
    t_ref,
    m_ref,
    w_in,
    w_bt,
    w_ot,
    par,
    enc_ref,
    gmix_ref,
    gctx_ref,
    gin_ref,
    gbt_ref,
    got_ref,
    vec_ref,
    slope,
    act,
    ginner,
    nlow_t,
    slow_t,
    w_o,
    got,
):
    step = pl.program_id(0)
    tile = h_ref.shape[0]
    units = w_in.shape[0]
    pairs = ctx_ref.shape[1]
    r = pl.ds(pl.multiple_of(step * tile, tile), tile)

    @pl.when(step == 0)
    def _():
        vec_ref[...] = jnp.zeros_like(vec_ref)
        got[...] = jnp.zeros_like(got)
        if packed:
            assemble_out(w_ot, w_o)
        else:
            w_o[...] = w_ot[...]

    gains, biases = par[4:6, :], par[6:10, :]
    scale = tokens_total / par[10:11, 0:1]
    ctx = concat_lanes([ctx_ref[n, p] for n in range(2) for p in range(pairs)])
    mixed = h_ref[...].astype(F32) + dot(ctx, w_o[...], NT) + biases[0:1, :]
    xhat1, rs1 = norm(mixed)
    normed = xhat1 * gains[0:1, :] + biases[1:2, :]
    nlow = normed.astype(BF)
    nlow_t[:, r] = nlow.T
    second = normed + biases[2:3, :]
    for u in range(units):
        inner = dot(nlow, w_in[u], NN) + par[u : u + 1, :]
        a, s = gelu_both(inner)
        a = a.astype(BF)
        act[u, r, :] = a
        slope[u] = s
        second = second + dot(a, w_bt[u], NT)
    xhat2, rs2 = norm(second)
    encoded = xhat2 * gains[1:2, :] + biases[3:4, :]
    enc_ref[...] = encoded
    error = encoded - t_ref[...]
    merr = mask_rows(m_ref, step, tile) * error
    genc = merr * scale
    gsec = norm_back(genc, gains[1:2, :], xhat2, rs2)
    slow = gsec.astype(BF)
    slow_t[:, r] = slow.T
    gnorm = gsec
    for u in range(units):
        gi = (dot(slow, w_bt[u], NN) * slope[u]).astype(BF)
        ginner[u, r, :] = gi
        vec_ref[6 + u : 7 + u, :] += jnp.sum(gi.astype(F32), axis=0, keepdims=True)
        gnorm = gnorm + dot(gi, w_in[u], NT)
    gmix = norm_back(gnorm, gains[0:1, :], xhat1, rs1)
    gmix_ref[...] = gmix
    mlow = gmix.astype(BF)
    gctx = dot(mlow, w_o[...], NN).astype(BF)
    for n in range(2):
        for p in range(pairs):
            gctx_ref[n, p] = gctx[:, (n * pairs + p) * 128 : (n * pairs + p + 1) * 128]
    sums = (gnorm * xhat1, genc * xhat2, gmix, gnorm, gsec, genc)
    for n, value in enumerate(sums):
        vec_ref[n : n + 1, :] += jnp.sum(value, axis=0, keepdims=True)
    vec_ref[10:11, :] += jnp.sum(merr * error, axis=0, keepdims=True)
    got[...] += dot(mlow.T, ctx, NN)

    @pl.when(step == pl.num_programs(0) - 1)
    def _():
        if packed:
            scatter_out(got, got_ref)
        else:
            got_ref[...] = got[...].astype(BF)
        for u in range(units):
            gin_ref[u] = dot(nlow_t[...], ginner[u], NN).astype(BF)
            gbt_ref[u] = dot(slow_t[...], act[u], NN).astype(BF)


def row_pass(tokens_total, ctx, hidden, teacher, mask, w_in, w_bt, w_ot, par, tile):
    n = hidden.shape[0]
    units, _, wide = w_in.shape
    pairs = ctx.shape[1]
    once = pl.Buffered(1)

    def whole(a):
        return pl.BlockSpec(a.shape, lambda i, nd=len(a.shape): (0,) * nd, pipeline_mode=once)

    def rows(width):
        return pl.BlockSpec((tile, width), lambda i: (i, 0))

    heads = pl.BlockSpec((2, pairs, tile, 128), lambda i: (0, 0, i, 0))
    outs = (
        SDS((n, D), F32),
        SDS((n, D), F32),
        SDS((2, pairs, n, 128), BF),
        SDS(w_in.shape, BF),
        SDS(w_in.shape, BF),
        SDS(w_ot.shape, BF),
        SDS((SMALL_ROWS, D), F32),
    )
    return pl.pallas_call(
        functools.partial(rows_kernel, float(tokens_total), len(w_ot.shape) > 2),
        grid=(n // tile,),
        out_shape=outs,
        in_specs=[heads, rows(D), rows(D)] + [whole(a) for a in (mask, w_in, w_bt, w_ot, par)],
        out_specs=(rows(D), rows(D), heads) + tuple(whole(a) for a in outs[3:]),
        scratch_shapes=[
            pltpu.VMEM((units, tile, wide), F32),
            pltpu.VMEM((units, n, wide), BF),
            pltpu.VMEM((units, n, wide), BF),
            pltpu.VMEM((D, n), BF),
            pltpu.VMEM((D, n), BF),
            pltpu.VMEM((D, D), BF),
            pltpu.VMEM((D, D), F32),
        ],
        compiler_params=params(62),
        name="row_pass",
    )(ctx, hidden, teacher, mask, w_in, w_bt, w_ot, par)
BACKWARD_TABLE = (
    (0, "a0"),
    (0, "b0"),
    (2, "a1"),
    (2, "b1"),
    (4, "v"),
    (5, "a0"),
    (5, "o"),
    (5, "b0"),
    (6, "a2"),
    (6, "b2"),
    (6, "v"),
    (7, "a1"),
    (8, "v"),
    (8, "b0"),
    (9, "b1"),
    (10, "v"),
    (11, "q0a"),
    (11, "a0"),
    (11, "q0b"),
    (12, "b0"),
    (13, "a0"),
    (13, "q0b"),
    (13, "o"),
    (13, "b1"),
    (13, "a2"),
    (13, "a1"),
    (14, "q0a"),
    (14, "q1b"),
    (15, "q0b"),
    (16, "o"),
    (17, "b2"),
    (AFTER, "q1b"),
    (AFTER, "q1a"),
    (AFTER, "q0a"),
    (AFTER, "b1"),
    (AFTER, "a2"),
    (AFTER, "a1"),
    (AFTER, "o"),
    (AFTER, "b2"),
    (AFTER + 1, "s"),
    (AFTER + 1, "q1b"),
    (AFTER + 1, "q2b"),
    (AFTER + 3, "s"),
    (AFTER + 3, "q1a"),
    (AFTER + 3, "a2"),
    (AFTER + 3, "q2a"),
    (AFTER + 3, "b2"),
    (AFTER + 3, "q2b"),
    (AFTER + 3, "s"),
    (AFTER + 3, "q1a"),
    (AFTER + 3, "q2b"),
    (AFTER + 3, "q2a"),
    (AFTER + 3, "q2a"),
)
BACKWARD_WINDOW = 1
CHUNKS = 3


def sum_specs(share, pairs):
    size = share // CHUNKS
    specs = []
    for n in range(CHUNKS):
        rows = (slice(n * size, (n + 1) * size),)
        specs.append((f"a{n}", "in", ("cyxz", 0, "yczx", rows)))
        specs.append((f"b{n}", "back", ("cxyz", 0, "yczx", rows)))
    specs.append(("o", "out", ("cxyz", 0, "yczx", ())))
    for p in range(pairs):
        orders = ("yxz", "xyz") if p % 2 == 0 else ("xyz", "yxz")
        lanes = (slice(0, 2 * 128), slice(2 * 128, 3 * 128))
        for name, order, lane in zip("ab", orders, lanes):
            specs.append((f"q{p}{name}", p, (order, 0, "yzx", (slice(None), lane))))
    return specs


def weight_grad(p, hid_t, dq, dk, dv):
    return dot(hid_t[...], concat_lanes([dq[p], dk[p], dv[p]]), NN)


def hidden_grad(dq, dk, dv, w, rows):
    pairs = dq.shape[0]
    grads = concat_lanes([g[p, rows, :] for p in range(pairs) for g in (dq, dk, dv)])
    return dot(grads, concat_lanes([w[p] for p in range(pairs)]), NT)


def attend_sum_kernel(
    idx_ref,
    prev_ref,
    last_ref,
    q_ref,
    k_ref,
    v_ref,
    ctx_ref,
    lse_ref,
    gctx_ref,
    hid_t,
    w_ref,
    gmix_ref,
    gin_ref,
    gbt_ref,
    got_ref,
    vec_ref,
    out_ref,
    gh_recv,
    sin_ref,
    sbt,
    sot_ref,
    sq_ref,
    vsum_ref,
    bsum_ref,
    send,
    recv,
    here,
    do_ref,
    dq,
    dk,
    dv,
    dk_acc,
    dv_acc,
    dk_run,
    dv_run,
    gq,
    gh_send,
    bias,
    sot,
    sq,
    v_recv,
    v_held,
    b_recv,
    b_held,
    *bufs,
):
    place = Place()
    c = place.c
    pairs = q_ref.shape[0]
    local = gmix_ref.shape[0]
    share = gin_ref.shape[-2]
    greet(place, "zxyc")
    sems = Sems(send, recv)
    grads = {"in": (gin_ref, sin_ref), "back": (gbt_ref, sbt), "out": (got_ref, sot)}
    for p in range(pairs):
        grads[p] = (gq.at[p], sq.at[p])
    jobs, spot, rest = {}, {}, list(bufs)
    for name, which, spec in sum_specs(share, pairs):
        grad, out = grads[which]
        count = len(Scatter.buffers(grad, spec, place.zn))
        spot[name] = here.at[len(jobs)]
        jobs[name] = Scatter(place, sems, grad, out, spec, rest[:count])
        rest = rest[count:]
    jobs["v"] = SumAll(place, sems, vec_ref, vsum_ref, "cyxz", v_recv, v_held)
    jobs["s"] = SumAll(place, sems, bias, bsum_ref, "yxz", b_recv, b_held)
    spot["v"] = spot["s"] = None
    waves = [[f"a{n}", f"b{n}"] for n in range(CHUNKS)]
    waves[-1] += ["o", "v"]
    swaps = sems.take(2)
    first = sems.copy(swaps, gctx_ref.at[1 - c], do_ref.at[c], place.peer("c"))
    first.start()
    mine = pltpu.make_async_copy(gctx_ref.at[c], do_ref.at[c], here.at[len(jobs)])
    mine.start()
    for wave in waves[:BACKWARD_WINDOW]:
        for name in wave:
            jobs[name].begin(spot[name])
    start_out = pltpu.make_async_copy(gmix_ref, out_ref, here.at[len(jobs) + 1])
    start_out.start()
    bias[...] = jnp.zeros_like(bias)

    def advance(name, stage, begin):
        jobs[name].wait(stage, spot[name])
        jobs[name].add(stage)
        for other in begin:
            jobs[other].begin(spot[other])

    due = relay(BACKWARD_TABLE, jobs, waves, BACKWARD_WINDOW, advance)
    for step in sorted(step for step in due.todo if step < 0):
        due.now(step)
    mine.wait()
    first.wait()
    attend = Backward(
        idx_ref, prev_ref, last_ref, q_ref, k_ref, v_ref, ctx_ref, do_ref, lse_ref, dq, dk, dv,
        dk_acc, dv_acc, dk_run, dv_run,
    )
    half = gq.shape[4]

    def done(p):
        t = weight_grad(p, hid_t, dq, dk, dv).astype(BF)
        for z in range(place.zn):
            for x in range(2):
                at = (z * 2 + x) * 2 * half
                src = [t[at + h * half : at + (h + 1) * half] for h in range(2)]
                for y in range(2):
                    gq[p, y, z, x] = concat_lanes(
                        [s[:, k * 128 + y * HD : k * 128 + (y + 1) * HD] for s in src for k in range(3)]
                    )
        lanes = pl.ds(pl.multiple_of(p * 128, 128), 128)
        for row, g in enumerate((dq, dv)):
            bias[row : row + 1, lanes] = jnp.sum(g[p].astype(F32), axis=0, keepdims=True)
        for n in range(pairs):

            @pl.when(p == n)
            def _(n=n):
                for name in (f"q{n}a", f"q{n}b"):
                    jobs[name].begin(spot[name])

    attend.run(pairs, due, done)
    jobs["s"].begin()
    size = local // 2

    def other(i, carry):
        t = hidden_grad(dq, dk, dv, w_ref, pl.ds(pl.multiple_of((1 - c) * local + i * size, size), size))
        gh_send[pl.ds(pl.multiple_of(i * size, size), size), :] = t.astype(BF)
        return carry

    due.now(AFTER)
    lax.fori_loop(0, 2, other, 0)
    swap = sems.copy(swaps + 1, gh_send, gh_recv, place.peer("c"))
    swap.start()
    start_out.wait()
    due.now(AFTER + 1)

    def own(i, carry):
        rows = pl.ds(pl.multiple_of(i * size, size), size)
        t = hidden_grad(dq, dk, dv, w_ref, pl.ds(pl.multiple_of(c * local + i * size, size), size))
        out_ref[rows, :] += t
        return carry

    lax.fori_loop(0, 2, own, 0)
    due.now(AFTER + 2)
    due.now(AFTER + 3)
    swap.wait()
    t = sot[...]
    wide = pairs * HD
    sot_ref[...] = jnp.concatenate([t[:, :wide], t[:, wide:]], axis=0).T
    for h in range(2):
        for k in range(3):
            at = (h * 3 + k) * HD
            sq_ref[k, h * half : (h + 1) * half, :] = concat_lanes([sq[p, :, at : at + HD] for p in range(pairs)])


def attend_sum(tables, q, k, v, ctx, lse, gctx, hid_t, w, gmix, g_in, g_bt, g_ot, vec, zn, cid):
    pairs, n, _ = q.shape
    local = gmix.shape[0]
    share, wide = g_in.shape[-2:]
    blocks = n // BLK
    packed = g_ot.shape[-2:]
    gq = (pairs, 2, zn, 2) + packed
    heads = pltpu.VMEM((pairs, n, 128), BF)
    bias = SDS((8, pairs * 128), F32)
    shapes = {"in": g_in, "back": g_bt, "out": g_ot}
    bufs = []
    copies = copies_of("cyxz", zn) + copies_of("yxz", zn) + 2
    specs = sum_specs(share, pairs)
    for _, which, spec in specs:
        bufs += Scatter.buffers(shapes.get(which, SDS(gq[1:], BF)), spec, zn)
        copies += copies_of(spec[0], zn)
    return pl.pallas_call(
        attend_sum_kernel,
        out_shape=(
            SDS((local, D), F32),
            SDS((local, D), BF),
            SDS((share, wide), F32),
            SDS((share, wide), F32),
            SDS((pairs * HD, share), F32),
            SDS((3, share, pairs * HD), F32),
            SDS(vec.shape, F32),
            bias,
        ),
        in_specs=[SM] * 3 + [VM] * 5 + [ANY, VM, VM, ANY, ANY, ANY, ANY, VM],
        out_specs=(VM,) * 8,
        scratch_shapes=[
            pltpu.SemaphoreType.DMA((copies,)),
            pltpu.SemaphoreType.DMA((copies,)),
            pltpu.SemaphoreType.DMA((len(specs) + 4,)),
            pltpu.VMEM(gctx.shape, BF),
            heads,
            heads,
            heads,
            pltpu.VMEM((n, 128), F32),
            pltpu.VMEM((n, 128), F32),
            pltpu.VMEM((3 * (blocks - 2) + 1, BLK, 128), F32),
            pltpu.VMEM((3 * (blocks - 2) + 1, BLK, 128), F32),
            pltpu.VMEM(gq, BF),
            pltpu.VMEM((local, D), BF),
            pltpu.VMEM(bias.shape, F32),
            pltpu.VMEM(packed, F32),
            pltpu.VMEM((pairs,) + packed, F32),
        ]
        + SumAll.buffers(vec, "cyxz", zn)
        + SumAll.buffers(bias, "yxz", zn)
        + bufs,
        compiler_params=params(63, cid),
        name="attend_sum",
    )(*tables, q, k, v, ctx, lse, gctx, hid_t, w, gmix, g_in, g_bt, g_ot, vec)


def take_kernel(
    par_ref,
    vec_ref,
    bias_ref,
    part_ref,
    recv_ref,
    sin_ref,
    sbt_ref,
    sot_ref,
    sq_ref,
    loss_ref,
    out_ref,
    oq_ref,
    ob_ref,
    oo_ref,
    oi_ref,
    obin_ref,
    obt_ref,
    og_ref,
    orow_ref,
):
    place = Place()
    dp = place.z * 2 + place.x
    t = place.y * 2 + place.c
    out_ref[...] = part_ref[...] + recv_ref[...].astype(F32)
    oq_ref[...] = sq_ref[...]
    oo_ref[...] = sot_ref[...]
    oi_ref[...] = sin_ref[...]
    obt_ref[...] = sbt_ref[...]
    loss_ref[...] = jnp.sum(vec_ref[10:11, :], axis=1, keepdims=True) / (float(D) * par_ref[10:11, 0:1])

    def exact(a, b):
        return lax.dot_general(a, b, NN, precision=lax.Precision.HIGHEST, preferred_element_type=F32)

    cols = og_ref.shape[1]
    part = dp * 4 + t
    l = lax.broadcasted_iota(jnp.int32, (D, cols), 0)
    i = lax.broadcasted_iota(jnp.int32, (D, cols), 1)
    both = exact(vec_ref[0:8, :], (l == part * cols + i).astype(F32))
    og_ref[...] = both[:2]
    orow_ref[...] = both[2:6]
    n = obin_ref.shape[0]
    units = obin_ref.shape[1]
    row = jnp.zeros((1, D), F32)
    for u in range(4):
        row = row + jnp.where(t == u, 1.0, 0.0) * vec_ref[6 + u : 7 + u, :]
    l = lax.broadcasted_iota(jnp.int32, (n, D), 1)
    i = lax.broadcasted_iota(jnp.int32, (n, D), 0)
    own = jnp.where(l % HD == dp * n + i, row, 0.0)
    l = lax.broadcasted_iota(jnp.int32, (D, units), 0)
    u = lax.broadcasted_iota(jnp.int32, (D, units), 1)
    obin_ref[...] = exact(own, (l // HD == u).astype(F32))
    e = bias_ref.shape[1]
    l = lax.broadcasted_iota(jnp.int32, (e, n), 0)
    i = lax.broadcasted_iota(jnp.int32, (e, n), 1)
    for p in range(ob_ref.shape[0]):
        ob_ref[p] = exact(bias_ref[...], (l == p * 128 + place.y * HD + dp * n + i).astype(F32))[:2]


def take(par, vec, bias, part, recv, s_in, s_bt, s_ot, s_q, b_in_shape, b_qv_shape):
    dp, tensor = lax.axis_size("dp"), lax.axis_size("tensor")
    cols = D // (dp * tensor)
    outs = (
        SDS((1, 1), F32),
        SDS(part.shape, F32),
        SDS(s_q.shape, F32),
        SDS((b_qv_shape[1], b_qv_shape[0], b_qv_shape[2]), F32),
        SDS(s_ot.shape, F32),
        SDS(s_in.shape, F32),
        SDS((b_in_shape[1], b_in_shape[0]), F32),
        SDS(s_bt.shape, F32),
        SDS((2, cols), F32),
        SDS((4, cols), F32),
    )
    return pl.pallas_call(
        take_kernel,
        out_shape=outs,
        in_specs=[VM] * 9,
        out_specs=(VM,) * len(outs),
        compiler_params=params(62),
        name="take_parts",
    )(par, vec, bias, part, recv, s_in, s_bt, s_ot, s_q)


def small_parts(b_qv, b_in, ln_gains, row_biases, count):
    dp, dpi = lax.axis_size("dp"), lax.axis_index("dp")
    t = lax.axis_index("tensor")
    y, c = t // 2, t % 2

    def at(i, size):
        return (jnp.arange(size) == i).astype(F32)

    heads, hd = b_qv.shape[1:]
    units = at(t, 4)[:, None, None, None] * b_in.astype(F32)[None, :, None, :] * at(dpi, dp)[None, None, :, None]
    rows = jnp.concatenate([ln_gains, row_biases]).astype(F32)
    rows = rows[:, None, :] * at(dpi, dp)[None, :, None] * (t == 0).astype(F32)
    total = count * at(0, D)
    bias = b_qv.astype(F32)[:, None, :, None, None, :] * at(c, 2)[None, :, None, None, None, None]
    bias = bias * at(y, 2)[None, None, None, :, None, None] * at(dpi, dp)[None, None, None, None, :, None]
    out = jnp.concatenate([units.reshape(4, D), rows.reshape(6, D), total.reshape(1, D), bias.reshape(2, D)])
    return jnp.pad(out, ((0, SMALL_ROWS - out.shape[0]), (0, 0)))


def finish(vector, bias, par, encoded, grad_in, s_qkv, s_out, s_in, s_back, b_in, pairs, hd):
    dp, tensor = lax.axis_size("dp"), lax.axis_size("tensor")
    dpi, ti = lax.axis_index("dp"), lax.axis_index("tensor")
    part = dpi * tensor + ti
    cols = D // (dp * tensor)
    gains_biases = lax.dynamic_slice_in_dim(vector[:6], part * cols, cols, 1)
    grad_b_in = lax.dynamic_index_in_dim(vector[6:10].reshape(tensor, b_in.shape[0], dp, hd), ti, 0, False)
    grad_b_in = lax.dynamic_index_in_dim(grad_b_in, dpi, 1, False)
    grad_qv = lax.dynamic_index_in_dim(bias.reshape(2, pairs, 2, dp, hd), ti // 2, 2, False)
    grad_qv = lax.dynamic_index_in_dim(grad_qv, dpi, 2, False)
    loss = jnp.sum(vector[10]) / (D * par[10, 0])
    return (
        loss,
        encoded,
        grad_in,
        s_qkv,
        grad_qv,
        s_out,
        s_in,
        grad_b_in,
        s_back,
        gains_biases[:2],
        gains_biases[2:],
    )


def per_device(
    hidden_in, teacher, valid_mask, random_blocks, w_qkv, b_qv, w_out, w_in, b_in, w_back, ln_gains, row_biases
):
    local = hidden_in.shape[0]
    dp, tensor = lax.axis_size("dp"), lax.axis_size("tensor")
    zn = dp // 2
    tokens_total = local * tensor * dp
    pairs = b_qv.shape[1]
    mask = valid_mask.reshape(-1, 128)
    tables = block_tables(random_blocks, lax.axis_index("tensor") % 2)
    q, k, v, ctx, lse, ctx_rows, hid_t, w, full_in, full_bt, full_ot, par = gather_attend(
        tables[0], w_qkv, hidden_in, (b_qv.transpose(1, 0, 2), b_in.T, ln_gains, row_biases, mask), w_in, w_back.T,
        w_out, pairs, zn, 0,
    )
    units = (tensor, D, w_in.shape[1])
    encoded, gmix, gctx, g_in, g_bt, g_ot, vec = row_pass(
        tokens_total, ctx_rows, hidden_in, teacher, mask, full_in.reshape(units), full_bt.reshape(units), full_ot,
        par, 256,
    )
    part, there, s_in, s_bt, s_ot, s_qkv, vector, bias = attend_sum(
        tables, q, k, v, ctx, lse, gctx, hid_t, w, gmix, g_in.reshape(full_in.shape), g_bt.reshape(full_in.shape),
        g_ot, vec, zn, 1,
    )
    loss, grad_in, g_qkv, g_bias, g_out, g_w_in, g_b_in, g_back, g_gains, g_rows = take(
        par, vector, bias, part, there, s_in, s_bt, s_ot, s_qkv, b_in.shape, b_qv.shape
    )
    return (
        loss.reshape(()), encoded, grad_in, g_qkv, g_bias.transpose(1, 0, 2), g_out, g_w_in, g_b_in.T, g_back.T,
        g_gains, g_rows,
    )


def project_attend_kernel(idx_ref, hid_ref, w_ref, b_ref, q_ref, k_ref, v_ref, ctx_ref, lse_ref, lse_t):
    chunk = hid_ref.shape[1] // 2
    for p in range(q_ref.shape[0]):

        def project(i, carry, p=p):
            project_rows(p, i, chunk, hid_ref, w_ref, b_ref[:, p * 128 : (p + 1) * 128], q_ref, k_ref, v_ref)
            return carry

        lax.fori_loop(0, 4, project, 0)
    Forward(idx_ref, q_ref, k_ref, v_ref, ctx_ref, lse_ref, lse_t).run(q_ref.shape[0])


def project_attend(idx, hid, w, bias, pairs):
    n = 2 * hid.shape[1]
    heads = SDS((pairs, n, 128), BF)
    blocks = SDS((pairs, n // BLK, BLK, 128), BF)
    return pl.pallas_call(
        project_attend_kernel,
        out_shape=(heads, blocks, blocks, heads, SDS((pairs, n // BLK, 128), F32)),
        in_specs=[SM, VM, VM, VM],
        out_specs=(VM,) * 5,
        scratch_shapes=[pltpu.VMEM((128, 128), F32)],
        compiler_params=params(56),
        name="project_attend",
    )(idx, hid, w, bias)


def attend_back_kernel(
    idx_ref, prev_ref, last_ref, q_ref, k_ref, v_ref, ctx_ref, lse_ref, do_ref, hid_ref, w_ref, gw_ref, gh_ref, gb_ref,
    dq, dk, dv, dk_acc, dv_acc, dk_run, dv_run, hid_t,
):
    pairs = q_ref.shape[0]
    local = hid_ref.shape[1]
    for i in range(2):
        hid_t[:, i * local : (i + 1) * local] = hid_ref[i].T
    attend = Backward(
        idx_ref, prev_ref, last_ref, q_ref, k_ref, v_ref, ctx_ref, do_ref, lse_ref, dq, dk, dv,
        dk_acc, dv_acc, dk_run, dv_run,
    )

    def done(p):
        gw_ref[p] = weight_grad(p, hid_t, dq, dk, dv)
        for n, g in enumerate((dq, dv)):
            gb_ref[p, n : n + 1, :] = jnp.sum(g[p].astype(F32), axis=0, keepdims=True)

    attend.run(pairs, None, done)
    size = local // 4

    def some(i, carry):
        rows = pl.ds(pl.multiple_of(i * size, size), size)
        gh_ref[rows, :] = hidden_grad(dq, dk, dv, w_ref, rows)
        return carry

    lax.fori_loop(0, 8, some, 0)


def attend_back(tables, q, k, v, ctx, lse, do, hid, w):
    pairs, n, _ = q.shape
    slots = 3 * (n // BLK - 2) + 1
    heads = pltpu.VMEM((pairs, n, 128), BF)
    return pl.pallas_call(
        attend_back_kernel,
        out_shape=(SDS((pairs, D, 3 * 128), F32), SDS((n, D), F32), SDS((pairs, 2, 128), F32)),
        in_specs=[SM] * 3 + [VM] * 8,
        out_specs=(VM,) * 3,
        scratch_shapes=[heads] * 3
        + [pltpu.VMEM((n, 128), F32)] * 2
        + [pltpu.VMEM((slots, BLK, 128), F32)] * 2
        + [pltpu.VMEM((D, n), BF)],
        compiler_params=params(60),
        name="attend_back",
    )(*tables, q, k, v, ctx, lse, do, hid, w)


def plain_device(
    hidden_in, teacher, valid_mask, random_blocks, w_qkv, b_qv, w_out, w_in, b_in, w_back, ln_gains, row_biases
):
    local = hidden_in.shape[0]
    dp, tensor = lax.axis_size("dp"), lax.axis_size("tensor")
    tokens_total = local * tensor * dp
    dpi, ti = lax.axis_index("dp"), lax.axis_index("tensor")
    y, c = ti // 2, ti % 2
    pairs, hd = b_qv.shape[1:]
    everyone = ("dp", "tensor")
    mask = valid_mask.astype(F32)
    par = lax.psum(small_parts(b_qv, b_in, ln_gains, row_biases, jnp.sum(mask)), everyone)
    tables = block_tables(random_blocks, c)

    def swap(x):
        there = lax.ppermute(x[1 - c], "tensor", [(i, i ^ 1) for i in range(tensor)])
        here = x[c]
        return jnp.stack([jnp.where(c == 0, here, there), jnp.where(c == 0, there, here)])

    hid = swap(jnp.stack([hidden_in, hidden_in]))
    w = lax.all_gather(lax.all_gather(w_qkv, "dp", axis=1, tiled=True), "tensor", axis=0)
    w = w.reshape(2, 2, 3, D, pairs, HD)[:, c].transpose(3, 2, 1, 0, 4).reshape(pairs, D, -1)
    w_o = lax.all_gather(lax.all_gather(w_out, "dp", axis=1, tiled=True), "tensor", axis=0)
    w_o = w_o.reshape(2, 2, pairs, HD, D).transpose(4, 1, 2, 0, 3).reshape(D, D)
    full_in = lax.all_gather(lax.all_gather(w_in, "dp", axis=0, tiled=True), "tensor", axis=0)
    full_bt = lax.all_gather(lax.all_gather(w_back.T, "dp", axis=0, tiled=True), "tensor", axis=0)
    bias = lax.dynamic_index_in_dim(par[11:13].reshape(2, 2, -1), c, 1, False)
    q, k, v, ctx, lse = project_attend(tables[0], hid, w, bias, pairs)
    ctx_rows = swap(ctx.reshape(pairs, 2, local, 128).swapaxes(0, 1))
    encoded, gmix, gctx, g_in, g_bt, g_ot, vec = row_pass(
        tokens_total, ctx_rows, hidden_in, teacher, valid_mask.reshape(-1, 128), full_in, full_bt, w_o, par, 256
    )
    gw, gh, gb = attend_back(tables, q, k, v, ctx, lse, swap(gctx), hid, w)
    there = lax.ppermute(gh.reshape(2, local, D)[1 - c].astype(BF), "tensor", [(i, i ^ 1) for i in range(tensor)])
    grad_in = gmix + gh.reshape(2, local, D)[c] + there.astype(F32)

    def spread(g):
        g = lax.psum_scatter(g, "tensor", scatter_dimension=0, tiled=False)
        return lax.psum_scatter(g, "dp", scatter_dimension=0, tiled=True)

    s_in, s_bt = spread(g_in.astype(F32)), spread(g_bt.astype(F32))
    s_ot = spread(g_ot.astype(F32).reshape(D, 2, pairs, 2, HD).transpose(3, 1, 0, 2, 4).reshape(tensor, D, -1))
    own = (jnp.arange(2) == c).astype(F32)
    gw = gw.reshape(pairs, D, 3, 2, HD).transpose(3, 1, 2, 0, 4).reshape(2, 1, D, -1) * own[None, :, None, None]
    s_qkv = spread(gw.reshape(tensor, D, -1)).reshape(-1, 3, pairs * HD).swapaxes(0, 1)
    bias = gb.swapaxes(0, 1).reshape(2, -1)
    bias = lax.psum(bias[:, None, :] * own[None, :, None], everyone)
    bias = lax.dynamic_index_in_dim(bias, c, 1, False)
    vector = lax.psum(vec, everyone)
    return finish(vector, bias, par, encoded, grad_in, s_qkv, s_ot.T, s_in, s_bt.T, b_in, pairs, hd)


def solution(mesh):
    rows = P(("dp", "tensor"), None)
    in_specs = (
        rows,
        rows,
        P(("dp", "tensor")),
        P(),
        P(None, "dp", "tensor"),
        P(None, "tensor", "dp"),
        P("tensor", "dp"),
        P("dp", "tensor"),
        P("tensor", "dp"),
        P("tensor", "dp"),
        P(None, "dp"),
        P(None, "dp"),
    )
    out_specs = (
        P(),
        rows,
        rows,
        P(None, "dp", "tensor"),
        P(None, "tensor", "dp"),
        P("tensor", "dp"),
        P("dp", "tensor"),
        P("tensor", "dp"),
        P("tensor", "dp"),
        P(None, ("dp", "tensor")),
        P(None, ("dp", "tensor")),
    )
    fills_tiles = (D // mesh.shape["dp"]) % 32 == 0
    step = per_device if fills_tiles else plain_device
    return jax.shard_map(step, mesh=mesh, in_specs=in_specs, out_specs=out_specs, check_vma=False)
```

```python
import functools

import jax
import jax.numpy as jnp
from jax import lax
from jax.experimental import pallas as pl
from jax.experimental.pallas import tpu as pltpu
from jax.sharding import PartitionSpec as P

D = 768
HD = 64
BLK = 64
SEQ_LEN = 2048
epsilon = 1e-06
NEG = -1e30
F32 = jnp.float32
BF = jnp.bfloat16
MESH = pl.DeviceIdType.MESH
NT = (((1,), (1,)), ((), ()))
NN = (((1,), (0,)), ((), ()))
TN = (((0,), (0,)), ((), ()))
VM = pl.BlockSpec(memory_space=pltpu.VMEM)
SM = pl.BlockSpec(memory_space=pltpu.SMEM)
ANY = pl.BlockSpec(memory_space=pl.ANY)
SDS = jax.ShapeDtypeStruct


def dot(a, b, dims):
    return lax.dot_general(a, b, dims, preferred_element_type=F32)


def params(mib, cid=None):
    if cid is None:
        return pltpu.CompilerParams(vmem_limit_bytes=mib << 20)
    return pltpu.CompilerParams(vmem_limit_bytes=mib << 20, collective_id=cid, has_side_effects=True)


class Place:
    def __init__(self):
        self.zn = lax.axis_size("dp") // 2
        dp, t = lax.axis_index("dp"), lax.axis_index("tensor")
        self.z, self.x, self.y, self.c = dp // 2, dp % 2, t // 2, t % 2

    def at(self, z=None, x=None, y=None, c=None):
        z = self.z if z is None else z
        x = self.x if x is None else x
        y = self.y if y is None else y
        c = self.c if c is None else c
        return (z * 2 + x, y * 2 + c)

    def peer(self, axis, k=1):
        if axis == "z":
            return self.at(z=(self.z + k) % self.zn)
        return {
            "x": self.at(x=1 - self.x),
            "y": self.at(y=1 - self.y),
            "c": self.at(c=1 - self.c),
        }[axis]

    def peers(self, axes):
        out = []
        for axis in axes:
            for k in range(1, self.zn if axis == "z" else 2):
                out.append(self.peer(axis, k))
        return out


def greet(place, axes):
    barrier = pltpu.get_barrier_semaphore()
    peers = place.peers(axes)
    for peer in peers:
        pl.semaphore_signal(barrier, inc=1, device_id=peer, device_id_type=MESH)
    pl.semaphore_wait(barrier, len(peers))


class Sems:
    def __init__(self, send, recv):
        self.send, self.recv, self.used = send, recv, 0

    def take(self, count):
        at = self.used
        self.used += count
        return at

    def copy(self, i, src, dst, device):
        return pltpu.make_async_remote_copy(
            src_ref=src,
            dst_ref=dst,
            send_sem=self.send.at[i],
            recv_sem=self.recv.at[i],
            device_id=device,
            device_id_type=MESH,
        )


def copies_of(order, zn):
    return sum(zn - 1 if a == "z" else 1 for a in order)


def concat_lanes(parts):
    return jnp.concatenate(parts, axis=1)


class Gather:
    def __init__(self, place, sems, shard, out, spec):
        self.place, self.shard, self.out = place, shard, out
        self.order, self.pre, self.axes, self.cut = spec
        self.sems = sems
        self.base = sems.take(copies_of(self.order, place.zn))

    def piece(self, whole):
        p = self.place
        own = {"y": p.y, "c": p.c, "z": p.z, "x": p.x}
        idx = (slice(None),) * self.pre
        idx += tuple(slice(None) if a in whole else own[a] for a in self.axes)
        return self.out.at[idx + self.cut]

    def mine(self):
        return self.shard.at[(slice(None),) * self.pre + self.cut] if self.cut else self.shard

    def local(self, sem):
        return pltpu.make_async_copy(self.mine(), self.piece(""), sem)

    def copies(self, stage):
        axis, zn = self.order[stage], self.place.zn
        if stage == 0:
            src, dst = self.mine(), self.piece("")
        else:
            src = dst = self.piece(self.order[:stage])
        at = self.base + copies_of(self.order[:stage], zn)
        return [
            self.sems.copy(at + k - 1, src, dst, self.place.peer(axis, k))
            for k in range(1, zn if axis == "z" else 2)
        ]

    def start(self, stage):
        for copy in self.copies(stage):
            copy.start()

    def wait(self, stage):
        for copy in self.copies(stage):
            copy.wait()


class Scatter:
    def __init__(self, place, sems, grad, out, spec, bufs):
        self.place, self.sems, self.grad, self.out = place, sems, grad, out
        self.order, self.pre, self.axes, self.cut = spec
        self.base = sems.take(copies_of(self.order, place.zn))
        self.keep, self.recv, self.send = bufs[0], [bufs[1]] + list(bufs[2::2]), [None] + list(bufs[3::2])
        self.own = {"y": place.y, "c": place.c, "z": place.z, "x": place.x}
        self.size = {"y": 2, "c": 2, "z": place.zn, "x": 2}

    @staticmethod
    def buffers(a, spec, zn):
        order, pre, axes, cut = spec
        size = {"y": 2, "c": 2, "z": zn, "x": 2}
        lead, tail = a.shape[:pre], a.shape[pre + len(axes) :]
        tail = tuple(len(range(*s.indices(d))) for s, d in zip(cut, tail)) + tail[len(cut) :]
        out = []
        for n, axis in enumerate(order):
            after = tuple(size[s] for s in axes if s not in order[: n + 1])
            one = lead + after + tail
            if n == 0:
                out.append(pltpu.VMEM(one, BF))
            out.append(pltpu.VMEM(((zn - 1,) if axis == "z" else ()) + one, BF))
            if n > 0:
                out.append(pltpu.VMEM(((zn,) if axis == "z" else ()) + one, BF))
        return out

    def copies(self, stage, only=None):
        p, axis = self.place, self.order[stage]
        at = self.base + copies_of(self.order[:stage], p.zn)
        recv, send = self.recv[stage], self.send[stage]
        if axis == "z":
            return [
                self.sems.copy(at + k - 1, send.at[k], recv.at[k - 1], p.peer("z", k))
                for k in (range(1, p.zn) if only is None else (only,))
            ]
        return [self.sems.copy(at, self.half(1 - self.own[axis]) if stage == 0 else send, recv, p.peer(axis))]

    def half(self, i):
        first = self.order[0]
        idx = (slice(None),) * self.pre + tuple(i if a == first else slice(None) for a in self.axes)
        return self.grad.at[idx + self.cut]

    def kept(self, here):
        return pltpu.make_async_copy(self.half(self.own[self.order[0]]), self.keep, here)

    def begin(self, here):
        self.copies(0)[0].start()
        self.kept(here).start()

    def wait(self, stage, here=None):
        for copy in self.copies(stage):
            copy.wait()
        if stage == 0:
            self.kept(here).wait()

    def total(self, n, lead, coords):
        def at(done):
            return lead + tuple(coords.get(a, self.own[a]) for a in self.axes if a not in done)

        t = self.keep[at(self.order[:1])].astype(F32)
        for m in range(n + 1):
            idx = at(self.order[: m + 1])
            if self.order[m] == "z":
                for k in range(self.place.zn - 1):
                    t = t + self.recv[m][(k,) + idx].astype(F32)
            else:
                t = t + self.recv[m][idx].astype(F32)
        return t

    def each(self, axes, fn, coords=None, lead=()):
        coords = coords or {}
        if len(lead) < self.pre:
            for i in range(self.grad.shape[len(lead)]):
                self.each(axes, fn, coords, lead + (i,))
        elif not axes:
            fn(lead, coords)
        elif axes[0] == "z":

            def body(i, carry):
                self.each(axes[1:], fn, {**coords, "z": i}, lead)
                return carry

            lax.fori_loop(0, self.size["z"], body, 0)
        else:
            for i in range(2):
                self.each(axes[1:], fn, {**coords, axes[0]: i}, lead)

    def add(self, n):
        p = self.place
        if n == len(self.order) - 1:

            def last(lead, coords):
                self.out[lead + self.cut] = self.total(n, lead, coords)

            self.each("", last)
            return
        nxt = self.order[n + 1]
        send = self.send[n + 1]
        left = [a for a in self.axes if a not in self.order[: n + 2]]
        if nxt == "z":
            for k in range(1, p.zn):
                to = (p.z + k) % p.zn

                def put(lead, coords, k=k, to=to):
                    send[(k,) + lead] = self.total(n, lead, {**coords, "z": to}).astype(BF)

                self.each(left, put)
                self.copies(n + 1, k)[0].start()
        else:

            def put(lead, coords):
                idx = lead + tuple(coords[a] for a in left)
                send[idx] = self.total(n, lead, {**coords, nxt: 1 - self.own[nxt]}).astype(BF)

            self.each(left, put)
            self.copies(n + 1)[0].start()


class SumAll:
    def __init__(self, place, sems, value, out, order, recv, held):
        self.order = order
        self.place, self.sems, self.value, self.out, self.recv, self.held = place, sems, value, out, recv, held
        self.base = sems.take(copies_of(self.order, place.zn))

    @staticmethod
    def buffers(a, order, zn):
        hops = len(order)
        return [pltpu.VMEM((hops - 2 + zn,) + a.shape, F32), pltpu.VMEM((hops - 1,) + a.shape, F32)]

    def copies(self, n):
        p = self.place
        axis = self.order[n]
        src = self.value if n == 0 else self.held.at[n - 1]
        at = self.base + n
        return [
            self.sems.copy(at + k - 1, src, self.recv.at[n + k - 1], p.peer(axis, k))
            for k in range(1, p.zn if axis == "z" else 2)
        ]

    def begin(self, here=None):
        self.copies(0)[0].start()

    def wait(self, n, here=None):
        for copy in self.copies(n):
            copy.wait()

    def add(self, n):
        mine = self.value[...] if n == 0 else self.held[n - 1]
        if n == len(self.order) - 1:
            for k in range(self.place.zn - 1):
                mine = mine + self.recv[n + k]
            self.out[...] = mine
            return
        self.held[n] = mine + self.recv[n]
        for copy in self.copies(n + 1):
            copy.start()


AFTER = 90


class Due:
    def __init__(self):
        self.todo = {}

    def add(self, step, fn):
        self.todo.setdefault(step, []).append(fn)

    def now(self, step):
        for fn in self.todo.get(step, []):
            fn()

    def __call__(self, g, first=0, last=AFTER):
        for step, fns in sorted(self.todo.items()):
            if first <= step < last:

                @pl.when(g == step - first)
                def _(fns=fns):
                    for fn in fns:
                        fn()


def relay(table, jobs, waves, window, finish):
    due, stage, behind = Due(), {}, list(waves[window:])
    for step, name in table:
        n = stage.get(name, 0)
        stage[name] = n + 1
        wave = [w for w in waves if name in w]
        begin = []
        if n == 0 and behind and wave and all(stage.get(other) for other in wave[0]):
            begin = behind.pop(0)
        due.add(step, functools.partial(finish, name, n, begin))
    assert not behind and all(stage.get(name) == len(job.order) for name, job in jobs.items())
    return due


UNROLL = 5


def stack_heads(q):
    lo = lax.broadcasted_iota(jnp.int32, q.shape, 1) < HD
    z = jnp.zeros_like(q)
    return jnp.concatenate([jnp.where(lo, q, z), jnp.where(lo, z, q)], axis=0)


def block_rows(j, count=1):
    return pl.ds(pl.multiple_of(j * BLK, BLK), count * BLK)


def flat_rows(t):
    return t.reshape(t.shape[0] * t.shape[1], t.shape[2])


def picks_of(idx_ref, p, j):
    pairs = idx_ref.shape[0] // 2
    return [(idx_ref[p, j * 3 + r], idx_ref[pairs + p, j * 3 + r]) for r in range(3)]


def slots_of(ref, p, j, picks, nb):
    lo = lax.broadcasted_iota(jnp.int32, (BLK, 2 * HD), 1) < HD
    parts = [ref[p, 0], ref[p, nb - 1], flat_rows(ref[p, pl.ds(j - 1, 3)])]
    for a, b in picks:
        parts.append(jnp.where(lo, ref[p, a], ref[p, b]))
    return jnp.concatenate(parts, axis=0)


class Forward:
    def __init__(self, idx_ref, q_ref, k_ref, v_ref, ctx_ref, lse_ref, lse_t):
        self.idx, self.q, self.k, self.v, self.ctx, self.lse, self.lse_t = (
            idx_ref,
            q_ref,
            k_ref,
            v_ref,
            ctx_ref,
            lse_ref,
            lse_t,
        )
        self.nb = q_ref.shape[1] // BLK
        self.steps = (self.nb - 2) // UNROLL

    def close(self, p, j, s, v):
        lo = lax.broadcasted_iota(jnp.int32, (BLK, 2 * HD), 1) < HD
        col = lax.broadcasted_iota(jnp.int32, (2 * BLK, 128), 1)
        m = jnp.max(s, axis=1, keepdims=True)
        e = jnp.exp(s - m)
        total = jnp.sum(e, axis=1, keepdims=True)
        o = dot(e.astype(BF), v, NN) * (1.0 / total)
        self.ctx[p, block_rows(j), :] = jnp.where(lo, o[:BLK], o[BLK:]).astype(BF)
        self.lse_t[...] = jnp.where(col == j, m + jnp.log(total), self.lse_t[...])

    def edges(self, p):
        for j in (0, self.nb - 1):
            q = stack_heads(self.q[p, j * BLK : (j + 1) * BLK, :])
            self.close(p, j, dot(q, flat_rows(self.k[p]), NT), flat_rows(self.v[p]))

    def tile(self, p, j):
        picks = picks_of(self.idx, p, j)
        q = stack_heads(self.q[p, block_rows(j), :])
        ks = slots_of(self.k, p, j, picks, self.nb)
        vs = slots_of(self.v, p, j, picks, self.nb)
        s = dot(q, ks, NT)
        col = lax.broadcasted_iota(jnp.int32, (2 * BLK, 128), 1)
        double = ((col < BLK) & (j == 1)) | ((col >= BLK) & (j == self.nb - 2))
        s = jnp.concatenate([jnp.where(double, NEG, s[:, :128]), s[:, 128:]], axis=1)
        self.close(p, j, s, vs)

    def step(self, p, i):
        for u in range(UNROLL):
            self.tile(p, 1 + i * UNROLL + u)

    def finish(self, p):
        self.lse[p] = jnp.transpose(self.lse_t[...])[: self.nb]

    def run(self, pairs, at=None):
        def body(g, carry):
            p, i = g // self.steps, g % self.steps
            if at is not None:
                at(g)

            @pl.when(i == 0)
            def _():
                self.edges(p)

            self.step(p, i)

            @pl.when(i == self.steps - 1)
            def _():
                self.finish(p)

            return carry

        lax.fori_loop(0, pairs * self.steps, body, 0)


def delta_row(do, ctx):
    d = jnp.transpose(do.astype(F32) * ctx.astype(F32))
    a = jnp.sum(d[:HD], axis=0, keepdims=True)
    b = jnp.sum(d[HD:], axis=0, keepdims=True)
    return jnp.concatenate([a, b], axis=1)


class Backward:
    def __init__(self, idx_ref, prev_ref, last_ref, q, k, v, ctx, do, lse, dq, dk, dv, dk_acc, dv_acc, dk_run, dv_run):
        self.idx, self.prev, self.last = idx_ref, prev_ref, last_ref
        self.q, self.k, self.v, self.ctx, self.do, self.lse = q, k, v, ctx, do, lse
        self.dq, self.dk, self.dv = dq, dk, dv
        self.accs = ((dk_acc, dk_run), (dv_acc, dv_run))
        self.nb = q.shape[1] // BLK
        self.steps = (self.nb - 2) // UNROLL

    def math(self, q, do, ks, vs, lse, delta, double=None):
        st = dot(ks, q, NT)
        pt = jnp.exp(st - lse)
        if double is not None:
            pt = jnp.concatenate([jnp.where(double, 0.0, pt[:128]), pt[128:]], axis=0)
        dst = (pt * (dot(vs, do, NT) - delta)).astype(BF)
        return dot(dst, ks, TN), dot(dst, q, NN), dot(pt.astype(BF), do, NN)

    def edges(self, p):
        qs, dos, ls, ds = [], [], [], []
        lo = lax.broadcasted_iota(jnp.int32, (BLK, 2 * HD), 1) < HD
        for j in (0, self.nb - 1):
            rows = slice(j * BLK, (j + 1) * BLK)
            do = self.do_block(p, j)
            qs.append(stack_heads(self.q[p, rows, :]))
            dos.append(stack_heads(do))
            ls.append(self.lse[p, j : j + 1, :])
            ds.append(delta_row(do, self.ctx[p, rows, :]))
        q, do = jnp.concatenate(qs, axis=0), jnp.concatenate(dos, axis=0)
        lse, delta = jnp.concatenate(ls, axis=1), jnp.concatenate(ds, axis=1)
        dq_sum = jnp.zeros((4 * BLK, 2 * HD), F32)
        for n in range(self.nb // 8):
            r = slice(n * 8 * BLK, (n + 1) * 8 * BLK)
            ks, vs = flat_rows(self.k[p, n * 8 : (n + 1) * 8]), flat_rows(self.v[p, n * 8 : (n + 1) * 8])
            dq, dk, dv = self.math(q, do, ks, vs, lse, delta)
            dq_sum = dq_sum + dq
            self.accs[0][0][r, :] = dk
            self.accs[1][0][r, :] = dv
        dq_sum = dq_sum * 0.125
        for n, j in enumerate((0, self.nb - 1)):
            part = dq_sum[n * 2 * BLK : (n + 1) * 2 * BLK]
            self.dq[p, j * BLK : (j + 1) * BLK, :] = jnp.where(lo, part[:BLK], part[BLK:]).astype(BF)
        for _, run in self.accs:
            run[0] = jnp.zeros((BLK, 2 * HD), F32)

    def do_block(self, p, j):
        half = self.nb // 2
        if isinstance(j, int):
            return self.do[j // half, p, (j % half) * BLK : (j % half + 1) * BLK, :]
        return self.do[j // half, p, block_rows(j % half), :]

    def tile(self, p, j):
        lo = lax.broadcasted_iota(jnp.int32, (BLK, 2 * HD), 1) < HD
        row = lax.broadcasted_iota(jnp.int32, (2 * BLK, 128), 0)
        nb, pairs = self.nb, self.idx.shape[0] // 2
        picks = picks_of(self.idx, p, j)
        q, do = self.q[p, block_rows(j), :], self.do_block(p, j)
        delta = delta_row(do, self.ctx[p, block_rows(j), :])
        ks = slots_of(self.k, p, j, picks, nb)
        vs = slots_of(self.v, p, j, picks, nb)
        double = ((row < BLK) & (j == 1)) | ((row >= BLK) & (j == nb - 2))
        dq, dk, dv = self.math(
            stack_heads(q), stack_heads(do), ks, vs, self.lse[p, pl.ds(j, 1), :], delta, double
        )
        self.dq[p, block_rows(j), :] = (jnp.where(lo, dq[:BLK], dq[BLK:]) * 0.125).astype(BF)
        for (acc, run), g in zip(self.accs, (dk, dv)):
            acc[0:BLK, :] += g[0:BLK]
            acc[(nb - 1) * BLK : nb * BLK, :] += g[BLK : 2 * BLK]
            acc[block_rows(j - 1, 3), :] += g[2 * BLK : 5 * BLK]
            for r in range(3):
                s = j * 3 + r
                before = jnp.where(lo, run[self.prev[p, s]], run[self.prev[pairs + p, s]])
                run[s - 2] = g[(5 + r) * BLK : (6 + r) * BLK] + before

    def step(self, p, i):
        for u in range(UNROLL):
            self.tile(p, 1 + i * UNROLL + u)

    def finish(self, p):
        lo = lax.broadcasted_iota(jnp.int32, (BLK, 2 * HD), 1) < HD
        pairs = self.idx.shape[0] // 2

        def body(n, carry):
            a, b = self.last[p, n], self.last[pairs + p, n]
            for (acc, run), out in zip(self.accs, (self.dk, self.dv)):
                t = acc[block_rows(n), :] + jnp.where(lo, run[a], run[b])
                out[p, block_rows(n), :] = t.astype(BF)
            return carry

        lax.fori_loop(0, self.nb, body, 0)

    def run(self, pairs, at=None, done=None):
        def body(g, carry):
            p, i = g // self.steps, g % self.steps
            if at is not None:
                at(g)

            @pl.when(i == 0)
            def _():
                self.edges(p)

            self.step(p, i)

            @pl.when(i == self.steps - 1)
            def _():
                self.finish(p)
                if done is not None:
                    done(p)

            return carry

        lax.fori_loop(0, pairs * self.steps, body, 0)


def block_tables(random_blocks, place_c):
    heads, blocks = random_blocks.shape[:2]
    own = lax.dynamic_index_in_dim(
        random_blocks.reshape((2, 2, heads // 4) + random_blocks.shape[1:]), place_c, 1, False
    ).reshape(heads // 2, blocks * 3, blocks)
    idx = jnp.sum(own * jnp.arange(blocks, dtype=jnp.int32), axis=-1)
    slots = blocks * 3
    s = jnp.arange(slots, dtype=jnp.int32)
    middle = (s >= 3) & (s < slots - 3)
    number = jnp.where(middle, s - 2, 0)
    same = (idx[:, :, None] == idx[:, None, :]) & (s[None, None, :] < s[None, :, None])
    prev = jnp.max(jnp.where(same, number[None, None, :], 0), axis=-1)
    last = jnp.max(jnp.where(own > 0, number[None, :, None], 0), axis=1)
    return idx, prev, last
SMALL_ROWS = 16


FORWARD_TABLE = (
    (-1000, "q0b"),
    (-999, "q1b"),
    (-998, "q0a"),
    (-997, "q1a"),
    (-996, "q0b"),
    (-995, "q1b"),
    (-994, "q0a"),
    (-993, "q1a"),
    (-992, "q2b"),
    (-991, "q0b"),
    (-990, "q1b"),
    (-989, "q2a"),
    (-988, "a0"),
    (-987, "b0"),
    (-986, "q2b"),
    (-985, "q1a"),
    (-984, "q0a"),
    (-983, "q2a"),
    (-982, "q2b"),
    (-981, "b0"),
    (-980, "a0"),
    (-979, "a1"),
    (-978, "b1"),
    (-977, "q2a"),
    (0, "o"),
    (1, "a2"),
    (1, "b2"),
    (5, "a1"),
    (6, "b0"),
    (6, "a2"),
    (7, "o"),
    (7, "b1"),
    (9, "b0"),
    (9, "b2"),
    (11, "a0"),
    (14, "a0"),
    (16, "a1"),
    (17, "a2"),
    (17, "o"),
    (18, "a1"),
    (19, "b1"),
    (20, "b2"),
    (20, "o"),
    (20, "a2"),
    (AFTER, "b1"),
    (AFTER, "b2"),
)
FORWARD_WINDOW = 2


def assemble_qkv(p, parts, w):
    zn, half = parts.shape[2], parts.shape[4]

    def body(n, carry):
        z, x = n // 2, n % 2
        for h in range(2):
            rows = pl.ds(pl.multiple_of(n * 2 * half + h * half, half), half)
            src = [parts[p, y, z, x, :, h * 3 * HD : (h + 1) * 3 * HD] for y in range(2)]
            for k in range(3):
                w[p, rows, k * 128 : (k + 1) * 128] = concat_lanes([s[:, k * HD : (k + 1) * HD] for s in src])
        return carry

    lax.fori_loop(0, zn * 2, body, 0)


def project_rows(p, i, chunk, hid, w, bias, q, k, v):
    per = hid.shape[1] // chunk
    src = hid[i // per, pl.ds(pl.multiple_of(i % per * chunk, chunk), chunk), :]
    t = dot(src, w[p], NN)
    part = (t[:, :128] + bias[0:1, :]).astype(BF).astype(F32) * 0.125
    q[p, pl.ds(pl.multiple_of(i * chunk, chunk), chunk), :] = part.astype(BF)
    rows = pl.ds(i * (chunk // BLK), chunk // BLK)
    k[p, rows] = t[:, 128:256].astype(BF).reshape(chunk // BLK, BLK, 128)
    v[p, rows] = (t[:, 256:] + bias[1:2, :]).astype(BF).reshape(chunk // BLK, BLK, 128)


def place_small(place, out, b_qv, b_in, ln_gains, row_biases, mask):
    def lane(rows):
        return lax.broadcasted_iota(jnp.int32, (rows, D), 1)

    def row(rows):
        return lax.broadcasted_iota(jnp.int32, (rows, D), 0)

    def ones(where):
        return where.astype(F32).astype(BF)

    dp = place.z * 2 + place.x
    t = place.y * 2 + place.c
    pairs, _, n = b_qv.shape
    units = b_in.shape[1]
    share = ln_gains.shape[1]
    out[...] = jnp.zeros_like(out)
    wide = dot(b_in[...], ones(lane(units) // HD == row(units)), NN)
    own = jnp.sum(jnp.where(lane(n) % HD == dp * n + row(n), wide, 0.0), axis=0, keepdims=True)
    for i in range(4):
        out[i : i + 1, :] = jnp.where(t == i, own, 0.0)
    at = ones(lane(share) == dp * share + row(share))
    one = jnp.where(t == 0, 1.0, 0.0)
    out[4:6, :] = dot(ln_gains[...], at, NN) * one
    out[6:10, :] = dot(row_biases[...], at, NN) * one
    count = jnp.sum(mask[...].astype(F32))
    out[10:11, :] = jnp.where(lane(1) == 0, count, 0.0)
    at = ones(lane(n) % HD == dp * n + row(n))
    total = jnp.zeros((2, D), F32)
    for p in range(pairs):
        here = (lane(2) // 128 == place.c * pairs + p) & (lane(2) % 128 // HD == place.y)
        total = total + jnp.where(here, dot(b_qv[p], at, NN), 0.0)
    out[11:13, :] = total


def gather_attend_kernel(
    idx_ref,
    wqkv_ref,
    h_ref,
    bqv_ref,
    bin_ref,
    gain_ref,
    rowb_ref,
    mask_ref,
    win_ref,
    wbt,
    wo_ref,
    q_out,
    k_out,
    v_out,
    ctx_out,
    lse_ref,
    rows_ref,
    hidt_out,
    w_out,
    fin_ref,
    fbt_ref,
    fot_ref,
    par_ref,
    send,
    recv,
    here,
    q_ref,
    k_ref,
    v_ref,
    ctx_ref,
    hidt_ref,
    w_ref,
    hid_ref,
    wq,
    parts,
    small_ref,
    wot,
    s_recv,
    s_held,
    lse_t,
):
    place = Place()
    c = place.c
    local = h_ref.shape[0]
    pairs = q_ref.shape[0]
    share = win_ref.shape[0]
    half = share // 2
    for p in range(pairs):
        cols = slice(p * HD, (p + 1) * HD)
        wq[p] = concat_lanes([wqkv_ref[k, h * half : (h + 1) * half, cols] for h in range(2) for k in range(3)])
    greet(place, "zxyc")
    sems = Sems(send, recv)
    jobs, waves = {}, []
    for p in range(pairs):
        orders = ("zxy", "zyx") if p % 2 == 0 else ("zyx", "zxy")
        lanes = (slice(0, 2 * 128), slice(2 * 128, 3 * 128))
        for name, order, lane in zip("ab", orders, lanes):
            spec = (order, 0, "yzx", (slice(None), lane))
            jobs[f"q{p}{name}"] = Gather(place, sems, wq.at[p], parts.at[p], spec)
        waves.append([f"q{p}a", f"q{p}b"])
    count = 3
    size = share // count
    for n in range(count):
        rows = (slice(n * size, (n + 1) * size),)
        jobs[f"a{n}"] = Gather(place, sems, win_ref, fin_ref, ("zxyc", 0, "yczx", rows))
        jobs[f"b{n}"] = Gather(place, sems, wbt, fbt_ref, ("zyxc", 0, "yczx", rows))
        waves.append([f"a{n}", f"b{n}"])
    jobs["o"] = Gather(place, sems, wot, fot_ref, ("zyxc", 0, "yczx", ()))
    waves[-1].append("o")
    hid = Gather(place, sems, h_ref, hid_ref, ("c", 0, "c", ()))
    small = SumAll(place, sems, small_ref, par_ref, "cyxz", s_recv, s_held)
    swap_at = sems.take(pairs)
    for wave in waves[:FORWARD_WINDOW]:
        for name in wave:
            jobs[name].start(0)
    hid.start(0)
    own = [pltpu.make_async_copy(wq.at[p], parts.at[p, place.y, place.z, place.x], here.at[p]) for p in range(pairs)]
    own.append(hid.local(here.at[pairs]))
    for copy in own:
        copy.start()
    place_small(place, small_ref, bqv_ref, bin_ref, gain_ref, rowb_ref, mask_ref)
    small.begin()
    t = wo_ref[...].T
    wot[...] = concat_lanes([t[:half], t[half:]])
    late = [
        pltpu.make_async_copy(src, out.at[place.y, c, place.z, place.x], here.at[pairs + 1 + n])
        for n, (src, out) in enumerate(((win_ref, fin_ref), (wbt, fbt_ref), (wot, fot_ref)))
    ]
    for copy in late:
        copy.start()
    for copy in own:
        copy.wait()
    in_flight = dict(zip("abo", late))

    def pass_on(name, stage, begin):
        if name[0] in in_flight:
            in_flight.pop(name[0]).wait()
        jobs[name].wait(stage)
        if stage + 1 < len(jobs[name].order):
            jobs[name].start(stage + 1)
        for other in begin:
            jobs[other].start(0)

    due = relay(FORWARD_TABLE, jobs, waves, FORWARD_WINDOW, pass_on)
    early = sorted(step for step in due.todo if step < 0)
    for n, step in enumerate(early):
        due.now(step)
        if n == 1:
            hid.wait(0)
            for i in range(2):
                hidt_ref[:, i * local : (i + 1) * local] = hid_ref[i].T
        if n < 4:
            small.wait(n)
            small.add(n)
    chunk = local // 2
    attend = Forward(idx_ref, q_ref, k_ref, v_ref, ctx_ref, lse_ref, lse_t)

    def there(p):
        rows = pl.ds(pl.multiple_of((1 - c) * local, local), local)
        return sems.copy(swap_at + p, ctx_ref.at[p, rows, :], rows_ref.at[c, p], place.peer("c"))

    bias = jnp.where(c == 0, par_ref[11:13, : pairs * 128], par_ref[11:13, pairs * 128 :])
    for p in range(pairs):
        assemble_qkv(p, parts, w_ref)

    def project(i, carry):
        due(i, 0, 4)
        for p in range(pairs):
            project_rows(p, i, chunk, hid_ref, w_ref, bias[:, p * 128 : (p + 1) * 128], q_ref, k_ref, v_ref)
        return carry

    lax.fori_loop(0, 4, project, 0)
    stores = [
        pltpu.make_async_copy(src, dst, here.at[pairs + 4 + n])
        for n, (src, dst) in enumerate(
            ((q_ref, q_out), (k_ref, k_out), (v_ref, v_out), (hidt_ref, hidt_out), (w_ref, w_out), (ctx_ref, ctx_out))
        )
    ]
    for copy in stores[:5]:
        copy.start()
    attend.run(pairs, lambda g: due(g, 4))
    for p in range(pairs):
        there(p).start()
    mine = pltpu.make_async_copy(
        ctx_ref.at[:, pl.ds(pl.multiple_of(c * local, local), local), :], rows_ref.at[c], here.at[0]
    )
    mine.start()
    stores[5].start()
    due.now(AFTER)
    for copy in stores:
        copy.wait()
    mine.wait()
    for p in range(pairs):
        there(p).wait()


def gather_attend(idx, w_qkv, hidden, smalls, w_in, w_bt, w_out, pairs, zn, cid):
    local = hidden.shape[0]
    n = 2 * local
    share, wide = w_in.shape
    heads_shape = SDS((pairs, n, 128), BF)
    blocks_shape = SDS((pairs, n // BLK, BLK, 128), BF)
    packed = (share // 2, 6 * HD)
    small = SDS((SMALL_ROWS, D), F32)
    copies = 2 * pairs * copies_of("zxy", zn) + 1 + copies_of("cyxz", zn) + 7 * copies_of("zxyc", zn) + pairs
    return pl.pallas_call(
        gather_attend_kernel,
        out_shape=(
            heads_shape,
            blocks_shape,
            blocks_shape,
            heads_shape,
            SDS((pairs, n // BLK, 128), F32),
            SDS((2, pairs, local, 128), BF),
            SDS((D, n), BF),
            SDS((pairs, D, 3 * 128), BF),
            SDS((2, 2, zn, 2, share, wide), BF),
            SDS((2, 2, zn, 2, share, wide), BF),
            SDS((2, 2, zn, 2) + packed, BF),
            SDS(small.shape, F32),
        ),
        in_specs=[SM, VM, ANY] + [VM] * len(smalls) + [ANY, ANY, VM],
        out_specs=(ANY,) * 4 + (VM,) + (ANY,) * 6 + (VM,),
        scratch_shapes=[
            pltpu.SemaphoreType.DMA((copies,)),
            pltpu.SemaphoreType.DMA((copies,)),
            pltpu.SemaphoreType.DMA((pairs + 10,)),
            pltpu.VMEM(heads_shape.shape, BF),
            pltpu.VMEM(blocks_shape.shape, BF),
            pltpu.VMEM(blocks_shape.shape, BF),
            pltpu.VMEM(heads_shape.shape, BF),
            pltpu.VMEM((D, n), BF),
            pltpu.VMEM((pairs, D, 3 * 128), BF),
            pltpu.VMEM((2, local, D), BF),
            pltpu.VMEM((pairs,) + packed, BF),
            pltpu.VMEM((pairs, 2, zn, 2) + packed, BF),
            pltpu.VMEM(small.shape, F32),
            pltpu.VMEM(packed, BF),
        ]
        + SumAll.buffers(small, "cyxz", zn)
        + [pltpu.VMEM((128, 128), F32)],
        compiler_params=params(56, cid),
        name="gather_attend",
    )(idx, w_qkv, hidden, *smalls, w_in, w_bt, w_out)
def norm(v):
    centred = v - jnp.mean(v, axis=-1, keepdims=True)
    rs = lax.rsqrt(jnp.mean(centred * centred, axis=-1, keepdims=True) + epsilon)
    return centred * rs, rs


def norm_back(g, gain, xhat, rs):
    gx = gain * g
    return rs * (gx - jnp.mean(gx, axis=-1, keepdims=True) - xhat * jnp.mean(gx * xhat, axis=-1, keepdims=True))


def gelu_both(v):
    k, a = 0.7978845608028654, 0.044715
    v2 = v * v
    th = jnp.tanh(k * v * (1.0 + a * v2))
    half = 0.5 * (1.0 + th)
    slope = half + (0.5 * k) * v * (1.0 - th * th) * (1.0 + (3.0 * a) * v2)
    return v * half, slope


def assemble_out(parts, w):
    zn, half = parts.shape[2], parts.shape[4]
    wide = parts.shape[5] // 2
    pairs = wide // HD

    def body(n, carry):
        z, x = n // 2, n % 2
        for h in range(2):
            rows = pl.ds(pl.multiple_of(n * 2 * half + h * half, half), half)
            for c in range(2):
                for p in range(pairs):
                    at = h * wide + p * HD
                    w[rows, (c * pairs + p) * 128 : (c * pairs + p + 1) * 128] = concat_lanes(
                        [parts[y, c, z, x, :, at : at + HD] for y in range(2)]
                    )
        return carry

    lax.fori_loop(0, zn * 2, body, 0)


def scatter_out(w, parts):
    zn, half = parts.shape[2], parts.shape[4]
    wide = parts.shape[5] // 2
    pairs = wide // HD

    def body(n, carry):
        z, x = n // 2, n % 2
        src = [w[pl.ds(pl.multiple_of(n * 2 * half + h * half, half), half), :] for h in range(2)]
        for y in range(2):
            for c in range(2):
                cols = [(c * pairs + p) * 128 + y * HD for p in range(pairs)]
                parts[y, c, z, x] = concat_lanes([s[:, a : a + HD] for s in src for a in cols]).astype(BF)
        return carry

    lax.fori_loop(0, zn * 2, body, 0)


def mask_rows(m_ref, step, tile):
    columns = m_ref[...].astype(F32).T
    at = lax.broadcasted_iota(jnp.int32, columns.shape, 1)
    per = tile // 128
    parts = [
        jnp.sum(jnp.where(at == step * per + i, columns, 0.0), axis=1, keepdims=True) for i in range(per)
    ]
    return jnp.concatenate(parts, axis=0)


def rows_kernel(
    tokens_total,
    packed,
    ctx_ref,
    h_ref,
    t_ref,
    m_ref,
    w_in,
    w_bt,
    w_ot,
    par,
    enc_ref,
    gmix_ref,
    gctx_ref,
    gin_ref,
    gbt_ref,
    got_ref,
    vec_ref,
    slope,
    act,
    ginner,
    nlow_t,
    slow_t,
    w_o,
    got,
):
    step = pl.program_id(0)
    tile = h_ref.shape[0]
    units = w_in.shape[0]
    pairs = ctx_ref.shape[1]
    r = pl.ds(pl.multiple_of(step * tile, tile), tile)

    @pl.when(step == 0)
    def _():
        vec_ref[...] = jnp.zeros_like(vec_ref)
        got[...] = jnp.zeros_like(got)
        if packed:
            assemble_out(w_ot, w_o)
        else:
            w_o[...] = w_ot[...]

    gains, biases = par[4:6, :], par[6:10, :]
    scale = tokens_total / par[10:11, 0:1]
    ctx = concat_lanes([ctx_ref[n, p] for n in range(2) for p in range(pairs)])
    mixed = h_ref[...].astype(F32) + dot(ctx, w_o[...], NT) + biases[0:1, :]
    xhat1, rs1 = norm(mixed)
    normed = xhat1 * gains[0:1, :] + biases[1:2, :]
    nlow = normed.astype(BF)
    nlow_t[:, r] = nlow.T
    second = normed + biases[2:3, :]
    for u in range(units):
        inner = dot(nlow, w_in[u], NN) + par[u : u + 1, :]
        a, s = gelu_both(inner)
        a = a.astype(BF)
        act[u, r, :] = a
        slope[u] = s
        second = second + dot(a, w_bt[u], NT)
    xhat2, rs2 = norm(second)
    encoded = xhat2 * gains[1:2, :] + biases[3:4, :]
    enc_ref[...] = encoded
    error = encoded - t_ref[...]
    merr = mask_rows(m_ref, step, tile) * error
    genc = merr * scale
    gsec = norm_back(genc, gains[1:2, :], xhat2, rs2)
    slow = gsec.astype(BF)
    slow_t[:, r] = slow.T
    gnorm = gsec
    for u in range(units):
        gi = (dot(slow, w_bt[u], NN) * slope[u]).astype(BF)
        ginner[u, r, :] = gi
        vec_ref[6 + u : 7 + u, :] += jnp.sum(gi.astype(F32), axis=0, keepdims=True)
        gnorm = gnorm + dot(gi, w_in[u], NT)
    gmix = norm_back(gnorm, gains[0:1, :], xhat1, rs1)
    gmix_ref[...] = gmix
    mlow = gmix.astype(BF)
    gctx = dot(mlow, w_o[...], NN).astype(BF)
    for n in range(2):
        for p in range(pairs):
            gctx_ref[n, p] = gctx[:, (n * pairs + p) * 128 : (n * pairs + p + 1) * 128]
    sums = (gnorm * xhat1, genc * xhat2, gmix, gnorm, gsec, genc)
    for n, value in enumerate(sums):
        vec_ref[n : n + 1, :] += jnp.sum(value, axis=0, keepdims=True)
    vec_ref[10:11, :] += jnp.sum(merr * error, axis=0, keepdims=True)
    got[...] += dot(mlow.T, ctx, NN)

    @pl.when(step == pl.num_programs(0) - 1)
    def _():
        if packed:
            scatter_out(got, got_ref)
        else:
            got_ref[...] = got[...].astype(BF)
        for u in range(units):
            gin_ref[u] = dot(nlow_t[...], ginner[u], NN).astype(BF)
            gbt_ref[u] = dot(slow_t[...], act[u], NN).astype(BF)


def row_pass(tokens_total, ctx, hidden, teacher, mask, w_in, w_bt, w_ot, par, tile):
    n = hidden.shape[0]
    units, _, wide = w_in.shape
    pairs = ctx.shape[1]
    once = pl.Buffered(1)

    def whole(a):
        return pl.BlockSpec(a.shape, lambda i, nd=len(a.shape): (0,) * nd, pipeline_mode=once)

    def rows(width):
        return pl.BlockSpec((tile, width), lambda i: (i, 0))

    heads = pl.BlockSpec((2, pairs, tile, 128), lambda i: (0, 0, i, 0))
    outs = (
        SDS((n, D), F32),
        SDS((n, D), F32),
        SDS((2, pairs, n, 128), BF),
        SDS(w_in.shape, BF),
        SDS(w_in.shape, BF),
        SDS(w_ot.shape, BF),
        SDS((SMALL_ROWS, D), F32),
    )
    return pl.pallas_call(
        functools.partial(rows_kernel, float(tokens_total), len(w_ot.shape) > 2),
        grid=(n // tile,),
        out_shape=outs,
        in_specs=[heads, rows(D), rows(D)] + [whole(a) for a in (mask, w_in, w_bt, w_ot, par)],
        out_specs=(rows(D), rows(D), heads) + tuple(whole(a) for a in outs[3:]),
        scratch_shapes=[
            pltpu.VMEM((units, tile, wide), F32),
            pltpu.VMEM((units, n, wide), BF),
            pltpu.VMEM((units, n, wide), BF),
            pltpu.VMEM((D, n), BF),
            pltpu.VMEM((D, n), BF),
            pltpu.VMEM((D, D), BF),
            pltpu.VMEM((D, D), F32),
        ],
        compiler_params=params(62),
        name="row_pass",
    )(ctx, hidden, teacher, mask, w_in, w_bt, w_ot, par)
BACKWARD_TABLE = (
    (0, "a0"),
    (0, "b0"),
    (2, "a1"),
    (2, "b1"),
    (4, "v"),
    (5, "a0"),
    (5, "o"),
    (5, "b0"),
    (6, "a2"),
    (6, "b2"),
    (6, "v"),
    (7, "a1"),
    (8, "v"),
    (8, "b0"),
    (9, "b1"),
    (10, "v"),
    (11, "q0a"),
    (11, "a0"),
    (11, "q0b"),
    (12, "b0"),
    (13, "a0"),
    (13, "q0b"),
    (13, "o"),
    (13, "b1"),
    (13, "a2"),
    (13, "a1"),
    (14, "q0a"),
    (14, "q1b"),
    (15, "q0b"),
    (16, "o"),
    (17, "b2"),
    (AFTER, "q1b"),
    (AFTER, "q1a"),
    (AFTER, "q0a"),
    (AFTER, "b1"),
    (AFTER, "a2"),
    (AFTER, "a1"),
    (AFTER, "o"),
    (AFTER, "b2"),
    (AFTER + 1, "s"),
    (AFTER + 1, "q1b"),
    (AFTER + 1, "q2b"),
    (AFTER + 3, "s"),
    (AFTER + 3, "q1a"),
    (AFTER + 3, "a2"),
    (AFTER + 3, "q2a"),
    (AFTER + 3, "b2"),
    (AFTER + 3, "q2b"),
    (AFTER + 3, "s"),
    (AFTER + 3, "q1a"),
    (AFTER + 3, "q2b"),
    (AFTER + 3, "q2a"),
    (AFTER + 3, "q2a"),
)
BACKWARD_WINDOW = 1
CHUNKS = 3


def sum_specs(share, pairs):
    size = share // CHUNKS
    specs = []
    for n in range(CHUNKS):
        rows = (slice(n * size, (n + 1) * size),)
        specs.append((f"a{n}", "in", ("cyxz", 0, "yczx", rows)))
        specs.append((f"b{n}", "back", ("cxyz", 0, "yczx", rows)))
    specs.append(("o", "out", ("cxyz", 0, "yczx", ())))
    for p in range(pairs):
        orders = ("yxz", "xyz") if p % 2 == 0 else ("xyz", "yxz")
        lanes = (slice(0, 2 * 128), slice(2 * 128, 3 * 128))
        for name, order, lane in zip("ab", orders, lanes):
            specs.append((f"q{p}{name}", p, (order, 0, "yzx", (slice(None), lane))))
    return specs


def weight_grad(p, hid_t, dq, dk, dv):
    return dot(hid_t[...], concat_lanes([dq[p], dk[p], dv[p]]), NN)


def hidden_grad(dq, dk, dv, w, rows):
    pairs = dq.shape[0]
    grads = concat_lanes([g[p, rows, :] for p in range(pairs) for g in (dq, dk, dv)])
    return dot(grads, concat_lanes([w[p] for p in range(pairs)]), NT)


def attend_sum_kernel(
    idx_ref,
    prev_ref,
    last_ref,
    q_in,
    k_in,
    v_in,
    ctx_in,
    lse_ref,
    gctx_ref,
    hid_in,
    w_in,
    gmix_ref,
    gin_ref,
    gbt_ref,
    got_ref,
    vec_ref,
    out_ref,
    gh_recv,
    sin_ref,
    sbt,
    sot_ref,
    sq_ref,
    vsum_ref,
    bsum_ref,
    send,
    recv,
    here,
    q_ref,
    k_ref,
    v_ref,
    ctx_ref,
    hid_t,
    w_ref,
    do_ref,
    dq,
    dk,
    dv,
    dk_acc,
    dv_acc,
    dk_run,
    dv_run,
    gq,
    gh_send,
    bias,
    sot,
    sq,
    v_recv,
    v_held,
    b_recv,
    b_held,
    *bufs,
):
    place = Place()
    c = place.c
    pairs = q_ref.shape[0]
    local = gmix_ref.shape[0]
    share = gin_ref.shape[-2]
    greet(place, "zxyc")
    sems = Sems(send, recv)
    grads = {"in": (gin_ref, sin_ref), "back": (gbt_ref, sbt), "out": (got_ref, sot)}
    for p in range(pairs):
        grads[p] = (gq.at[p], sq.at[p])
    jobs, spot, rest = {}, {}, list(bufs)
    for name, which, spec in sum_specs(share, pairs):
        grad, out = grads[which]
        count = len(Scatter.buffers(grad, spec, place.zn))
        spot[name] = here.at[len(jobs)]
        jobs[name] = Scatter(place, sems, grad, out, spec, rest[:count])
        rest = rest[count:]
    jobs["v"] = SumAll(place, sems, vec_ref, vsum_ref, "cyxz", v_recv, v_held)
    jobs["s"] = SumAll(place, sems, bias, bsum_ref, "yxz", b_recv, b_held)
    spot["v"] = spot["s"] = None
    waves = [[f"a{n}", f"b{n}"] for n in range(CHUNKS)]
    waves[-1] += ["o", "v"]
    swaps = sems.take(2)
    first = sems.copy(swaps, gctx_ref.at[1 - c], do_ref.at[c], place.peer("c"))
    first.start()
    mine = pltpu.make_async_copy(gctx_ref.at[c], do_ref.at[c], here.at[len(jobs)])
    mine.start()
    for wave in waves[:BACKWARD_WINDOW]:
        for name in wave:
            jobs[name].begin(spot[name])
    loads = [
        pltpu.make_async_copy(src, dst, here.at[len(jobs) + 2 + n])
        for n, (src, dst) in enumerate(
            ((q_in, q_ref), (k_in, k_ref), (v_in, v_ref), (ctx_in, ctx_ref), (hid_in, hid_t), (w_in, w_ref))
        )
    ]
    for copy in loads:
        copy.start()
    start_out = pltpu.make_async_copy(gmix_ref, out_ref, here.at[len(jobs) + 1])
    start_out.start()
    bias[...] = jnp.zeros_like(bias)

    def advance(name, stage, begin):
        jobs[name].wait(stage, spot[name])
        jobs[name].add(stage)
        for other in begin:
            jobs[other].begin(spot[other])

    due = relay(BACKWARD_TABLE, jobs, waves, BACKWARD_WINDOW, advance)
    for step in sorted(step for step in due.todo if step < 0):
        due.now(step)
    mine.wait()
    first.wait()
    for copy in loads:
        copy.wait()
    attend = Backward(
        idx_ref, prev_ref, last_ref, q_ref, k_ref, v_ref, ctx_ref, do_ref, lse_ref, dq, dk, dv,
        dk_acc, dv_acc, dk_run, dv_run,
    )
    half = gq.shape[4]

    def done(p):
        t = weight_grad(p, hid_t, dq, dk, dv).astype(BF)
        for z in range(place.zn):
            for x in range(2):
                at = (z * 2 + x) * 2 * half
                src = [t[at + h * half : at + (h + 1) * half] for h in range(2)]
                for y in range(2):
                    gq[p, y, z, x] = concat_lanes(
                        [s[:, k * 128 + y * HD : k * 128 + (y + 1) * HD] for s in src for k in range(3)]
                    )
        lanes = pl.ds(pl.multiple_of(p * 128, 128), 128)
        for row, g in enumerate((dq, dv)):
            bias[row : row + 1, lanes] = jnp.sum(g[p].astype(F32), axis=0, keepdims=True)
        for n in range(pairs):

            @pl.when(p == n)
            def _(n=n):
                for name in (f"q{n}a", f"q{n}b"):
                    jobs[name].begin(spot[name])

    attend.run(pairs, due, done)
    jobs["s"].begin()
    size = local // 2

    def other(i, carry):
        t = hidden_grad(dq, dk, dv, w_ref, pl.ds(pl.multiple_of((1 - c) * local + i * size, size), size))
        gh_send[pl.ds(pl.multiple_of(i * size, size), size), :] = t.astype(BF)
        return carry

    due.now(AFTER)
    lax.fori_loop(0, 2, other, 0)
    swap = sems.copy(swaps + 1, gh_send, gh_recv, place.peer("c"))
    swap.start()
    start_out.wait()
    due.now(AFTER + 1)

    def own(i, carry):
        rows = pl.ds(pl.multiple_of(i * size, size), size)
        t = hidden_grad(dq, dk, dv, w_ref, pl.ds(pl.multiple_of(c * local + i * size, size), size))
        out_ref[rows, :] += t
        return carry

    lax.fori_loop(0, 2, own, 0)
    due.now(AFTER + 2)
    due.now(AFTER + 3)
    swap.wait()
    t = sot[...]
    wide = pairs * HD
    sot_ref[...] = jnp.concatenate([t[:, :wide], t[:, wide:]], axis=0).T
    for h in range(2):
        for k in range(3):
            at = (h * 3 + k) * HD
            sq_ref[k, h * half : (h + 1) * half, :] = concat_lanes([sq[p, :, at : at + HD] for p in range(pairs)])


def attend_sum(tables, q, k, v, ctx, lse, gctx, hid_t, w, gmix, g_in, g_bt, g_ot, vec, zn, cid):
    pairs, n, _ = q.shape
    local = gmix.shape[0]
    share, wide = g_in.shape[-2:]
    blocks = n // BLK
    packed = g_ot.shape[-2:]
    gq = (pairs, 2, zn, 2) + packed
    heads = pltpu.VMEM((pairs, n, 128), BF)
    bias = SDS((8, pairs * 128), F32)
    shapes = {"in": g_in, "back": g_bt, "out": g_ot}
    bufs = []
    copies = copies_of("cyxz", zn) + copies_of("yxz", zn) + 2
    specs = sum_specs(share, pairs)
    for _, which, spec in specs:
        bufs += Scatter.buffers(shapes.get(which, SDS(gq[1:], BF)), spec, zn)
        copies += copies_of(spec[0], zn)
    return pl.pallas_call(
        attend_sum_kernel,
        out_shape=(
            SDS((local, D), F32),
            SDS((local, D), BF),
            SDS((share, wide), F32),
            SDS((share, wide), F32),
            SDS((pairs * HD, share), F32),
            SDS((3, share, pairs * HD), F32),
            SDS(vec.shape, F32),
            bias,
        ),
        in_specs=[SM] * 3 + [ANY] * 4 + [VM] + [ANY] * 7 + [VM],
        out_specs=(VM,) * 8,
        scratch_shapes=[
            pltpu.SemaphoreType.DMA((copies,)),
            pltpu.SemaphoreType.DMA((copies,)),
            pltpu.SemaphoreType.DMA((len(specs) + 10,)),
            pltpu.VMEM(q.shape, BF),
            pltpu.VMEM(k.shape, BF),
            pltpu.VMEM(v.shape, BF),
            pltpu.VMEM(ctx.shape, BF),
            pltpu.VMEM(hid_t.shape, BF),
            pltpu.VMEM(w.shape, BF),
            pltpu.VMEM(gctx.shape, BF),
            heads,
            heads,
            heads,
            pltpu.VMEM((n, 128), F32),
            pltpu.VMEM((n, 128), F32),
            pltpu.VMEM((3 * (blocks - 2) + 1, BLK, 128), F32),
            pltpu.VMEM((3 * (blocks - 2) + 1, BLK, 128), F32),
            pltpu.VMEM(gq, BF),
            pltpu.VMEM((local, D), BF),
            pltpu.VMEM(bias.shape, F32),
            pltpu.VMEM(packed, F32),
            pltpu.VMEM((pairs,) + packed, F32),
        ]
        + SumAll.buffers(vec, "cyxz", zn)
        + SumAll.buffers(bias, "yxz", zn)
        + bufs,
        compiler_params=params(62, cid),
        name="attend_sum",
    )(*tables, q, k, v, ctx, lse, gctx, hid_t, w, gmix, g_in, g_bt, g_ot, vec)


def take_kernel(
    par_ref,
    vec_ref,
    bias_ref,
    part_ref,
    recv_ref,
    sin_ref,
    sbt_ref,
    sot_ref,
    sq_ref,
    loss_ref,
    out_ref,
    oq_ref,
    ob_ref,
    oo_ref,
    oi_ref,
    obin_ref,
    obt_ref,
    og_ref,
    orow_ref,
):
    place = Place()
    dp = place.z * 2 + place.x
    t = place.y * 2 + place.c
    out_ref[...] = part_ref[...] + recv_ref[...].astype(F32)
    oq_ref[...] = sq_ref[...]
    oo_ref[...] = sot_ref[...]
    oi_ref[...] = sin_ref[...]
    obt_ref[...] = sbt_ref[...]
    loss_ref[...] = jnp.sum(vec_ref[10:11, :], axis=1, keepdims=True) / (float(D) * par_ref[10:11, 0:1])

    def exact(a, b):
        return lax.dot_general(a, b, NN, precision=lax.Precision.HIGHEST, preferred_element_type=F32)

    cols = og_ref.shape[1]
    part = dp * 4 + t
    l = lax.broadcasted_iota(jnp.int32, (D, cols), 0)
    i = lax.broadcasted_iota(jnp.int32, (D, cols), 1)
    both = exact(vec_ref[0:8, :], (l == part * cols + i).astype(F32))
    og_ref[...] = both[:2]
    orow_ref[...] = both[2:6]
    n = obin_ref.shape[0]
    units = obin_ref.shape[1]
    row = jnp.zeros((1, D), F32)
    for u in range(4):
        row = row + jnp.where(t == u, 1.0, 0.0) * vec_ref[6 + u : 7 + u, :]
    l = lax.broadcasted_iota(jnp.int32, (n, D), 1)
    i = lax.broadcasted_iota(jnp.int32, (n, D), 0)
    own = jnp.where(l % HD == dp * n + i, row, 0.0)
    l = lax.broadcasted_iota(jnp.int32, (D, units), 0)
    u = lax.broadcasted_iota(jnp.int32, (D, units), 1)
    obin_ref[...] = exact(own, (l // HD == u).astype(F32))
    e = bias_ref.shape[1]
    l = lax.broadcasted_iota(jnp.int32, (e, n), 0)
    i = lax.broadcasted_iota(jnp.int32, (e, n), 1)
    for p in range(ob_ref.shape[0]):
        ob_ref[p] = exact(bias_ref[...], (l == p * 128 + place.y * HD + dp * n + i).astype(F32))[:2]


def take(par, vec, bias, part, recv, s_in, s_bt, s_ot, s_q, b_in_shape, b_qv_shape):
    dp, tensor = lax.axis_size("dp"), lax.axis_size("tensor")
    cols = D // (dp * tensor)
    outs = (
        SDS((1, 1), F32),
        SDS(part.shape, F32),
        SDS(s_q.shape, F32),
        SDS((b_qv_shape[1], b_qv_shape[0], b_qv_shape[2]), F32),
        SDS(s_ot.shape, F32),
        SDS(s_in.shape, F32),
        SDS((b_in_shape[1], b_in_shape[0]), F32),
        SDS(s_bt.shape, F32),
        SDS((2, cols), F32),
        SDS((4, cols), F32),
    )
    return pl.pallas_call(
        take_kernel,
        out_shape=outs,
        in_specs=[VM] * 9,
        out_specs=(VM,) * len(outs),
        compiler_params=params(62),
        name="take_parts",
    )(par, vec, bias, part, recv, s_in, s_bt, s_ot, s_q)


def small_parts(b_qv, b_in, ln_gains, row_biases, count):
    dp, dpi = lax.axis_size("dp"), lax.axis_index("dp")
    t = lax.axis_index("tensor")
    y, c = t // 2, t % 2

    def at(i, size):
        return (jnp.arange(size) == i).astype(F32)

    heads, hd = b_qv.shape[1:]
    units = at(t, 4)[:, None, None, None] * b_in.astype(F32)[None, :, None, :] * at(dpi, dp)[None, None, :, None]
    rows = jnp.concatenate([ln_gains, row_biases]).astype(F32)
    rows = rows[:, None, :] * at(dpi, dp)[None, :, None] * (t == 0).astype(F32)
    total = count * at(0, D)
    bias = b_qv.astype(F32)[:, None, :, None, None, :] * at(c, 2)[None, :, None, None, None, None]
    bias = bias * at(y, 2)[None, None, None, :, None, None] * at(dpi, dp)[None, None, None, None, :, None]
    out = jnp.concatenate([units.reshape(4, D), rows.reshape(6, D), total.reshape(1, D), bias.reshape(2, D)])
    return jnp.pad(out, ((0, SMALL_ROWS - out.shape[0]), (0, 0)))


def finish(vector, bias, par, encoded, grad_in, s_qkv, s_out, s_in, s_back, b_in, pairs, hd):
    dp, tensor = lax.axis_size("dp"), lax.axis_size("tensor")
    dpi, ti = lax.axis_index("dp"), lax.axis_index("tensor")
    part = dpi * tensor + ti
    cols = D // (dp * tensor)
    gains_biases = lax.dynamic_slice_in_dim(vector[:6], part * cols, cols, 1)
    grad_b_in = lax.dynamic_index_in_dim(vector[6:10].reshape(tensor, b_in.shape[0], dp, hd), ti, 0, False)
    grad_b_in = lax.dynamic_index_in_dim(grad_b_in, dpi, 1, False)
    grad_qv = lax.dynamic_index_in_dim(bias.reshape(2, pairs, 2, dp, hd), ti // 2, 2, False)
    grad_qv = lax.dynamic_index_in_dim(grad_qv, dpi, 2, False)
    loss = jnp.sum(vector[10]) / (D * par[10, 0])
    return (
        loss,
        encoded,
        grad_in,
        s_qkv,
        grad_qv,
        s_out,
        s_in,
        grad_b_in,
        s_back,
        gains_biases[:2],
        gains_biases[2:],
    )


def per_device(
    hidden_in, teacher, valid_mask, random_blocks, w_qkv, b_qv, w_out, w_in, b_in, w_back, ln_gains, row_biases
):
    local = hidden_in.shape[0]
    dp, tensor = lax.axis_size("dp"), lax.axis_size("tensor")
    zn = dp // 2
    tokens_total = local * tensor * dp
    pairs = b_qv.shape[1]
    mask = valid_mask.reshape(-1, 128)
    tables = block_tables(random_blocks, lax.axis_index("tensor") % 2)
    q, k, v, ctx, lse, ctx_rows, hid_t, w, full_in, full_bt, full_ot, par = gather_attend(
        tables[0], w_qkv, hidden_in, (b_qv.transpose(1, 0, 2), b_in.T, ln_gains, row_biases, mask), w_in, w_back.T,
        w_out, pairs, zn, 0,
    )
    units = (tensor, D, w_in.shape[1])
    encoded, gmix, gctx, g_in, g_bt, g_ot, vec = row_pass(
        tokens_total, ctx_rows, hidden_in, teacher, mask, full_in.reshape(units), full_bt.reshape(units), full_ot,
        par, 256,
    )
    part, there, s_in, s_bt, s_ot, s_qkv, vector, bias = attend_sum(
        tables, q, k, v, ctx, lse, gctx, hid_t, w, gmix, g_in.reshape(full_in.shape), g_bt.reshape(full_in.shape),
        g_ot, vec, zn, 1,
    )
    loss, grad_in, g_qkv, g_bias, g_out, g_w_in, g_b_in, g_back, g_gains, g_rows = take(
        par, vector, bias, part, there, s_in, s_bt, s_ot, s_qkv, b_in.shape, b_qv.shape
    )
    return (
        loss.reshape(()), encoded, grad_in, g_qkv, g_bias.transpose(1, 0, 2), g_out, g_w_in, g_b_in.T, g_back.T,
        g_gains, g_rows,
    )


def project_attend_kernel(idx_ref, hid_ref, w_ref, b_ref, q_ref, k_ref, v_ref, ctx_ref, lse_ref, lse_t):
    chunk = hid_ref.shape[1] // 2
    for p in range(q_ref.shape[0]):

        def project(i, carry, p=p):
            project_rows(p, i, chunk, hid_ref, w_ref, b_ref[:, p * 128 : (p + 1) * 128], q_ref, k_ref, v_ref)
            return carry

        lax.fori_loop(0, 4, project, 0)
    Forward(idx_ref, q_ref, k_ref, v_ref, ctx_ref, lse_ref, lse_t).run(q_ref.shape[0])


def project_attend(idx, hid, w, bias, pairs):
    n = 2 * hid.shape[1]
    heads = SDS((pairs, n, 128), BF)
    blocks = SDS((pairs, n // BLK, BLK, 128), BF)
    return pl.pallas_call(
        project_attend_kernel,
        out_shape=(heads, blocks, blocks, heads, SDS((pairs, n // BLK, 128), F32)),
        in_specs=[SM, VM, VM, VM],
        out_specs=(VM,) * 5,
        scratch_shapes=[pltpu.VMEM((128, 128), F32)],
        compiler_params=params(56),
        name="project_attend",
    )(idx, hid, w, bias)


def attend_back_kernel(
    idx_ref, prev_ref, last_ref, q_ref, k_ref, v_ref, ctx_ref, lse_ref, do_ref, hid_ref, w_ref, gw_ref, gh_ref, gb_ref,
    dq, dk, dv, dk_acc, dv_acc, dk_run, dv_run, hid_t,
):
    pairs = q_ref.shape[0]
    local = hid_ref.shape[1]
    for i in range(2):
        hid_t[:, i * local : (i + 1) * local] = hid_ref[i].T
    attend = Backward(
        idx_ref, prev_ref, last_ref, q_ref, k_ref, v_ref, ctx_ref, do_ref, lse_ref, dq, dk, dv,
        dk_acc, dv_acc, dk_run, dv_run,
    )

    def done(p):
        gw_ref[p] = weight_grad(p, hid_t, dq, dk, dv)
        for n, g in enumerate((dq, dv)):
            gb_ref[p, n : n + 1, :] = jnp.sum(g[p].astype(F32), axis=0, keepdims=True)

    attend.run(pairs, None, done)
    size = local // 4

    def some(i, carry):
        rows = pl.ds(pl.multiple_of(i * size, size), size)
        gh_ref[rows, :] = hidden_grad(dq, dk, dv, w_ref, rows)
        return carry

    lax.fori_loop(0, 8, some, 0)


def attend_back(tables, q, k, v, ctx, lse, do, hid, w):
    pairs, n, _ = q.shape
    slots = 3 * (n // BLK - 2) + 1
    heads = pltpu.VMEM((pairs, n, 128), BF)
    return pl.pallas_call(
        attend_back_kernel,
        out_shape=(SDS((pairs, D, 3 * 128), F32), SDS((n, D), F32), SDS((pairs, 2, 128), F32)),
        in_specs=[SM] * 3 + [VM] * 8,
        out_specs=(VM,) * 3,
        scratch_shapes=[heads] * 3
        + [pltpu.VMEM((n, 128), F32)] * 2
        + [pltpu.VMEM((slots, BLK, 128), F32)] * 2
        + [pltpu.VMEM((D, n), BF)],
        compiler_params=params(60),
        name="attend_back",
    )(*tables, q, k, v, ctx, lse, do, hid, w)


def plain_device(
    hidden_in, teacher, valid_mask, random_blocks, w_qkv, b_qv, w_out, w_in, b_in, w_back, ln_gains, row_biases
):
    local = hidden_in.shape[0]
    dp, tensor = lax.axis_size("dp"), lax.axis_size("tensor")
    tokens_total = local * tensor * dp
    dpi, ti = lax.axis_index("dp"), lax.axis_index("tensor")
    y, c = ti // 2, ti % 2
    pairs, hd = b_qv.shape[1:]
    everyone = ("dp", "tensor")
    mask = valid_mask.astype(F32)
    par = lax.psum(small_parts(b_qv, b_in, ln_gains, row_biases, jnp.sum(mask)), everyone)
    tables = block_tables(random_blocks, c)

    def swap(x):
        there = lax.ppermute(x[1 - c], "tensor", [(i, i ^ 1) for i in range(tensor)])
        here = x[c]
        return jnp.stack([jnp.where(c == 0, here, there), jnp.where(c == 0, there, here)])

    hid = swap(jnp.stack([hidden_in, hidden_in]))
    w = lax.all_gather(lax.all_gather(w_qkv, "dp", axis=1, tiled=True), "tensor", axis=0)
    w = w.reshape(2, 2, 3, D, pairs, HD)[:, c].transpose(3, 2, 1, 0, 4).reshape(pairs, D, -1)
    w_o = lax.all_gather(lax.all_gather(w_out, "dp", axis=1, tiled=True), "tensor", axis=0)
    w_o = w_o.reshape(2, 2, pairs, HD, D).transpose(4, 1, 2, 0, 3).reshape(D, D)
    full_in = lax.all_gather(lax.all_gather(w_in, "dp", axis=0, tiled=True), "tensor", axis=0)
    full_bt = lax.all_gather(lax.all_gather(w_back.T, "dp", axis=0, tiled=True), "tensor", axis=0)
    bias = lax.dynamic_index_in_dim(par[11:13].reshape(2, 2, -1), c, 1, False)
    q, k, v, ctx, lse = project_attend(tables[0], hid, w, bias, pairs)
    ctx_rows = swap(ctx.reshape(pairs, 2, local, 128).swapaxes(0, 1))
    encoded, gmix, gctx, g_in, g_bt, g_ot, vec = row_pass(
        tokens_total, ctx_rows, hidden_in, teacher, valid_mask.reshape(-1, 128), full_in, full_bt, w_o, par, 256
    )
    gw, gh, gb = attend_back(tables, q, k, v, ctx, lse, swap(gctx), hid, w)
    there = lax.ppermute(gh.reshape(2, local, D)[1 - c].astype(BF), "tensor", [(i, i ^ 1) for i in range(tensor)])
    grad_in = gmix + gh.reshape(2, local, D)[c] + there.astype(F32)

    def spread(g):
        g = lax.psum_scatter(g, "tensor", scatter_dimension=0, tiled=False)
        return lax.psum_scatter(g, "dp", scatter_dimension=0, tiled=True)

    s_in, s_bt = spread(g_in.astype(F32)), spread(g_bt.astype(F32))
    s_ot = spread(g_ot.astype(F32).reshape(D, 2, pairs, 2, HD).transpose(3, 1, 0, 2, 4).reshape(tensor, D, -1))
    own = (jnp.arange(2) == c).astype(F32)
    gw = gw.reshape(pairs, D, 3, 2, HD).transpose(3, 1, 2, 0, 4).reshape(2, 1, D, -1) * own[None, :, None, None]
    s_qkv = spread(gw.reshape(tensor, D, -1)).reshape(-1, 3, pairs * HD).swapaxes(0, 1)
    bias = gb.swapaxes(0, 1).reshape(2, -1)
    bias = lax.psum(bias[:, None, :] * own[None, :, None], everyone)
    bias = lax.dynamic_index_in_dim(bias, c, 1, False)
    vector = lax.psum(vec, everyone)
    return finish(vector, bias, par, encoded, grad_in, s_qkv, s_ot.T, s_in, s_bt.T, b_in, pairs, hd)


def solution(mesh):
    rows = P(("dp", "tensor"), None)
    in_specs = (
        rows,
        rows,
        P(("dp", "tensor")),
        P(),
        P(None, "dp", "tensor"),
        P(None, "tensor", "dp"),
        P("tensor", "dp"),
        P("dp", "tensor"),
        P("tensor", "dp"),
        P("tensor", "dp"),
        P(None, "dp"),
        P(None, "dp"),
    )
    out_specs = (
        P(),
        rows,
        rows,
        P(None, "dp", "tensor"),
        P(None, "tensor", "dp"),
        P("tensor", "dp"),
        P("dp", "tensor"),
        P("tensor", "dp"),
        P("tensor", "dp"),
        P(None, ("dp", "tensor")),
        P(None, ("dp", "tensor")),
    )
    fills_tiles = (D // mesh.shape["dp"]) % 32 == 0
    step = per_device if fills_tiles else plain_device
    return jax.shard_map(step, mesh=mesh, in_specs=in_specs, out_specs=out_specs, check_vma=False)
```

```python
import functools

import jax
import jax.numpy as jnp
from jax import lax
from jax.experimental import pallas as pl
from jax.experimental.pallas import tpu as pltpu
from jax.sharding import PartitionSpec as P

D = 768
HD = 64
BLK = 64
SEQ_LEN = 2048
epsilon = 1e-06
NEG = -1e30
F32 = jnp.float32
BF = jnp.bfloat16
MESH = pl.DeviceIdType.MESH
NT = (((1,), (1,)), ((), ()))
NN = (((1,), (0,)), ((), ()))
TN = (((0,), (0,)), ((), ()))
VM = pl.BlockSpec(memory_space=pltpu.VMEM)
SM = pl.BlockSpec(memory_space=pltpu.SMEM)
ANY = pl.BlockSpec(memory_space=pl.ANY)
SDS = jax.ShapeDtypeStruct


def dot(a, b, dims):
    return lax.dot_general(a, b, dims, preferred_element_type=F32)


def params(mib, cid=None):
    if cid is None:
        return pltpu.CompilerParams(vmem_limit_bytes=mib << 20)
    return pltpu.CompilerParams(vmem_limit_bytes=mib << 20, collective_id=cid, has_side_effects=True)


class Place:
    def __init__(self):
        self.zn = lax.axis_size("dp") // 2
        dp, t = lax.axis_index("dp"), lax.axis_index("tensor")
        self.z, self.x, self.y, self.c = dp // 2, dp % 2, t // 2, t % 2

    def at(self, z=None, x=None, y=None, c=None):
        z = self.z if z is None else z
        x = self.x if x is None else x
        y = self.y if y is None else y
        c = self.c if c is None else c
        return (z * 2 + x, y * 2 + c)

    def peer(self, axis, k=1):
        if axis == "z":
            return self.at(z=(self.z + k) % self.zn)
        return {
            "x": self.at(x=1 - self.x),
            "y": self.at(y=1 - self.y),
            "c": self.at(c=1 - self.c),
        }[axis]

    def peers(self, axes):
        out = []
        for axis in axes:
            for k in range(1, self.zn if axis == "z" else 2):
                out.append(self.peer(axis, k))
        return out


def greet(place, axes):
    barrier = pltpu.get_barrier_semaphore()
    peers = place.peers(axes)
    for peer in peers:
        pl.semaphore_signal(barrier, inc=1, device_id=peer, device_id_type=MESH)
    pl.semaphore_wait(barrier, len(peers))


class Sems:
    def __init__(self, send, recv):
        self.send, self.recv, self.used = send, recv, 0

    def take(self, count):
        at = self.used
        self.used += count
        return at

    def copy(self, i, src, dst, device):
        return pltpu.make_async_remote_copy(
            src_ref=src,
            dst_ref=dst,
            send_sem=self.send.at[i],
            recv_sem=self.recv.at[i],
            device_id=device,
            device_id_type=MESH,
        )


def copies_of(order, zn):
    return sum(zn - 1 if a == "z" else 1 for a in order)


def concat_lanes(parts):
    return jnp.concatenate(parts, axis=1)


class Gather:
    def __init__(self, place, sems, shard, out, spec):
        self.place, self.shard, self.out = place, shard, out
        self.order, self.pre, self.axes, self.cut = spec
        self.sems = sems
        self.base = sems.take(copies_of(self.order, place.zn))

    def piece(self, whole):
        p = self.place
        own = {"y": p.y, "c": p.c, "z": p.z, "x": p.x}
        idx = (slice(None),) * self.pre
        idx += tuple(slice(None) if a in whole else own[a] for a in self.axes)
        return self.out.at[idx + self.cut]

    def mine(self):
        return self.shard.at[(slice(None),) * self.pre + self.cut] if self.cut else self.shard

    def local(self, sem):
        return pltpu.make_async_copy(self.mine(), self.piece(""), sem)

    def copies(self, stage):
        axis, zn = self.order[stage], self.place.zn
        if stage == 0:
            src, dst = self.mine(), self.piece("")
        else:
            src = dst = self.piece(self.order[:stage])
        at = self.base + copies_of(self.order[:stage], zn)
        return [
            self.sems.copy(at + k - 1, src, dst, self.place.peer(axis, k))
            for k in range(1, zn if axis == "z" else 2)
        ]

    def start(self, stage):
        for copy in self.copies(stage):
            copy.start()

    def wait(self, stage):
        for copy in self.copies(stage):
            copy.wait()


class Scatter:
    def __init__(self, place, sems, grad, out, spec, bufs):
        self.place, self.sems, self.grad, self.out = place, sems, grad, out
        self.order, self.pre, self.axes, self.cut = spec
        self.base = sems.take(copies_of(self.order, place.zn))
        self.keep, self.recv, self.send = bufs[0], [bufs[1]] + list(bufs[2::2]), [None] + list(bufs[3::2])
        self.own = {"y": place.y, "c": place.c, "z": place.z, "x": place.x}
        self.size = {"y": 2, "c": 2, "z": place.zn, "x": 2}

    @staticmethod
    def buffers(a, spec, zn):
        order, pre, axes, cut = spec
        size = {"y": 2, "c": 2, "z": zn, "x": 2}
        lead, tail = a.shape[:pre], a.shape[pre + len(axes) :]
        tail = tuple(len(range(*s.indices(d))) for s, d in zip(cut, tail)) + tail[len(cut) :]
        out = []
        for n, axis in enumerate(order):
            after = tuple(size[s] for s in axes if s not in order[: n + 1])
            one = lead + after + tail
            if n == 0:
                out.append(pltpu.VMEM(one, BF))
            out.append(pltpu.VMEM(((zn - 1,) if axis == "z" else ()) + one, BF))
            if n > 0:
                out.append(pltpu.VMEM(((zn,) if axis == "z" else ()) + one, BF))
        return out

    def copies(self, stage, only=None):
        p, axis = self.place, self.order[stage]
        at = self.base + copies_of(self.order[:stage], p.zn)
        recv, send = self.recv[stage], self.send[stage]
        if axis == "z":
            return [
                self.sems.copy(at + k - 1, send.at[k], recv.at[k - 1], p.peer("z", k))
                for k in (range(1, p.zn) if only is None else (only,))
            ]
        return [self.sems.copy(at, self.half(1 - self.own[axis]) if stage == 0 else send, recv, p.peer(axis))]

    def half(self, i):
        first = self.order[0]
        idx = (slice(None),) * self.pre + tuple(i if a == first else slice(None) for a in self.axes)
        return self.grad.at[idx + self.cut]

    def kept(self, here):
        return pltpu.make_async_copy(self.half(self.own[self.order[0]]), self.keep, here)

    def begin(self, here):
        self.copies(0)[0].start()
        self.kept(here).start()

    def wait(self, stage, here=None):
        for copy in self.copies(stage):
            copy.wait()
        if stage == 0:
            self.kept(here).wait()

    def total(self, n, lead, coords):
        def at(done):
            return lead + tuple(coords.get(a, self.own[a]) for a in self.axes if a not in done)

        t = self.keep[at(self.order[:1])].astype(F32)
        for m in range(n + 1):
            idx = at(self.order[: m + 1])
            if self.order[m] == "z":
                for k in range(self.place.zn - 1):
                    t = t + self.recv[m][(k,) + idx].astype(F32)
            else:
                t = t + self.recv[m][idx].astype(F32)
        return t

    def each(self, axes, fn, coords=None, lead=()):
        coords = coords or {}
        if len(lead) < self.pre:
            for i in range(self.grad.shape[len(lead)]):
                self.each(axes, fn, coords, lead + (i,))
        elif not axes:
            fn(lead, coords)
        elif axes[0] == "z":

            def body(i, carry):
                self.each(axes[1:], fn, {**coords, "z": i}, lead)
                return carry

            lax.fori_loop(0, self.size["z"], body, 0)
        else:
            for i in range(2):
                self.each(axes[1:], fn, {**coords, axes[0]: i}, lead)

    def add(self, n):
        p = self.place
        if n == len(self.order) - 1:

            def last(lead, coords):
                self.out[lead + self.cut] = self.total(n, lead, coords)

            self.each("", last)
            return
        nxt = self.order[n + 1]
        send = self.send[n + 1]
        left = [a for a in self.axes if a not in self.order[: n + 2]]
        if nxt == "z":
            for k in range(1, p.zn):
                to = (p.z + k) % p.zn

                def put(lead, coords, k=k, to=to):
                    send[(k,) + lead] = self.total(n, lead, {**coords, "z": to}).astype(BF)

                self.each(left, put)
                self.copies(n + 1, k)[0].start()
        else:

            def put(lead, coords):
                idx = lead + tuple(coords[a] for a in left)
                send[idx] = self.total(n, lead, {**coords, nxt: 1 - self.own[nxt]}).astype(BF)

            self.each(left, put)
            self.copies(n + 1)[0].start()


class SumAll:
    def __init__(self, place, sems, value, out, order, recv, held):
        self.order = order
        self.place, self.sems, self.value, self.out, self.recv, self.held = place, sems, value, out, recv, held
        self.base = sems.take(copies_of(self.order, place.zn))

    @staticmethod
    def buffers(a, order, zn):
        hops = len(order)
        return [pltpu.VMEM((hops - 2 + zn,) + a.shape, F32), pltpu.VMEM((hops - 1,) + a.shape, F32)]

    def copies(self, n):
        p = self.place
        axis = self.order[n]
        src = self.value if n == 0 else self.held.at[n - 1]
        at = self.base + n
        return [
            self.sems.copy(at + k - 1, src, self.recv.at[n + k - 1], p.peer(axis, k))
            for k in range(1, p.zn if axis == "z" else 2)
        ]

    def begin(self, here=None):
        self.copies(0)[0].start()

    def wait(self, n, here=None):
        for copy in self.copies(n):
            copy.wait()

    def add(self, n):
        mine = self.value[...] if n == 0 else self.held[n - 1]
        if n == len(self.order) - 1:
            for k in range(self.place.zn - 1):
                mine = mine + self.recv[n + k]
            self.out[...] = mine
            return
        self.held[n] = mine + self.recv[n]
        for copy in self.copies(n + 1):
            copy.start()


AFTER = 90


class Due:
    def __init__(self):
        self.todo = {}

    def add(self, step, fn):
        self.todo.setdefault(step, []).append(fn)

    def now(self, step):
        for fn in self.todo.get(step, []):
            fn()

    def __call__(self, g, first=0, last=AFTER):
        for step, fns in sorted(self.todo.items()):
            if first <= step < last:

                @pl.when(g == step - first)
                def _(fns=fns):
                    for fn in fns:
                        fn()


def relay(table, jobs, waves, window, finish):
    due, stage, behind = Due(), {}, list(waves[window:])
    for step, name in table:
        n = stage.get(name, 0)
        stage[name] = n + 1
        wave = [w for w in waves if name in w]
        begin = []
        if n == 0 and behind and wave and all(stage.get(other) for other in wave[0]):
            begin = behind.pop(0)
        due.add(step, functools.partial(finish, name, n, begin))
    assert not behind and all(stage.get(name) == len(job.order) for name, job in jobs.items())
    return due


UNROLL = 5


def stack_heads(q):
    lo = lax.broadcasted_iota(jnp.int32, q.shape, 1) < HD
    z = jnp.zeros_like(q)
    return jnp.concatenate([jnp.where(lo, q, z), jnp.where(lo, z, q)], axis=0)


def block_rows(j, count=1):
    return pl.ds(pl.multiple_of(j * BLK, BLK), count * BLK)


def flat_rows(t):
    return t.reshape(t.shape[0] * t.shape[1], t.shape[2])


def picks_of(idx_ref, p, j):
    pairs = idx_ref.shape[0] // 2
    return [(idx_ref[p, j * 3 + r], idx_ref[pairs + p, j * 3 + r]) for r in range(3)]


def slots_of(ref, p, j, picks, nb):
    lo = lax.broadcasted_iota(jnp.int32, (BLK, 2 * HD), 1) < HD
    parts = [ref[p, 0], ref[p, nb - 1], flat_rows(ref[p, pl.ds(j - 1, 3)])]
    for a, b in picks:
        parts.append(jnp.where(lo, ref[p, a], ref[p, b]))
    return jnp.concatenate(parts, axis=0)


class Forward:
    def __init__(self, idx_ref, q_ref, k_ref, v_ref, ctx_ref, lse_ref, lse_t):
        self.idx, self.q, self.k, self.v, self.ctx, self.lse, self.lse_t = (
            idx_ref,
            q_ref,
            k_ref,
            v_ref,
            ctx_ref,
            lse_ref,
            lse_t,
        )
        self.nb = q_ref.shape[1] // BLK
        self.steps = (self.nb - 2) // UNROLL

    def close(self, p, j, s, v):
        lo = lax.broadcasted_iota(jnp.int32, (BLK, 2 * HD), 1) < HD
        col = lax.broadcasted_iota(jnp.int32, (2 * BLK, 128), 1)
        m = jnp.max(s, axis=1, keepdims=True)
        e = jnp.exp(s - m)
        total = jnp.sum(e, axis=1, keepdims=True)
        o = dot(e.astype(BF), v, NN) * (1.0 / total)
        self.ctx[p, block_rows(j), :] = jnp.where(lo, o[:BLK], o[BLK:]).astype(BF)
        self.lse_t[...] = jnp.where(col == j, m + jnp.log(total), self.lse_t[...])

    def edges(self, p):
        for j in (0, self.nb - 1):
            q = stack_heads(self.q[p, j * BLK : (j + 1) * BLK, :])
            self.close(p, j, dot(q, flat_rows(self.k[p]), NT), flat_rows(self.v[p]))

    def tile(self, p, j):
        picks = picks_of(self.idx, p, j)
        q = stack_heads(self.q[p, block_rows(j), :])
        ks = slots_of(self.k, p, j, picks, self.nb)
        vs = slots_of(self.v, p, j, picks, self.nb)
        s = dot(q, ks, NT)
        col = lax.broadcasted_iota(jnp.int32, (2 * BLK, 128), 1)
        double = ((col < BLK) & (j == 1)) | ((col >= BLK) & (j == self.nb - 2))
        s = jnp.concatenate([jnp.where(double, NEG, s[:, :128]), s[:, 128:]], axis=1)
        self.close(p, j, s, vs)

    def step(self, p, i):
        for u in range(UNROLL):
            self.tile(p, 1 + i * UNROLL + u)

    def finish(self, p):
        self.lse[p] = jnp.transpose(self.lse_t[...])[: self.nb]

    def run(self, pairs, at=None):
        def body(g, carry):
            p, i = g // self.steps, g % self.steps
            if at is not None:
                at(g)

            @pl.when(i == 0)
            def _():
                self.edges(p)

            self.step(p, i)

            @pl.when(i == self.steps - 1)
            def _():
                self.finish(p)

            return carry

        lax.fori_loop(0, pairs * self.steps, body, 0)


def delta_row(do, ctx):
    d = jnp.transpose(do.astype(F32) * ctx.astype(F32))
    a = jnp.sum(d[:HD], axis=0, keepdims=True)
    b = jnp.sum(d[HD:], axis=0, keepdims=True)
    return jnp.concatenate([a, b], axis=1)


class Backward:
    def __init__(self, idx_ref, prev_ref, last_ref, q, k, v, ctx, do, lse, dq, dk, dv, dk_acc, dv_acc, dk_run, dv_run):
        self.idx, self.prev, self.last = idx_ref, prev_ref, last_ref
        self.q, self.k, self.v, self.ctx, self.do, self.lse = q, k, v, ctx, do, lse
        self.dq, self.dk, self.dv = dq, dk, dv
        self.accs = ((dk_acc, dk_run), (dv_acc, dv_run))
        self.nb = q.shape[1] // BLK
        self.steps = (self.nb - 2) // UNROLL

    def math(self, q, do, ks, vs, lse, delta, double=None):
        st = dot(ks, q, NT)
        pt = jnp.exp(st - lse)
        if double is not None:
            pt = jnp.concatenate([jnp.where(double, 0.0, pt[:128]), pt[128:]], axis=0)
        dst = (pt * (dot(vs, do, NT) - delta)).astype(BF)
        return dot(dst, ks, TN), dot(dst, q, NN), dot(pt.astype(BF), do, NN)

    def edges(self, p):
        qs, dos, ls, ds = [], [], [], []
        lo = lax.broadcasted_iota(jnp.int32, (BLK, 2 * HD), 1) < HD
        for j in (0, self.nb - 1):
            rows = slice(j * BLK, (j + 1) * BLK)
            do = self.do_block(p, j)
            qs.append(stack_heads(self.q[p, rows, :]))
            dos.append(stack_heads(do))
            ls.append(self.lse[p, j : j + 1, :])
            ds.append(delta_row(do, self.ctx[p, rows, :]))
        q, do = jnp.concatenate(qs, axis=0), jnp.concatenate(dos, axis=0)
        lse, delta = jnp.concatenate(ls, axis=1), jnp.concatenate(ds, axis=1)
        dq_sum = jnp.zeros((4 * BLK, 2 * HD), F32)
        for n in range(self.nb // 8):
            r = slice(n * 8 * BLK, (n + 1) * 8 * BLK)
            ks, vs = flat_rows(self.k[p, n * 8 : (n + 1) * 8]), flat_rows(self.v[p, n * 8 : (n + 1) * 8])
            dq, dk, dv = self.math(q, do, ks, vs, lse, delta)
            dq_sum = dq_sum + dq
            self.accs[0][0][r, :] = dk
            self.accs[1][0][r, :] = dv
        dq_sum = dq_sum * 0.125
        for n, j in enumerate((0, self.nb - 1)):
            part = dq_sum[n * 2 * BLK : (n + 1) * 2 * BLK]
            self.dq[p, j * BLK : (j + 1) * BLK, :] = jnp.where(lo, part[:BLK], part[BLK:]).astype(BF)
        for _, run in self.accs:
            run[0] = jnp.zeros((BLK, 2 * HD), F32)

    def do_block(self, p, j):
        half = self.nb // 2
        if isinstance(j, int):
            return self.do[j // half, p, (j % half) * BLK : (j % half + 1) * BLK, :]
        return self.do[j // half, p, block_rows(j % half), :]

    def tile(self, p, j):
        lo = lax.broadcasted_iota(jnp.int32, (BLK, 2 * HD), 1) < HD
        row = lax.broadcasted_iota(jnp.int32, (2 * BLK, 128), 0)
        nb, pairs = self.nb, self.idx.shape[0] // 2
        picks = picks_of(self.idx, p, j)
        q, do = self.q[p, block_rows(j), :], self.do_block(p, j)
        delta = delta_row(do, self.ctx[p, block_rows(j), :])
        ks = slots_of(self.k, p, j, picks, nb)
        vs = slots_of(self.v, p, j, picks, nb)
        double = ((row < BLK) & (j == 1)) | ((row >= BLK) & (j == nb - 2))
        dq, dk, dv = self.math(
            stack_heads(q), stack_heads(do), ks, vs, self.lse[p, pl.ds(j, 1), :], delta, double
        )
        self.dq[p, block_rows(j), :] = (jnp.where(lo, dq[:BLK], dq[BLK:]) * 0.125).astype(BF)
        for (acc, run), g in zip(self.accs, (dk, dv)):
            acc[0:BLK, :] += g[0:BLK]
            acc[(nb - 1) * BLK : nb * BLK, :] += g[BLK : 2 * BLK]
            acc[block_rows(j - 1, 3), :] += g[2 * BLK : 5 * BLK]
            for r in range(3):
                s = j * 3 + r
                before = jnp.where(lo, run[self.prev[p, s]], run[self.prev[pairs + p, s]])
                run[s - 2] = g[(5 + r) * BLK : (6 + r) * BLK] + before

    def step(self, p, i):
        for u in range(UNROLL):
            self.tile(p, 1 + i * UNROLL + u)

    def finish(self, p):
        lo = lax.broadcasted_iota(jnp.int32, (BLK, 2 * HD), 1) < HD
        pairs = self.idx.shape[0] // 2

        def body(n, carry):
            a, b = self.last[p, n], self.last[pairs + p, n]
            for (acc, run), out in zip(self.accs, (self.dk, self.dv)):
                t = acc[block_rows(n), :] + jnp.where(lo, run[a], run[b])
                out[p, block_rows(n), :] = t.astype(BF)
            return carry

        lax.fori_loop(0, self.nb, body, 0)

    def run(self, pairs, at=None, done=None):
        def body(g, carry):
            p, i = g // self.steps, g % self.steps
            if at is not None:
                at(g)

            @pl.when(i == 0)
            def _():
                self.edges(p)

            self.step(p, i)

            @pl.when(i == self.steps - 1)
            def _():
                self.finish(p)
                if done is not None:
                    done(p)

            return carry

        lax.fori_loop(0, pairs * self.steps, body, 0)


def block_tables(random_blocks, place_c):
    heads, blocks = random_blocks.shape[:2]
    own = lax.dynamic_index_in_dim(
        random_blocks.reshape((2, 2, heads // 4) + random_blocks.shape[1:]), place_c, 1, False
    ).reshape(heads // 2, blocks * 3, blocks)
    idx = jnp.sum(own * jnp.arange(blocks, dtype=jnp.int32), axis=-1)
    slots = blocks * 3
    s = jnp.arange(slots, dtype=jnp.int32)
    middle = (s >= 3) & (s < slots - 3)
    number = jnp.where(middle, s - 2, 0)
    same = (idx[:, :, None] == idx[:, None, :]) & (s[None, None, :] < s[None, :, None])
    prev = jnp.max(jnp.where(same, number[None, None, :], 0), axis=-1)
    last = jnp.max(jnp.where(own > 0, number[None, :, None], 0), axis=1)
    return idx, prev, last
SMALL_ROWS = 16


FORWARD_TABLE = (
    (-1000, "q0b"),
    (-999, "q1b"),
    (-998, "q0a"),
    (-997, "q1a"),
    (-996, "q0b"),
    (-995, "q1b"),
    (-994, "q0a"),
    (-993, "q1a"),
    (-992, "q2b"),
    (-991, "q2a"),
    (-990, "q0b"),
    (-989, "q1b"),
    (-988, "a0"),
    (-987, "b0"),
    (-986, "q2b"),
    (-985, "q1a"),
    (-984, "q0a"),
    (-983, "q2a"),
    (-982, "b0"),
    (-981, "q2b"),
    (-980, "a0"),
    (-979, "a1"),
    (-978, "b1"),
    (-977, "q2a"),
    (0, "o"),
    (1, "a2"),
    (1, "b2"),
    (5, "a1"),
    (6, "b0"),
    (6, "a2"),
    (7, "b1"),
    (7, "o"),
    (9, "b0"),
    (10, "b2"),
    (11, "a0"),
    (14, "a0"),
    (17, "a1"),
    (17, "a2"),
    (17, "o"),
    (19, "b1"),
    (20, "b2"),
    (21, "o"),
    (AFTER, "a1"),
    (AFTER, "a2"),
    (AFTER, "b1"),
    (AFTER, "b2"),
)
FORWARD_WINDOW = 2


def assemble_qkv(p, parts, w):
    zn, half = parts.shape[2], parts.shape[4]

    def body(n, carry):
        z, x = n // 2, n % 2
        for h in range(2):
            rows = pl.ds(pl.multiple_of(n * 2 * half + h * half, half), half)
            src = [parts[p, y, z, x, :, h * 3 * HD : (h + 1) * 3 * HD] for y in range(2)]
            for k in range(3):
                w[p, rows, k * 128 : (k + 1) * 128] = concat_lanes([s[:, k * HD : (k + 1) * HD] for s in src])
        return carry

    lax.fori_loop(0, zn * 2, body, 0)


def project_rows(p, i, chunk, hid, w, bias, q, k, v):
    per = hid.shape[1] // chunk
    src = hid[i // per, pl.ds(pl.multiple_of(i % per * chunk, chunk), chunk), :]
    t = dot(src, w[p], NN)
    part = (t[:, :128] + bias[0:1, :]).astype(BF).astype(F32) * 0.125
    q[p, pl.ds(pl.multiple_of(i * chunk, chunk), chunk), :] = part.astype(BF)
    rows = pl.ds(i * (chunk // BLK), chunk // BLK)
    k[p, rows] = t[:, 128:256].astype(BF).reshape(chunk // BLK, BLK, 128)
    v[p, rows] = (t[:, 256:] + bias[1:2, :]).astype(BF).reshape(chunk // BLK, BLK, 128)


def place_small(place, out, b_qv, b_in, ln_gains, row_biases, mask):
    def lane(rows):
        return lax.broadcasted_iota(jnp.int32, (rows, D), 1)

    def row(rows):
        return lax.broadcasted_iota(jnp.int32, (rows, D), 0)

    def ones(where):
        return where.astype(F32).astype(BF)

    dp = place.z * 2 + place.x
    t = place.y * 2 + place.c
    pairs, _, n = b_qv.shape
    units = b_in.shape[1]
    share = ln_gains.shape[1]
    out[...] = jnp.zeros_like(out)
    wide = dot(b_in[...], ones(lane(units) // HD == row(units)), NN)
    own = jnp.sum(jnp.where(lane(n) % HD == dp * n + row(n), wide, 0.0), axis=0, keepdims=True)
    for i in range(4):
        out[i : i + 1, :] = jnp.where(t == i, own, 0.0)
    at = ones(lane(share) == dp * share + row(share))
    one = jnp.where(t == 0, 1.0, 0.0)
    out[4:6, :] = dot(ln_gains[...], at, NN) * one
    out[6:10, :] = dot(row_biases[...], at, NN) * one
    count = jnp.sum(mask[...].astype(F32))
    out[10:11, :] = jnp.where(lane(1) == 0, count, 0.0)
    at = ones(lane(n) % HD == dp * n + row(n))
    total = jnp.zeros((2, D), F32)
    for p in range(pairs):
        here = (lane(2) // 128 == place.c * pairs + p) & (lane(2) % 128 // HD == place.y)
        total = total + jnp.where(here, dot(b_qv[p], at, NN), 0.0)
    out[11:13, :] = total


def gather_attend_kernel(
    idx_ref,
    wqkv_ref,
    h_ref,
    bqv_ref,
    bin_ref,
    gain_ref,
    rowb_ref,
    mask_ref,
    win_ref,
    wbt,
    wo_ref,
    q_out,
    k_out,
    v_out,
    ctx_out,
    lse_ref,
    rows_ref,
    hidt_out,
    w_out,
    fin_ref,
    fbt_ref,
    fot_ref,
    par_ref,
    send,
    recv,
    here,
    q_ref,
    k_ref,
    v_ref,
    ctx_ref,
    hidt_ref,
    w_ref,
    hid_ref,
    wq,
    parts,
    small_ref,
    wot,
    s_recv,
    s_held,
    lse_t,
):
    place = Place()
    c = place.c
    local = h_ref.shape[0]
    pairs = q_ref.shape[0]
    share = win_ref.shape[0]
    half = share // 2
    for p in range(pairs):
        cols = slice(p * HD, (p + 1) * HD)
        wq[p] = concat_lanes([wqkv_ref[k, h * half : (h + 1) * half, cols] for h in range(2) for k in range(3)])
    greet(place, "zxyc")
    sems = Sems(send, recv)
    jobs, waves = {}, []
    for p in range(pairs):
        orders = ("zxy", "zyx") if p % 2 == 0 else ("zyx", "zxy")
        lanes = (slice(0, 2 * 128), slice(2 * 128, 3 * 128))
        for name, order, lane in zip("ab", orders, lanes):
            spec = (order, 0, "yzx", (slice(None), lane))
            jobs[f"q{p}{name}"] = Gather(place, sems, wq.at[p], parts.at[p], spec)
        waves.append([f"q{p}a", f"q{p}b"])
    count = 3
    size = share // count
    for n in range(count):
        rows = (slice(n * size, (n + 1) * size),)
        jobs[f"a{n}"] = Gather(place, sems, win_ref, fin_ref, ("zxyc", 0, "yczx", rows))
        jobs[f"b{n}"] = Gather(place, sems, wbt, fbt_ref, ("zyxc", 0, "yczx", rows))
        waves.append([f"a{n}", f"b{n}"])
    jobs["o"] = Gather(place, sems, wot, fot_ref, ("zyxc", 0, "yczx", ()))
    waves[-1].append("o")
    hid = Gather(place, sems, h_ref, hid_ref, ("c", 0, "c", ()))
    small = SumAll(place, sems, small_ref, par_ref, "cyxz", s_recv, s_held)
    swap_at = sems.take(pairs)
    for wave in waves[:FORWARD_WINDOW]:
        for name in wave:
            jobs[name].start(0)
    hid.start(0)
    own = [pltpu.make_async_copy(wq.at[p], parts.at[p, place.y, place.z, place.x], here.at[p]) for p in range(pairs)]
    own.append(hid.local(here.at[pairs]))
    for copy in own:
        copy.start()
    place_small(place, small_ref, bqv_ref, bin_ref, gain_ref, rowb_ref, mask_ref)
    small.begin()
    t = wo_ref[...].T
    wot[...] = concat_lanes([t[:half], t[half:]])
    late = [
        pltpu.make_async_copy(src, out.at[place.y, c, place.z, place.x], here.at[pairs + 1 + n])
        for n, (src, out) in enumerate(((win_ref, fin_ref), (wbt, fbt_ref), (wot, fot_ref)))
    ]
    for copy in late:
        copy.start()
    for copy in own:
        copy.wait()
    in_flight = dict(zip("abo", late))

    def pass_on(name, stage, begin):
        if name[0] in in_flight:
            in_flight.pop(name[0]).wait()
        jobs[name].wait(stage)
        if stage + 1 < len(jobs[name].order):
            jobs[name].start(stage + 1)
        for other in begin:
            jobs[other].start(0)

    due = relay(FORWARD_TABLE, jobs, waves, FORWARD_WINDOW, pass_on)
    early = sorted(step for step in due.todo if step < 0)
    for n, step in enumerate(early):
        due.now(step)
        if n == 1:
            hid.wait(0)
            for i in range(2):
                hidt_ref[:, i * local : (i + 1) * local] = hid_ref[i].T
        if n < 4:
            small.wait(n)
            small.add(n)
    chunk = local // 2
    attend = Forward(idx_ref, q_ref, k_ref, v_ref, ctx_ref, lse_ref, lse_t)

    def there(p):
        rows = pl.ds(pl.multiple_of((1 - c) * local, local), local)
        return sems.copy(swap_at + p, ctx_ref.at[p, rows, :], rows_ref.at[c, p], place.peer("c"))

    bias = jnp.where(c == 0, par_ref[11:13, : pairs * 128], par_ref[11:13, pairs * 128 :])
    for p in range(pairs):
        assemble_qkv(p, parts, w_ref)

    def project(i, carry):
        due(i, 0, 4)
        for p in range(pairs):
            project_rows(p, i, chunk, hid_ref, w_ref, bias[:, p * 128 : (p + 1) * 128], q_ref, k_ref, v_ref)
        return carry

    lax.fori_loop(0, 4, project, 0)
    stores = [
        pltpu.make_async_copy(src, dst, here.at[pairs + 4 + n])
        for n, (src, dst) in enumerate(
            ((q_ref, q_out), (k_ref, k_out), (v_ref, v_out), (hidt_ref, hidt_out), (w_ref, w_out), (ctx_ref, ctx_out))
        )
    ]
    for copy in stores[:5]:
        copy.start()
    attend.run(pairs, lambda g: due(g, 4))
    for p in range(pairs):
        there(p).start()
    mine = pltpu.make_async_copy(
        ctx_ref.at[:, pl.ds(pl.multiple_of(c * local, local), local), :], rows_ref.at[c], here.at[0]
    )
    mine.start()
    stores[5].start()
    due.now(AFTER)
    for copy in stores:
        copy.wait()
    mine.wait()
    for p in range(pairs):
        there(p).wait()


def gather_attend(idx, w_qkv, hidden, smalls, w_in, w_bt, w_out, pairs, zn, cid):
    local = hidden.shape[0]
    n = 2 * local
    share, wide = w_in.shape
    heads_shape = SDS((pairs, n, 128), BF)
    blocks_shape = SDS((pairs, n // BLK, BLK, 128), BF)
    packed = (share // 2, 6 * HD)
    small = SDS((SMALL_ROWS, D), F32)
    copies = 2 * pairs * copies_of("zxy", zn) + 1 + copies_of("cyxz", zn) + 7 * copies_of("zxyc", zn) + pairs
    return pl.pallas_call(
        gather_attend_kernel,
        out_shape=(
            heads_shape,
            blocks_shape,
            blocks_shape,
            heads_shape,
            SDS((pairs, n // BLK, 128), F32),
            SDS((2, pairs, local, 128), BF),
            SDS((D, n), BF),
            SDS((pairs, D, 3 * 128), BF),
            SDS((2, 2, zn, 2, share, wide), BF),
            SDS((2, 2, zn, 2, share, wide), BF),
            SDS((2, 2, zn, 2) + packed, BF),
            SDS(small.shape, F32),
        ),
        in_specs=[SM, VM, ANY] + [VM] * len(smalls) + [ANY, ANY, VM],
        out_specs=(ANY,) * 4 + (VM,) + (ANY,) * 6 + (VM,),
        scratch_shapes=[
            pltpu.SemaphoreType.DMA((copies,)),
            pltpu.SemaphoreType.DMA((copies,)),
            pltpu.SemaphoreType.DMA((pairs + 10,)),
            pltpu.VMEM(heads_shape.shape, BF),
            pltpu.VMEM(blocks_shape.shape, BF),
            pltpu.VMEM(blocks_shape.shape, BF),
            pltpu.VMEM(heads_shape.shape, BF),
            pltpu.VMEM((D, n), BF),
            pltpu.VMEM((pairs, D, 3 * 128), BF),
            pltpu.VMEM((2, local, D), BF),
            pltpu.VMEM((pairs,) + packed, BF),
            pltpu.VMEM((pairs, 2, zn, 2) + packed, BF),
            pltpu.VMEM(small.shape, F32),
            pltpu.VMEM(packed, BF),
        ]
        + SumAll.buffers(small, "cyxz", zn)
        + [pltpu.VMEM((128, 128), F32)],
        compiler_params=params(56, cid),
        name="gather_attend",
    )(idx, w_qkv, hidden, *smalls, w_in, w_bt, w_out)
def norm(v):
    centred = v - jnp.mean(v, axis=-1, keepdims=True)
    rs = lax.rsqrt(jnp.mean(centred * centred, axis=-1, keepdims=True) + epsilon)
    return centred * rs, rs


def norm_back(g, gain, xhat, rs):
    gx = gain * g
    return rs * (gx - jnp.mean(gx, axis=-1, keepdims=True) - xhat * jnp.mean(gx * xhat, axis=-1, keepdims=True))


def gelu_both(v):
    k, a = 0.7978845608028654, 0.044715
    v2 = v * v
    th = jnp.tanh(k * v * (1.0 + a * v2))
    half = 0.5 * (1.0 + th)
    slope = half + (0.5 * k) * v * (1.0 - th * th) * (1.0 + (3.0 * a) * v2)
    return v * half, slope


def assemble_out(parts, w):
    zn, half = parts.shape[2], parts.shape[4]
    wide = parts.shape[5] // 2
    pairs = wide // HD

    def body(n, carry):
        z, x = n // 2, n % 2
        for h in range(2):
            rows = pl.ds(pl.multiple_of(n * 2 * half + h * half, half), half)
            for c in range(2):
                for p in range(pairs):
                    at = h * wide + p * HD
                    w[rows, (c * pairs + p) * 128 : (c * pairs + p + 1) * 128] = concat_lanes(
                        [parts[y, c, z, x, :, at : at + HD] for y in range(2)]
                    )
        return carry

    lax.fori_loop(0, zn * 2, body, 0)


def scatter_out(w, parts):
    zn, half = parts.shape[2], parts.shape[4]
    wide = parts.shape[5] // 2
    pairs = wide // HD

    def body(n, carry):
        z, x = n // 2, n % 2
        src = [w[pl.ds(pl.multiple_of(n * 2 * half + h * half, half), half), :] for h in range(2)]
        for y in range(2):
            for c in range(2):
                cols = [(c * pairs + p) * 128 + y * HD for p in range(pairs)]
                parts[y, c, z, x] = concat_lanes([s[:, a : a + HD] for s in src for a in cols]).astype(BF)
        return carry

    lax.fori_loop(0, zn * 2, body, 0)


def mask_rows(m_ref, step, tile):
    columns = m_ref[...].astype(F32).T
    at = lax.broadcasted_iota(jnp.int32, columns.shape, 1)
    per = tile // 128
    parts = [
        jnp.sum(jnp.where(at == step * per + i, columns, 0.0), axis=1, keepdims=True) for i in range(per)
    ]
    return jnp.concatenate(parts, axis=0)


def rows_kernel(
    tokens_total,
    packed,
    ctx_ref,
    h_ref,
    t_ref,
    m_ref,
    w_in,
    w_bt,
    w_ot,
    par,
    enc_ref,
    gmix_ref,
    gctx_ref,
    gin_ref,
    gbt_ref,
    got_ref,
    vec_ref,
    slope,
    act,
    ginner,
    nlow_t,
    slow_t,
    w_o,
    got,
):
    step = pl.program_id(0)
    tile = h_ref.shape[0]
    units = w_in.shape[0]
    pairs = ctx_ref.shape[1]
    r = pl.ds(pl.multiple_of(step * tile, tile), tile)

    @pl.when(step == 0)
    def _():
        vec_ref[...] = jnp.zeros_like(vec_ref)
        got[...] = jnp.zeros_like(got)
        if packed:
            assemble_out(w_ot, w_o)
        else:
            w_o[...] = w_ot[...]

    gains, biases = par[4:6, :], par[6:10, :]
    scale = tokens_total / par[10:11, 0:1]
    ctx = concat_lanes([ctx_ref[n, p] for n in range(2) for p in range(pairs)])
    mixed = h_ref[...].astype(F32) + dot(ctx, w_o[...], NT) + biases[0:1, :]
    xhat1, rs1 = norm(mixed)
    normed = xhat1 * gains[0:1, :] + biases[1:2, :]
    nlow = normed.astype(BF)
    nlow_t[:, r] = nlow.T
    second = normed + biases[2:3, :]
    for u in range(units):
        inner = dot(nlow, w_in[u], NN) + par[u : u + 1, :]
        a, s = gelu_both(inner)
        a = a.astype(BF)
        act[u, r, :] = a
        slope[u] = s
        second = second + dot(a, w_bt[u], NT)
    xhat2, rs2 = norm(second)
    encoded = xhat2 * gains[1:2, :] + biases[3:4, :]
    enc_ref[...] = encoded
    error = encoded - t_ref[...]
    merr = mask_rows(m_ref, step, tile) * error
    genc = merr * scale
    gsec = norm_back(genc, gains[1:2, :], xhat2, rs2)
    slow = gsec.astype(BF)
    slow_t[:, r] = slow.T
    gnorm = gsec
    for u in range(units):
        gi = (dot(slow, w_bt[u], NN) * slope[u]).astype(BF)
        ginner[u, r, :] = gi
        vec_ref[6 + u : 7 + u, :] += jnp.sum(gi.astype(F32), axis=0, keepdims=True)
        gnorm = gnorm + dot(gi, w_in[u], NT)
    gmix = norm_back(gnorm, gains[0:1, :], xhat1, rs1)
    gmix_ref[...] = gmix
    mlow = gmix.astype(BF)
    gctx = dot(mlow, w_o[...], NN).astype(BF)
    for n in range(2):
        for p in range(pairs):
            gctx_ref[n, p] = gctx[:, (n * pairs + p) * 128 : (n * pairs + p + 1) * 128]
    sums = (gnorm * xhat1, genc * xhat2, gmix, gnorm, gsec, genc)
    for n, value in enumerate(sums):
        vec_ref[n : n + 1, :] += jnp.sum(value, axis=0, keepdims=True)
    vec_ref[10:11, :] += jnp.sum(merr * error, axis=0, keepdims=True)
    got[...] += dot(mlow.T, ctx, NN)

    @pl.when(step == pl.num_programs(0) - 1)
    def _():
        if packed:
            scatter_out(got, got_ref)
        else:
            got_ref[...] = got[...].astype(BF)
        for u in range(units):
            gin_ref[u] = dot(nlow_t[...], ginner[u], NN).astype(BF)
            gbt_ref[u] = dot(slow_t[...], act[u], NN).astype(BF)


def row_pass(tokens_total, ctx, hidden, teacher, mask, w_in, w_bt, w_ot, par, tile):
    n = hidden.shape[0]
    units, _, wide = w_in.shape
    pairs = ctx.shape[1]
    once = pl.Buffered(1)

    def whole(a):
        return pl.BlockSpec(a.shape, lambda i, nd=len(a.shape): (0,) * nd, pipeline_mode=once)

    def rows(width):
        return pl.BlockSpec((tile, width), lambda i: (i, 0))

    heads = pl.BlockSpec((2, pairs, tile, 128), lambda i: (0, 0, i, 0))
    outs = (
        SDS((n, D), F32),
        SDS((n, D), F32),
        SDS((2, pairs, n, 128), BF),
        SDS(w_in.shape, BF),
        SDS(w_in.shape, BF),
        SDS(w_ot.shape, BF),
        SDS((SMALL_ROWS, D), F32),
    )
    return pl.pallas_call(
        functools.partial(rows_kernel, float(tokens_total), len(w_ot.shape) > 2),
        grid=(n // tile,),
        out_shape=outs,
        in_specs=[heads, rows(D), rows(D)] + [whole(a) for a in (mask, w_in, w_bt, w_ot, par)],
        out_specs=(rows(D), rows(D), heads) + tuple(whole(a) for a in outs[3:]),
        scratch_shapes=[
            pltpu.VMEM((units, tile, wide), F32),
            pltpu.VMEM((units, n, wide), BF),
            pltpu.VMEM((units, n, wide), BF),
            pltpu.VMEM((D, n), BF),
            pltpu.VMEM((D, n), BF),
            pltpu.VMEM((D, D), BF),
            pltpu.VMEM((D, D), F32),
        ],
        compiler_params=params(62),
        name="row_pass",
    )(ctx, hidden, teacher, mask, w_in, w_bt, w_ot, par)
BACKWARD_TABLE = (
    (1, "a0"),
    (1, "b0"),
    (5, "a1"),
    (5, "b1"),
    (6, "a0"),
    (6, "b0"),
    (6, "v"),
    (7, "o"),
    (7, "a2"),
    (7, "b2"),
    (8, "v"),
    (10, "q0b"),
    (11, "a1"),
    (11, "v"),
    (11, "b1"),
    (12, "q0a"),
    (12, "a0"),
    (12, "b0"),
    (12, "v"),
    (12, "q0b"),
    (15, "q0b"),
    (15, "b1"),
    (16, "q1b"),
    (16, "a2"),
    (17, "o"),
    (17, "a0"),
    (17, "b0"),
    (AFTER, "q0a"),
    (AFTER, "a1"),
    (AFTER, "b1"),
    (AFTER, "b2"),
    (AFTER, "q1b"),
    (AFTER, "q1a"),
    (AFTER, "o"),
    (AFTER + 1, "a2"),
    (AFTER + 1, "s"),
    (AFTER + 3, "q2b"),
    (AFTER + 3, "q0a"),
    (AFTER + 3, "q1b"),
    (AFTER + 3, "s"),
    (AFTER + 3, "a1"),
    (AFTER + 3, "q1a"),
    (AFTER + 3, "o"),
    (AFTER + 3, "a2"),
    (AFTER + 3, "s"),
    (AFTER + 3, "q2a"),
    (AFTER + 3, "q2b"),
    (AFTER + 3, "b2"),
    (AFTER + 3, "q1a"),
    (AFTER + 3, "q2b"),
    (AFTER + 3, "q2a"),
    (AFTER + 3, "b2"),
    (AFTER + 3, "q2a"),
)
BACKWARD_WINDOW = 1
CHUNKS = 3


def sum_specs(share, pairs):
    size = share // CHUNKS
    specs = []
    for n in range(CHUNKS):
        rows = (slice(n * size, (n + 1) * size),)
        specs.append((f"a{n}", "in", ("cyxz", 0, "yczx", rows)))
        specs.append((f"b{n}", "back", ("cxyz", 0, "yczx", rows)))
    specs.append(("o", "out", ("cxyz", 0, "yczx", ())))
    for p in range(pairs):
        orders = ("yxz", "xyz") if p % 2 == 0 else ("xyz", "yxz")
        lanes = (slice(0, 2 * 128), slice(2 * 128, 3 * 128))
        for name, order, lane in zip("ab", orders, lanes):
            specs.append((f"q{p}{name}", p, (order, 0, "yzx", (slice(None), lane))))
    return specs


def weight_grad(p, hid_t, dq, dk, dv):
    return dot(hid_t[...], concat_lanes([dq[p], dk[p], dv[p]]), NN)


def hidden_grad(dq, dk, dv, w, rows):
    pairs = dq.shape[0]
    grads = concat_lanes([g[p, rows, :] for p in range(pairs) for g in (dq, dk, dv)])
    return dot(grads, concat_lanes([w[p] for p in range(pairs)]), NT)


def attend_sum_kernel(
    idx_ref,
    prev_ref,
    last_ref,
    q_in,
    k_in,
    v_in,
    ctx_in,
    lse_ref,
    gctx_ref,
    hid_in,
    w_in,
    gmix_ref,
    gin_ref,
    gbt_ref,
    got_ref,
    vec_ref,
    out_ref,
    gh_recv,
    sin_ref,
    sbt,
    sot_ref,
    sq_ref,
    vsum_ref,
    bsum_ref,
    send,
    recv,
    here,
    q_ref,
    k_ref,
    v_ref,
    ctx_ref,
    hid_t,
    w_ref,
    do_ref,
    dq,
    dk,
    dv,
    dk_acc,
    dv_acc,
    dk_run,
    dv_run,
    gq,
    gh_send,
    bias,
    sot,
    sq,
    v_recv,
    v_held,
    b_recv,
    b_held,
    *bufs,
):
    place = Place()
    c = place.c
    pairs = q_ref.shape[0]
    local = gmix_ref.shape[0]
    share = gin_ref.shape[-2]
    greet(place, "zxyc")
    sems = Sems(send, recv)
    grads = {"in": (gin_ref, sin_ref), "back": (gbt_ref, sbt), "out": (got_ref, sot)}
    for p in range(pairs):
        grads[p] = (gq.at[p], sq.at[p])
    jobs, spot, rest = {}, {}, list(bufs)
    for name, which, spec in sum_specs(share, pairs):
        grad, out = grads[which]
        count = len(Scatter.buffers(grad, spec, place.zn))
        spot[name] = here.at[len(jobs)]
        jobs[name] = Scatter(place, sems, grad, out, spec, rest[:count])
        rest = rest[count:]
    jobs["v"] = SumAll(place, sems, vec_ref, vsum_ref, "cyxz", v_recv, v_held)
    jobs["s"] = SumAll(place, sems, bias, bsum_ref, "yxz", b_recv, b_held)
    spot["v"] = spot["s"] = None
    waves = [[f"a{n}", f"b{n}"] for n in range(CHUNKS)]
    waves[-1] += ["o", "v"]
    swaps = sems.take(2)
    first = sems.copy(swaps, gctx_ref.at[1 - c], do_ref.at[c], place.peer("c"))
    first.start()
    mine = pltpu.make_async_copy(gctx_ref.at[c], do_ref.at[c], here.at[len(jobs)])
    mine.start()
    for wave in waves[:BACKWARD_WINDOW]:
        for name in wave:
            jobs[name].begin(spot[name])
    loads = [
        pltpu.make_async_copy(src, dst, here.at[len(jobs) + 2 + n])
        for n, (src, dst) in enumerate(
            ((q_in, q_ref), (k_in, k_ref), (v_in, v_ref), (ctx_in, ctx_ref), (hid_in, hid_t), (w_in, w_ref))
        )
    ]
    for copy in loads:
        copy.start()
    start_out = pltpu.make_async_copy(gmix_ref, out_ref, here.at[len(jobs) + 1])
    start_out.start()
    bias[...] = jnp.zeros_like(bias)

    def advance(name, stage, begin):
        jobs[name].wait(stage, spot[name])
        jobs[name].add(stage)
        for other in begin:
            jobs[other].begin(spot[other])

    due = relay(BACKWARD_TABLE, jobs, waves, BACKWARD_WINDOW, advance)
    for step in sorted(step for step in due.todo if step < 0):
        due.now(step)
    mine.wait()
    first.wait()
    for copy in loads:
        copy.wait()
    attend = Backward(
        idx_ref, prev_ref, last_ref, q_ref, k_ref, v_ref, ctx_ref, do_ref, lse_ref, dq, dk, dv,
        dk_acc, dv_acc, dk_run, dv_run,
    )
    half = gq.shape[4]

    def done(p):
        t = weight_grad(p, hid_t, dq, dk, dv).astype(BF)
        for z in range(place.zn):
            for x in range(2):
                at = (z * 2 + x) * 2 * half
                src = [t[at + h * half : at + (h + 1) * half] for h in range(2)]
                for y in range(2):
                    gq[p, y, z, x] = concat_lanes(
                        [s[:, k * 128 + y * HD : k * 128 + (y + 1) * HD] for s in src for k in range(3)]
                    )
        lanes = pl.ds(pl.multiple_of(p * 128, 128), 128)
        for row, g in enumerate((dq, dv)):
            bias[row : row + 1, lanes] = jnp.sum(g[p].astype(F32), axis=0, keepdims=True)
        for n in range(pairs):

            @pl.when(p == n)
            def _(n=n):
                for name in (f"q{n}a", f"q{n}b"):
                    jobs[name].begin(spot[name])

    attend.run(pairs, due, done)
    jobs["s"].begin()
    size = local // 2

    def other(i, carry):
        t = hidden_grad(dq, dk, dv, w_ref, pl.ds(pl.multiple_of((1 - c) * local + i * size, size), size))
        gh_send[pl.ds(pl.multiple_of(i * size, size), size), :] = t.astype(BF)
        return carry

    due.now(AFTER)
    lax.fori_loop(0, 2, other, 0)
    swap = sems.copy(swaps + 1, gh_send, gh_recv, place.peer("c"))
    swap.start()
    start_out.wait()
    due.now(AFTER + 1)

    def own(i, carry):
        rows = pl.ds(pl.multiple_of(i * size, size), size)
        t = hidden_grad(dq, dk, dv, w_ref, pl.ds(pl.multiple_of(c * local + i * size, size), size))
        out_ref[rows, :] += t
        return carry

    lax.fori_loop(0, 2, own, 0)
    due.now(AFTER + 2)
    due.now(AFTER + 3)
    swap.wait()
    t = sot[...]
    wide = pairs * HD
    sot_ref[...] = jnp.concatenate([t[:, :wide], t[:, wide:]], axis=0).T
    for h in range(2):
        for k in range(3):
            at = (h * 3 + k) * HD
            sq_ref[k, h * half : (h + 1) * half, :] = concat_lanes([sq[p, :, at : at + HD] for p in range(pairs)])


def attend_sum(tables, q, k, v, ctx, lse, gctx, hid_t, w, gmix, g_in, g_bt, g_ot, vec, zn, cid):
    pairs, n, _ = q.shape
    local = gmix.shape[0]
    share, wide = g_in.shape[-2:]
    blocks = n // BLK
    packed = g_ot.shape[-2:]
    gq = (pairs, 2, zn, 2) + packed
    heads = pltpu.VMEM((pairs, n, 128), BF)
    bias = SDS((8, pairs * 128), F32)
    shapes = {"in": g_in, "back": g_bt, "out": g_ot}
    bufs = []
    copies = copies_of("cyxz", zn) + copies_of("yxz", zn) + 2
    specs = sum_specs(share, pairs)
    for _, which, spec in specs:
        bufs += Scatter.buffers(shapes.get(which, SDS(gq[1:], BF)), spec, zn)
        copies += copies_of(spec[0], zn)
    return pl.pallas_call(
        attend_sum_kernel,
        out_shape=(
            SDS((local, D), F32),
            SDS((local, D), BF),
            SDS((share, wide), F32),
            SDS((share, wide), F32),
            SDS((pairs * HD, share), F32),
            SDS((3, share, pairs * HD), F32),
            SDS(vec.shape, F32),
            bias,
        ),
        in_specs=[SM] * 3 + [ANY] * 4 + [VM] + [ANY] * 7 + [VM],
        out_specs=(VM,) * 8,
        scratch_shapes=[
            pltpu.SemaphoreType.DMA((copies,)),
            pltpu.SemaphoreType.DMA((copies,)),
            pltpu.SemaphoreType.DMA((len(specs) + 10,)),
            pltpu.VMEM(q.shape, BF),
            pltpu.VMEM(k.shape, BF),
            pltpu.VMEM(v.shape, BF),
            pltpu.VMEM(ctx.shape, BF),
            pltpu.VMEM(hid_t.shape, BF),
            pltpu.VMEM(w.shape, BF),
            pltpu.VMEM(gctx.shape, BF),
            heads,
            heads,
            heads,
            pltpu.VMEM((n, 128), F32),
            pltpu.VMEM((n, 128), F32),
            pltpu.VMEM((3 * (blocks - 2) + 1, BLK, 128), F32),
            pltpu.VMEM((3 * (blocks - 2) + 1, BLK, 128), F32),
            pltpu.VMEM(gq, BF),
            pltpu.VMEM((local, D), BF),
            pltpu.VMEM(bias.shape, F32),
            pltpu.VMEM(packed, F32),
            pltpu.VMEM((pairs,) + packed, F32),
        ]
        + SumAll.buffers(vec, "cyxz", zn)
        + SumAll.buffers(bias, "yxz", zn)
        + bufs,
        compiler_params=params(62, cid),
        name="attend_sum",
    )(*tables, q, k, v, ctx, lse, gctx, hid_t, w, gmix, g_in, g_bt, g_ot, vec)


def take_kernel(
    par_ref,
    vec_ref,
    bias_ref,
    part_ref,
    recv_ref,
    sin_ref,
    sbt_ref,
    sot_ref,
    sq_ref,
    loss_ref,
    out_ref,
    oq_ref,
    ob_ref,
    oo_ref,
    oi_ref,
    obin_ref,
    obt_ref,
    og_ref,
    orow_ref,
):
    place = Place()
    dp = place.z * 2 + place.x
    t = place.y * 2 + place.c
    out_ref[...] = part_ref[...] + recv_ref[...].astype(F32)
    oq_ref[...] = sq_ref[...]
    oo_ref[...] = sot_ref[...]
    oi_ref[...] = sin_ref[...]
    obt_ref[...] = sbt_ref[...]
    loss_ref[...] = jnp.sum(vec_ref[10:11, :], axis=1, keepdims=True) / (float(D) * par_ref[10:11, 0:1])

    def exact(a, b):
        return lax.dot_general(a, b, NN, precision=lax.Precision.HIGHEST, preferred_element_type=F32)

    cols = og_ref.shape[1]
    part = dp * 4 + t
    l = lax.broadcasted_iota(jnp.int32, (D, cols), 0)
    i = lax.broadcasted_iota(jnp.int32, (D, cols), 1)
    both = exact(vec_ref[0:8, :], (l == part * cols + i).astype(F32))
    og_ref[...] = both[:2]
    orow_ref[...] = both[2:6]
    n = obin_ref.shape[0]
    units = obin_ref.shape[1]
    row = jnp.zeros((1, D), F32)
    for u in range(4):
        row = row + jnp.where(t == u, 1.0, 0.0) * vec_ref[6 + u : 7 + u, :]
    l = lax.broadcasted_iota(jnp.int32, (n, D), 1)
    i = lax.broadcasted_iota(jnp.int32, (n, D), 0)
    own = jnp.where(l % HD == dp * n + i, row, 0.0)
    l = lax.broadcasted_iota(jnp.int32, (D, units), 0)
    u = lax.broadcasted_iota(jnp.int32, (D, units), 1)
    obin_ref[...] = exact(own, (l // HD == u).astype(F32))
    e = bias_ref.shape[1]
    l = lax.broadcasted_iota(jnp.int32, (e, n), 0)
    i = lax.broadcasted_iota(jnp.int32, (e, n), 1)
    for p in range(ob_ref.shape[0]):
        ob_ref[p] = exact(bias_ref[...], (l == p * 128 + place.y * HD + dp * n + i).astype(F32))[:2]


def take(par, vec, bias, part, recv, s_in, s_bt, s_ot, s_q, b_in_shape, b_qv_shape):
    dp, tensor = lax.axis_size("dp"), lax.axis_size("tensor")
    cols = D // (dp * tensor)
    outs = (
        SDS((1, 1), F32),
        SDS(part.shape, F32),
        SDS(s_q.shape, F32),
        SDS((b_qv_shape[1], b_qv_shape[0], b_qv_shape[2]), F32),
        SDS(s_ot.shape, F32),
        SDS(s_in.shape, F32),
        SDS((b_in_shape[1], b_in_shape[0]), F32),
        SDS(s_bt.shape, F32),
        SDS((2, cols), F32),
        SDS((4, cols), F32),
    )
    return pl.pallas_call(
        take_kernel,
        out_shape=outs,
        in_specs=[VM] * 9,
        out_specs=(VM,) * len(outs),
        compiler_params=params(62),
        name="take_parts",
    )(par, vec, bias, part, recv, s_in, s_bt, s_ot, s_q)


def small_parts(b_qv, b_in, ln_gains, row_biases, count):
    dp, dpi = lax.axis_size("dp"), lax.axis_index("dp")
    t = lax.axis_index("tensor")
    y, c = t // 2, t % 2

    def at(i, size):
        return (jnp.arange(size) == i).astype(F32)

    heads, hd = b_qv.shape[1:]
    units = at(t, 4)[:, None, None, None] * b_in.astype(F32)[None, :, None, :] * at(dpi, dp)[None, None, :, None]
    rows = jnp.concatenate([ln_gains, row_biases]).astype(F32)
    rows = rows[:, None, :] * at(dpi, dp)[None, :, None] * (t == 0).astype(F32)
    total = count * at(0, D)
    bias = b_qv.astype(F32)[:, None, :, None, None, :] * at(c, 2)[None, :, None, None, None, None]
    bias = bias * at(y, 2)[None, None, None, :, None, None] * at(dpi, dp)[None, None, None, None, :, None]
    out = jnp.concatenate([units.reshape(4, D), rows.reshape(6, D), total.reshape(1, D), bias.reshape(2, D)])
    return jnp.pad(out, ((0, SMALL_ROWS - out.shape[0]), (0, 0)))


def finish(vector, bias, par, encoded, grad_in, s_qkv, s_out, s_in, s_back, b_in, pairs, hd):
    dp, tensor = lax.axis_size("dp"), lax.axis_size("tensor")
    dpi, ti = lax.axis_index("dp"), lax.axis_index("tensor")
    part = dpi * tensor + ti
    cols = D // (dp * tensor)
    gains_biases = lax.dynamic_slice_in_dim(vector[:6], part * cols, cols, 1)
    grad_b_in = lax.dynamic_index_in_dim(vector[6:10].reshape(tensor, b_in.shape[0], dp, hd), ti, 0, False)
    grad_b_in = lax.dynamic_index_in_dim(grad_b_in, dpi, 1, False)
    grad_qv = lax.dynamic_index_in_dim(bias.reshape(2, pairs, 2, dp, hd), ti // 2, 2, False)
    grad_qv = lax.dynamic_index_in_dim(grad_qv, dpi, 2, False)
    loss = jnp.sum(vector[10]) / (D * par[10, 0])
    return (
        loss,
        encoded,
        grad_in,
        s_qkv,
        grad_qv,
        s_out,
        s_in,
        grad_b_in,
        s_back,
        gains_biases[:2],
        gains_biases[2:],
    )


def per_device(
    hidden_in, teacher, valid_mask, random_blocks, w_qkv, b_qv, w_out, w_in, b_in, w_back, ln_gains, row_biases
):
    local = hidden_in.shape[0]
    dp, tensor = lax.axis_size("dp"), lax.axis_size("tensor")
    zn = dp // 2
    tokens_total = local * tensor * dp
    pairs = b_qv.shape[1]
    mask = valid_mask.reshape(-1, 128)
    tables = block_tables(random_blocks, lax.axis_index("tensor") % 2)
    q, k, v, ctx, lse, ctx_rows, hid_t, w, full_in, full_bt, full_ot, par = gather_attend(
        tables[0], w_qkv, hidden_in, (b_qv.transpose(1, 0, 2), b_in.T, ln_gains, row_biases, mask), w_in, w_back.T,
        w_out, pairs, zn, 0,
    )
    units = (tensor, D, w_in.shape[1])
    encoded, gmix, gctx, g_in, g_bt, g_ot, vec = row_pass(
        tokens_total, ctx_rows, hidden_in, teacher, mask, full_in.reshape(units), full_bt.reshape(units), full_ot,
        par, 256,
    )
    part, there, s_in, s_bt, s_ot, s_qkv, vector, bias = attend_sum(
        tables, q, k, v, ctx, lse, gctx, hid_t, w, gmix, g_in.reshape(full_in.shape), g_bt.reshape(full_in.shape),
        g_ot, vec, zn, 1,
    )
    loss, grad_in, g_qkv, g_bias, g_out, g_w_in, g_b_in, g_back, g_gains, g_rows = take(
        par, vector, bias, part, there, s_in, s_bt, s_ot, s_qkv, b_in.shape, b_qv.shape
    )
    return (
        loss.reshape(()), encoded, grad_in, g_qkv, g_bias.transpose(1, 0, 2), g_out, g_w_in, g_b_in.T, g_back.T,
        g_gains, g_rows,
    )


def project_attend_kernel(idx_ref, hid_ref, w_ref, b_ref, q_ref, k_ref, v_ref, ctx_ref, lse_ref, lse_t):
    chunk = hid_ref.shape[1] // 2
    for p in range(q_ref.shape[0]):

        def project(i, carry, p=p):
            project_rows(p, i, chunk, hid_ref, w_ref, b_ref[:, p * 128 : (p + 1) * 128], q_ref, k_ref, v_ref)
            return carry

        lax.fori_loop(0, 4, project, 0)
    Forward(idx_ref, q_ref, k_ref, v_ref, ctx_ref, lse_ref, lse_t).run(q_ref.shape[0])


def project_attend(idx, hid, w, bias, pairs):
    n = 2 * hid.shape[1]
    heads = SDS((pairs, n, 128), BF)
    blocks = SDS((pairs, n // BLK, BLK, 128), BF)
    return pl.pallas_call(
        project_attend_kernel,
        out_shape=(heads, blocks, blocks, heads, SDS((pairs, n // BLK, 128), F32)),
        in_specs=[SM, VM, VM, VM],
        out_specs=(VM,) * 5,
        scratch_shapes=[pltpu.VMEM((128, 128), F32)],
        compiler_params=params(56),
        name="project_attend",
    )(idx, hid, w, bias)


def attend_back_kernel(
    idx_ref, prev_ref, last_ref, q_ref, k_ref, v_ref, ctx_ref, lse_ref, do_ref, hid_ref, w_ref, gw_ref, gh_ref, gb_ref,
    dq, dk, dv, dk_acc, dv_acc, dk_run, dv_run, hid_t,
):
    pairs = q_ref.shape[0]
    local = hid_ref.shape[1]
    for i in range(2):
        hid_t[:, i * local : (i + 1) * local] = hid_ref[i].T
    attend = Backward(
        idx_ref, prev_ref, last_ref, q_ref, k_ref, v_ref, ctx_ref, do_ref, lse_ref, dq, dk, dv,
        dk_acc, dv_acc, dk_run, dv_run,
    )

    def done(p):
        gw_ref[p] = weight_grad(p, hid_t, dq, dk, dv)
        for n, g in enumerate((dq, dv)):
            gb_ref[p, n : n + 1, :] = jnp.sum(g[p].astype(F32), axis=0, keepdims=True)

    attend.run(pairs, None, done)
    size = local // 4

    def some(i, carry):
        rows = pl.ds(pl.multiple_of(i * size, size), size)
        gh_ref[rows, :] = hidden_grad(dq, dk, dv, w_ref, rows)
        return carry

    lax.fori_loop(0, 8, some, 0)


def attend_back(tables, q, k, v, ctx, lse, do, hid, w):
    pairs, n, _ = q.shape
    slots = 3 * (n // BLK - 2) + 1
    heads = pltpu.VMEM((pairs, n, 128), BF)
    return pl.pallas_call(
        attend_back_kernel,
        out_shape=(SDS((pairs, D, 3 * 128), F32), SDS((n, D), F32), SDS((pairs, 2, 128), F32)),
        in_specs=[SM] * 3 + [VM] * 8,
        out_specs=(VM,) * 3,
        scratch_shapes=[heads] * 3
        + [pltpu.VMEM((n, 128), F32)] * 2
        + [pltpu.VMEM((slots, BLK, 128), F32)] * 2
        + [pltpu.VMEM((D, n), BF)],
        compiler_params=params(60),
        name="attend_back",
    )(*tables, q, k, v, ctx, lse, do, hid, w)


def plain_device(
    hidden_in, teacher, valid_mask, random_blocks, w_qkv, b_qv, w_out, w_in, b_in, w_back, ln_gains, row_biases
):
    local = hidden_in.shape[0]
    dp, tensor = lax.axis_size("dp"), lax.axis_size("tensor")
    tokens_total = local * tensor * dp
    dpi, ti = lax.axis_index("dp"), lax.axis_index("tensor")
    y, c = ti // 2, ti % 2
    pairs, hd = b_qv.shape[1:]
    everyone = ("dp", "tensor")
    mask = valid_mask.astype(F32)
    par = lax.psum(small_parts(b_qv, b_in, ln_gains, row_biases, jnp.sum(mask)), everyone)
    tables = block_tables(random_blocks, c)

    def swap(x):
        there = lax.ppermute(x[1 - c], "tensor", [(i, i ^ 1) for i in range(tensor)])
        here = x[c]
        return jnp.stack([jnp.where(c == 0, here, there), jnp.where(c == 0, there, here)])

    hid = swap(jnp.stack([hidden_in, hidden_in]))
    w = lax.all_gather(lax.all_gather(w_qkv, "dp", axis=1, tiled=True), "tensor", axis=0)
    w = w.reshape(2, 2, 3, D, pairs, HD)[:, c].transpose(3, 2, 1, 0, 4).reshape(pairs, D, -1)
    w_o = lax.all_gather(lax.all_gather(w_out, "dp", axis=1, tiled=True), "tensor", axis=0)
    w_o = w_o.reshape(2, 2, pairs, HD, D).transpose(4, 1, 2, 0, 3).reshape(D, D)
    full_in = lax.all_gather(lax.all_gather(w_in, "dp", axis=0, tiled=True), "tensor", axis=0)
    full_bt = lax.all_gather(lax.all_gather(w_back.T, "dp", axis=0, tiled=True), "tensor", axis=0)
    bias = lax.dynamic_index_in_dim(par[11:13].reshape(2, 2, -1), c, 1, False)
    q, k, v, ctx, lse = project_attend(tables[0], hid, w, bias, pairs)
    ctx_rows = swap(ctx.reshape(pairs, 2, local, 128).swapaxes(0, 1))
    encoded, gmix, gctx, g_in, g_bt, g_ot, vec = row_pass(
        tokens_total, ctx_rows, hidden_in, teacher, valid_mask.reshape(-1, 128), full_in, full_bt, w_o, par, 256
    )
    gw, gh, gb = attend_back(tables, q, k, v, ctx, lse, swap(gctx), hid, w)
    there = lax.ppermute(gh.reshape(2, local, D)[1 - c].astype(BF), "tensor", [(i, i ^ 1) for i in range(tensor)])
    grad_in = gmix + gh.reshape(2, local, D)[c] + there.astype(F32)

    def spread(g):
        g = lax.psum_scatter(g, "tensor", scatter_dimension=0, tiled=False)
        return lax.psum_scatter(g, "dp", scatter_dimension=0, tiled=True)

    s_in, s_bt = spread(g_in.astype(F32)), spread(g_bt.astype(F32))
    s_ot = spread(g_ot.astype(F32).reshape(D, 2, pairs, 2, HD).transpose(3, 1, 0, 2, 4).reshape(tensor, D, -1))
    own = (jnp.arange(2) == c).astype(F32)
    gw = gw.reshape(pairs, D, 3, 2, HD).transpose(3, 1, 2, 0, 4).reshape(2, 1, D, -1) * own[None, :, None, None]
    s_qkv = spread(gw.reshape(tensor, D, -1)).reshape(-1, 3, pairs * HD).swapaxes(0, 1)
    bias = gb.swapaxes(0, 1).reshape(2, -1)
    bias = lax.psum(bias[:, None, :] * own[None, :, None], everyone)
    bias = lax.dynamic_index_in_dim(bias, c, 1, False)
    vector = lax.psum(vec, everyone)
    return finish(vector, bias, par, encoded, grad_in, s_qkv, s_ot.T, s_in, s_bt.T, b_in, pairs, hd)


def solution(mesh):
    rows = P(("dp", "tensor"), None)
    in_specs = (
        rows,
        rows,
        P(("dp", "tensor")),
        P(),
        P(None, "dp", "tensor"),
        P(None, "tensor", "dp"),
        P("tensor", "dp"),
        P("dp", "tensor"),
        P("tensor", "dp"),
        P("tensor", "dp"),
        P(None, "dp"),
        P(None, "dp"),
    )
    out_specs = (
        P(),
        rows,
        rows,
        P(None, "dp", "tensor"),
        P(None, "tensor", "dp"),
        P("tensor", "dp"),
        P("dp", "tensor"),
        P("tensor", "dp"),
        P("tensor", "dp"),
        P(None, ("dp", "tensor")),
        P(None, ("dp", "tensor")),
    )
    fills_tiles = (D // mesh.shape["dp"]) % 32 == 0
    step = per_device if fills_tiles else plain_device
    return jax.shard_map(step, mesh=mesh, in_specs=in_specs, out_specs=out_specs, check_vma=False)
```
